32 devices in a mesh: comp: 2 (over core), gy: 4 (over y, x), gx: 4 (over z).
Axes of the slice: x: 2, y: 2, z: 4, core: 2. Of those that a mesh axis runs over, the one named last changes fastest.
Arguments:
- ocean_state: float32 [16, 8, 16, 512], P('comp', None, 'gx', 'gy'), may hold values from -4 to 4, as said below
- irradiance: float32 [16, 512], P('gx', 'gy'), may hold values from 0.5 to 4
- land_mask: int32 [16, 512], P('gx', 'gy'), may hold values 0 or 1
- bottom_level: int32 [16, 512], P('gx', 'gy'), may hold values from 1 to 8
Outputs:
- new_state: float32 [16, 8, 16, 512], P('comp', None, 'gx', 'gy')
The draws below stay inside these ranges and needn't reach their ends.
Inputs may be any that keep to these rules, and one draw needn't show every extreme that they name: `ocean_state`: channels 0 to 3 hold velocity along x, velocity along y, temperature and salinity now, channels 4 to 7 the same one step earlier; the 8 tracer channels are positive.
All inputs are finite; a program needn't handle non-finite values. No bound on the sum of `land_mask` on one device may be relied on, other than what follows from the above.
Results may differ from the reference program's by a relative error of at most 0.0003.
Values sent between devices are 32-bit elements; how exact they have to be, the bound alone decides.
No kernel may reach another device: no remote copies, remote signals or barrier semaphores. Data moves between devices by JAX's collectives and lax.ppermute only.
A program may use at most 64 MiB of HBM per device.

```python
import math
import jax
import jax.numpy as jnp
from jax import lax

TRACERS = 8
LEV = 8
CX = 4
STEPS = 2
NX = 16
NY = 512


def draw_ocean_state(key, part):
    shape = (TRACERS, LEV, NX, NY)
    key_flow = jax.random.fold_in(key, 11)
    key_bgc = jax.random.fold_in(key, 12)
    dynamics = jnp.clip(jax.random.normal(key_flow, shape, jnp.float32), -4.0, 4.0)
    tracers = jnp.exp(jax.random.uniform(key_bgc, shape, jnp.float32, math.log(0.1), math.log(3.0)))
    return jnp.concatenate([dynamics, tracers], axis=0)


def plant(entries, own_key, low, high):
    index_at = [jax.random.randint(jax.random.fold_in(own_key, axis), (), 0, length) for axis, length in enumerate(entries.shape)]
    longest = entries.shape.index(max(entries.shape))
    beside = index_at[:longest] + [(index_at[longest] + 1) % entries.shape[longest]] + index_at[longest + 1:]
    return entries.at[tuple(index_at)].set(low).at[tuple(beside)].set(high)


def level_of(stream_key, shape, pieces, least, top_value):
    gain = 1.0
    for position, parts in pieces:
        heights = jax.random.uniform(jax.random.fold_in(jax.random.fold_in(stream_key, 6), position), (parts,), jnp.float32, least / len(pieces), top_value / len(pieces))
        gain = gain * jnp.repeat(jnp.exp(heights), shape[position] // parts).reshape((-1,) + (1,) * (len(shape) - 1 - position))
    return gain


def setup_inputs(seed: int = 0) -> dict:
    arg_keys = jax.random.split(jax.random.key(seed), 5)
    ocean_state = draw_ocean_state(jax.random.fold_in(arg_keys[4], 71), 0)
    irradiance = jnp.clip(jnp.exp(math.log(4.0) - 2.0794415 * jax.random.uniform(arg_keys[1], (NX, NY), jnp.float32) ** level_of(arg_keys[1], (NX, NY), ((0, 4), (1, 4)), -0.2, 0.2)), 0.5, 4.0)
    land_mask = plant((jax.random.randint(arg_keys[2], (NX, NY), 0, 8) < 7).astype(jnp.int32), jax.random.fold_in(arg_keys[2], 1), 0, 1)
    bottom_level = plant(jax.random.randint(arg_keys[3], (NX, NY), 1, LEV + 1), jax.random.fold_in(arg_keys[3], 1), 1, LEV).astype(jnp.int32)
    return dict(ocean_state=ocean_state, irradiance=irradiance, land_mask=land_mask, bottom_level=bottom_level)


TIME_STEP = 0.1
VISCOSITY = 0.2
DIFFUSION = 0.2
ASSELIN_GAIN = 0.1
THERMAL_EXPAND = 0.2
HALINE_CONTRACT = 0.8
GRAVITY_STEP = 0.1
CORIOLIS_BASE = 0.3
CORIOLIS_SLOPE = 0.4
MIXING_FLOOR = 0.05
MIXING_SPAN = 1.0
STRATIFICATION = 4.0
HEATING_GAIN = 3.0
WATER_ABSORB = 0.08
PIGMENT_ABSORB = 0.05
LIGHT_HALF = 0.5
THERMAL_GAIN_PER = 0.06
GROWTH_SMALL = 0.6
GROWTH_LARGE = 0.9
NUTRIENT_HALF_SMALL = 0.2
NUTRIENT_HALF_LARGE = 0.8
GRAZING_RATE = 0.8
GRAZING_HALF = 1.0
PHYTO_DEATH = 0.1
ZOOPLANKTON_DEATH = 0.15
EXCRETION = 0.1
ASSIMILATION = 0.7
REMINERAL_SMALL = 0.3
REMINERAL_LARGE = 0.1
NITRIFICATION = 0.2
OXYGEN_YIELD = 1.3
OXYGEN_DEMAND = 1.0


def interior(field_in):
    return field_in[..., 1:-1, 1:-1]


def neighbours(field_in):
    return (field_in[..., 2:, 1:-1], field_in[..., :-2, 1:-1], field_in[..., 1:-1, 2:], field_in[..., 1:-1, :-2])


def laplacian(field_in, entire_ocean_indicator):
    centre = interior(field_in)
    total = jnp.zeros_like(centre)
    for other, wet_other in zip(neighbours(field_in), neighbours(entire_ocean_indicator)):
        total = total + wet_other * (other - centre)
    return total * interior(entire_ocean_indicator)


def advection(east_speed, north_speed, field_in, entire_ocean_indicator):
    centre = interior(field_in)
    wet_centre = interior(entire_ocean_indicator)
    east_centre = interior(east_speed)
    north_centre = interior(north_speed)
    field_near = neighbours(field_in)
    wet_near = neighbours(entire_ocean_indicator)
    east_near = neighbours(east_speed)
    north_near = neighbours(north_speed)
    flux_east = 0.25 * (east_centre + east_near[0]) * (centre + field_near[0]) * wet_centre * wet_near[0]
    flux_west = 0.25 * (east_centre + east_near[1]) * (centre + field_near[1]) * wet_centre * wet_near[1]
    flux_north = 0.25 * (north_centre + north_near[2]) * (centre + field_near[2]) * wet_centre * wet_near[2]
    flux_south = 0.25 * (north_centre + north_near[3]) * (centre + field_near[3]) * wet_centre * wet_near[3]
    return flux_east - flux_west + flux_north - flux_south


def pressure_force(pressure, entire_ocean_indicator):
    centre = interior(pressure)
    wet_centre = interior(entire_ocean_indicator)
    near = neighbours(pressure)
    wet_near = neighbours(entire_ocean_indicator)
    force_east = 0.5 * wet_centre * (wet_near[0] * (near[0] - centre) + wet_near[1] * (centre - near[1]))
    force_north = 0.5 * wet_centre * (wet_near[2] * (near[2] - centre) + wet_near[3] * (centre - near[3]))
    return force_east, force_north


def ocean_water_mass_per_volume(thermal_state_grid, salt_content_grid, entire_ocean_indicator):
    return (HALINE_CONTRACT * salt_content_grid - THERMAL_EXPAND * thermal_state_grid) * entire_ocean_indicator


def make_flow(dynamics_full, entire_ocean_indicator):
    density = ocean_water_mass_per_volume(dynamics_full[2], dynamics_full[3], entire_ocean_indicator)
    below = jnp.concatenate([density[1:], density[-1:]], axis=0)
    wet_below = jnp.concatenate([entire_ocean_indicator[1:], jnp.zeros_like(entire_ocean_indicator[:1])], axis=0)
    strat = jnp.maximum(below - density, 0.0)
    mixing = (MIXING_FLOOR + MIXING_SPAN / (1.0 + STRATIFICATION * strat)) * entire_ocean_indicator * wet_below
    return jnp.stack([dynamics_full[0], dynamics_full[1], dynamics_full[2], mixing], axis=0)


def absorption(arriving_constituents, lit_in):
    wet_centre = (lit_in > 0).astype(jnp.float32)
    surface = lit_in[0]
    pigment = jnp.abs(arriving_constituents[2]) + jnp.abs(arriving_constituents[3])
    absorb = WATER_ABSORB + PIGMENT_ABSORB * pigment
    column = jnp.cumsum(absorb, axis=0)
    heating = surface * (jnp.exp(absorb - column) - jnp.exp(-column)) * wet_centre
    middle = surface * jnp.exp(0.5 * absorb - column)
    return heating, middle


def biotic_source_terms(arriving_constituents, thermal_state_grid, layer_centre_irradiance):
    nitrate, ammonium, small_phyto, large_phyto = arriving_constituents[0], arriving_constituents[1], arriving_constituents[2], arriving_constituents[3]
    grazers, small_detritus, large_detritus = arriving_constituents[4], arriving_constituents[5], arriving_constituents[6]
    nitrate_size = jnp.abs(nitrate)
    ammonium_size = jnp.abs(ammonium)
    light_limit = layer_centre_irradiance / (layer_centre_irradiance + LIGHT_HALF)
    thermal_change_per_step = jnp.exp(THERMAL_GAIN_PER * thermal_state_grid)
    small_common = GROWTH_SMALL * thermal_change_per_step * light_limit * small_phyto / (NUTRIENT_HALF_SMALL + nitrate_size + ammonium_size)
    large_common = GROWTH_LARGE * thermal_change_per_step * light_limit * large_phyto / (NUTRIENT_HALF_LARGE + nitrate_size + ammonium_size)
    small_nitrate = small_common * nitrate_size
    small_ammonium = small_common * ammonium_size
    large_nitrate = large_common * nitrate_size
    large_ammonium = large_common * ammonium_size
    prey = jnp.abs(small_phyto) + jnp.abs(large_phyto)
    graze_factor = GRAZING_RATE * grazers / (GRAZING_HALF + prey)
    graze_small = graze_factor * small_phyto
    graze_large = graze_factor * large_phyto
    remin = REMINERAL_SMALL * small_detritus + REMINERAL_LARGE * large_detritus
    nitrify = NITRIFICATION * ammonium
    growth = small_nitrate + small_ammonium + large_nitrate + large_ammonium
    tend_nitrate = nitrify - small_nitrate - large_nitrate
    tend_ammonium = remin + EXCRETION * grazers - nitrify - small_ammonium - large_ammonium
    tend_small = small_nitrate + small_ammonium - graze_small - PHYTO_DEATH * small_phyto
    tend_large = large_nitrate + large_ammonium - graze_large - PHYTO_DEATH * large_phyto
    tend_grazers = ASSIMILATION * (graze_small + graze_large) - EXCRETION * grazers - ZOOPLANKTON_DEATH * grazers
    tend_small_det = PHYTO_DEATH * small_phyto + (1.0 - ASSIMILATION) * graze_small - REMINERAL_SMALL * small_detritus
    tend_large_det = (PHYTO_DEATH * large_phyto + ZOOPLANKTON_DEATH * grazers
                      + (1.0 - ASSIMILATION) * graze_large - REMINERAL_LARGE * large_detritus)
    tend_oxygen = OXYGEN_YIELD * growth - OXYGEN_DEMAND * (remin + 2.0 * nitrify)
    return jnp.stack([tend_nitrate, tend_ammonium, tend_small, tend_large, tend_grazers,
                      tend_small_det, tend_large_det, tend_oxygen], axis=0)


def dynamics_update(dynamics_full, entire_ocean_indicator, heating, row_start, total_rows):
    wet_centre = interior(entire_ocean_indicator)
    density = ocean_water_mass_per_volume(dynamics_full[2], dynamics_full[3], entire_ocean_indicator)
    pressure = GRAVITY_STEP * jnp.cumsum(density, axis=0)
    force_east, force_north = pressure_force(pressure, entire_ocean_indicator)
    row_count = dynamics_full.shape[3] - 2
    row_index = (jnp.arange(row_count, dtype=jnp.int32) + row_start + 1).astype(jnp.float32)
    coriolis = CORIOLIS_BASE + CORIOLIS_SLOPE * row_index / total_rows
    earlier = dynamics_full[4:8]
    diffused = laplacian(earlier, entire_ocean_indicator)
    carried = advection(dynamics_full[0], dynamics_full[1], dynamics_full[2:4], entire_ocean_indicator)
    now_centre = interior(dynamics_full[0:4])
    tend_east = coriolis * now_centre[1] - force_east + VISCOSITY * diffused[0]
    tend_north = -coriolis * now_centre[0] - force_north + VISCOSITY * diffused[1]
    tend_temp = -carried[0] + DIFFUSION * diffused[2] + HEATING_GAIN * heating
    tend_salt = -carried[1] + DIFFUSION * diffused[3]
    tendency = jnp.stack([tend_east, tend_north, tend_temp, tend_salt], axis=0)
    earlier_centre = interior(earlier)
    after = earlier_centre + 2.0 * TIME_STEP * tendency * wet_centre
    filtered = now_centre + ASSELIN_GAIN * (earlier_centre - 2.0 * now_centre + after) * wet_centre
    return jnp.concatenate([after, filtered], axis=0)


def tracer_update(tracers_full, flow_full, entire_ocean_indicator, middle):
    wet_centre = interior(entire_ocean_indicator)
    centre = interior(tracers_full)
    carried = advection(flow_full[0], flow_full[1], tracers_full, entire_ocean_indicator)
    spread = laplacian(tracers_full, entire_ocean_indicator)
    mixing = interior(flow_full[3])
    below = jnp.concatenate([centre[:, 1:], jnp.zeros_like(centre[:, :1])], axis=1)
    flux_down = mixing * (below - centre)
    flux_above = jnp.concatenate([jnp.zeros_like(flux_down[:, :1]), flux_down[:, :-1]], axis=1)
    vertical = flux_down - flux_above
    react = biotic_source_terms(centre, interior(flow_full[2]), middle)
    return centre + TIME_STEP * (DIFFUSION * spread - carried + vertical + react) * wet_centre


def pad_global(field_in):
    wrapped = jnp.concatenate([field_in[..., -1:, :], field_in, field_in[..., :1, :]], axis=-2)
    zero_row = jnp.zeros_like(wrapped[..., :1])
    return jnp.concatenate([zero_row, wrapped, zero_row], axis=-1)


def reference(ocean_state, irradiance, land_mask, bottom_level):
    depth_index = jnp.arange(LEV, dtype=jnp.int32)[:, None, None]
    wet_cells = ((land_mask[None] == 1) & (depth_index < bottom_level[None])).astype(jnp.float32)
    lit_wet = irradiance[None] * wet_cells
    lit_padded = pad_global(lit_wet)
    dynamics = ocean_state[:TRACERS]
    tracers = ocean_state[TRACERS:]
    offsets = jnp.arange(NX // CX, dtype=jnp.int32) * CX
    for step_index in range(STEPS):
        dyn_padded = pad_global(dynamics)
        trc_padded = pad_global(tracers)

        def tile_step(offset):
            dyn_tile = lax.dynamic_slice_in_dim(dyn_padded, offset, CX + 2, axis=2)
            trc_tile = lax.dynamic_slice_in_dim(trc_padded, offset, CX + 2, axis=2)
            lit_tile = lax.dynamic_slice_in_dim(lit_padded, offset, CX + 2, axis=1)
            wet_tile = (lit_tile > 0).astype(jnp.float32)
            partner_flow = make_flow(dyn_tile, wet_tile)
            heating, middle = absorption(interior(trc_tile), interior(lit_tile))
            new_dyn = dynamics_update(dyn_tile, wet_tile, heating, -1, NY)
            new_trc = tracer_update(trc_tile, partner_flow, wet_tile, middle)
            return new_dyn, new_trc

        new_dyn, new_trc = lax.map(tile_step, offsets)
        dynamics = jnp.transpose(new_dyn, (1, 2, 0, 3, 4)).reshape(TRACERS, LEV, NX, NY)
        tracers = jnp.transpose(new_trc, (1, 2, 0, 3, 4)).reshape(TRACERS, LEV, NX, NY)
    return jnp.concatenate([dynamics, tracers], axis=0)
```

```python
import jax
import jax.numpy as jnp
from jax import lax
from jax.experimental import pallas as pl
from jax.experimental.pallas import tpu as pltpu
from jax.sharding import PartitionSpec as P

HALO = 2
FIELDS = 8
U, V, TEMP, SALT, UB, VB, TB, SB = range(FIELDS)
VEL_X = (U, UB)


def lane_roll(x, shift):
    shift %= x.shape[1]
    return pltpu.roll(x, shift, 1) if shift else x


def level_roll(x, shift):
    shift %= x.shape[0]
    return pltpu.roll(x, shift, 0) if shift else x


class Shape:
    def __init__(self, lev, cx, rows):
        self.lev, self.cx, self.rows = lev, cx, rows
        self.cols = cx + 2 * HALO
        self.group = rows // self.cols
        self.per_tile = self.group // (2 * HALO)
        self.half = self.group // 2
        self.edge_tiles = -(-FIELDS // self.per_tile) + 1
        assert self.per_tile >= 2 and self.group >= 4 * HALO and 2 * cx <= lev
        assert self.cols * self.group == rows
        self.mask_tile = FIELDS * cx
        self.halo_tiles = FIELDS * HALO
        self.edge_base = 2 * self.halo_tiles + 2

    def lanes(self):
        return lax.broadcasted_iota(jnp.int32, (self.lev, self.rows), 1)

    def levels(self):
        return lax.broadcasted_iota(jnp.int32, (self.lev, self.rows), 0)

    def row(self, ref, tile, r):
        return jnp.broadcast_to(ref[tile, r : r + 1, :], (self.lev, self.rows))

    def edge_place(self, acc, value, j, channel, lane):
        at = j * self.group + channel * 2 * HALO + HALO
        return jnp.where((lane >= at - HALO) & (lane < at + HALO), lane_roll(value, at), acc)


def pack_kernel(sh, state_ref, irr_ref, land_ref, bottom_ref, x_ref, e_ref, ma_ref, mb_ref):
    odd = lax.axis_index("gx") % 2 == 1
    flip = jnp.where(odd & (lax.axis_index("comp") == 0), -1.0, 1.0)
    lane = sh.lanes()
    cx = sh.cx
    zero = jnp.zeros((sh.lev, sh.rows), jnp.float32)
    edges = [zero] * sh.edge_tiles
    for ch in range(FIELDS):
        raw = [state_ref[pl.ds(ch * sh.lev * cx + i, sh.lev, stride=cx), :] for i in range(cx)]
        cols = [jnp.where(odd, raw[cx - 1 - k], raw[k]) for k in range(cx)]
        if ch in VEL_X:
            cols = [c * flip for c in cols]
        t, q = divmod(ch, sh.per_tile)
        for k in range(cx):
            x_ref[ch * cx + k] = cols[k]
            edges[t] = sh.edge_place(edges[t], cols[k], k + HALO, q, lane)
        for d in range(HALO):
            mb_ref[ch * HALO + d] = cols[d]
            ma_ref[ch * HALO + d] = cols[cx - 1 - d]
    depth = jnp.where(land_ref[...] == 1, bottom_ref[...], 0).astype(jnp.float32)
    irr = irr_ref[...]
    rows = []
    for value in (irr, depth):
        rows += [
            jnp.where(odd, value[cx - 1 - k : cx - k, :], value[k : k + 1, :]) for k in range(cx)
        ]
    for r, value in enumerate(rows):
        x_ref[sh.mask_tile, r : r + 1, :] = value
        mb_ref[sh.halo_tiles, r : r + 1, :] = value
        ma_ref[sh.halo_tiles, r : r + 1, :] = value
        q, k = divmod(r, cx)
        wide = jnp.broadcast_to(value, (sh.lev, sh.rows))
        edges[-1] = sh.edge_place(edges[-1], wide, k + HALO, q, lane)
    for t in range(sh.edge_tiles):
        e_ref[t] = edges[t]


def merge_kernel(sh, e_ref, ra_ref, rb_ref, eo_ref, h_ref):
    flip = jnp.where(lax.axis_index("comp") == 0, -1.0, 1.0)
    lane = sh.lanes()
    cx = sh.cx
    edges = [e_ref[t] for t in range(sh.edge_tiles)]
    sides = (
        (ra_ref, 0, lambda d: cx + HALO + d, lambda d: cx - 1 - d),
        (rb_ref, 1, lambda d: HALO - 1 - d, lambda d: d),
    )
    for ref, side, place, source in sides:
        for ch in range(FIELDS):
            t, q = divmod(ch, sh.per_tile)
            for d in range(HALO):
                value = ref[ch * HALO + d]
                if ch in VEL_X:
                    value = value * flip
                h_ref[side * sh.halo_tiles + ch * HALO + d] = value
                edges[t] = sh.edge_place(edges[t], value, place(d), q, lane)
        h_ref[2 * sh.halo_tiles + side] = ref[sh.halo_tiles]
        for q in range(2):
            for d in range(HALO):
                value = sh.row(ref, sh.halo_tiles, q * cx + source(d))
                edges[-1] = sh.edge_place(edges[-1], value, place(d), q, lane)
    for t in range(sh.edge_tiles):
        eo_ref[t] = edges[t]
        h_ref[sh.edge_base + t] = edges[t]


STRIP = "strip"


class Field:
    def __init__(self, sh, lane, col, strip):
        self.sh, self.lane, self.col, self.strip = sh, lane, col, strip

    def centre(self, site):
        return self.strip() if site == STRIP else self.col(site)

    def east(self, site):
        return lane_roll(self.strip(), -self.sh.group) if site == STRIP else self.col(site + 1)

    def west(self, site):
        return lane_roll(self.strip(), self.sh.group) if site == STRIP else self.col(site - 1)

    def north(self, site):
        if site == STRIP:
            return lane_roll(self.strip(), -1)
        sh = self.sh
        end = sh.rows - 1
        beyond = lane_roll(self.strip(), end - (site * sh.group + sh.half + HALO))
        return jnp.where(self.lane == end, beyond, lane_roll(self.col(site), -1))

    def south(self, site):
        if site == STRIP:
            return lane_roll(self.strip(), 1)
        sh = self.sh
        beyond = lane_roll(self.strip(), -(site * sh.group + HALO - 1))
        return jnp.where(self.lane == 0, beyond, lane_roll(self.col(site), 1))

    def around(self, site):
        return self.east(site), self.west(site), self.north(site), self.south(site)


def step_kernel(sh, xo, xp, ho, hp, rao, rbo, rap, rbp, out_ref, strips, fresh, masks):
    lane, level = sh.lanes(), sh.levels()
    cx, group = sh.cx, sh.group
    gy, ny = lax.axis_index("gy"), lax.axis_size("gy")
    odd_x = lax.axis_index("gx") % 2 == 1
    mirror = jnp.where(odd_x, -1.0, 1.0)
    even_y = gy % 2 == 0
    slot = lane % (2 * HALO)
    in_group = lane % group
    first_step = list(range(1, sh.cols - 1))
    own = list(range(HALO, HALO + cx))
    sites = first_step + [STRIP]
    zero = jnp.zeros((sh.lev, sh.rows), jnp.float32)

    def cumulate(x):
        reach = 1
        while reach < sh.lev:
            x = x + jnp.where(level >= reach, level_roll(x, reach), 0.0)
            reach *= 2
        return x

    def place(site):
        return sh.cols if site == STRIP else site

    def build_strips(h, ra, rb, base, tiles, channels):
        for t in tiles:
            a, b, mine = ra[t], rb[t], h[sh.edge_base + t]
            left = jnp.where(gy > 0, jnp.where(even_y, b, a), zero)
            right = jnp.where(gy < ny - 1, jnp.where(even_y, a, b), zero)
            low = jnp.where(slot < HALO, left, mine)
            high = jnp.where(slot < HALO, mine, right)
            for q in range(channels):
                at = q * 2 * HALO
                strips[base + (t - tiles[0]) * channels + q] = jnp.where(
                    in_group < sh.half, lane_roll(low, -at), lane_roll(high, sh.half - at)
                )

    field_tiles = range(sh.edge_tiles - 1)
    build_strips(ho, rao, rbo, 0, field_tiles, sh.per_tile)
    build_strips(hp, rap, rbp, FIELDS, field_tiles, sh.per_tile)
    build_strips(ho, rao, rbo, 2 * FIELDS, [sh.edge_tiles - 1], 2)

    def mask_row(kind, j):
        if HALO <= j < HALO + cx:
            return sh.row(xo, sh.mask_tile, kind * cx + j - HALO)
        if j < HALO:
            return sh.row(ho, 2 * sh.halo_tiles + 1, kind * cx + HALO - 1 - j)
        return sh.row(ho, 2 * sh.halo_tiles, kind * cx + cx - 1 - (j - HALO - cx))

    levelf = level.astype(jnp.float32)

    def depth_at(site):
        return strips[2 * FIELDS + 1] if site == STRIP else mask_row(1, site)

    def irr_at(site):
        return strips[2 * FIELDS] if site == STRIP else mask_row(0, site)

    for j in range(sh.cols):
        masks[j] = jnp.where(levelf < depth_at(j), 1.0, 0.0)
    masks[sh.cols] = jnp.where(levelf < depth_at(STRIP), 1.0, 0.0)
    wet = Field(sh, lane, lambda j: masks[j], lambda: masks[sh.cols])
    face_base = sh.cols + 1
    for site in sites:
        w = wet.centre(site)
        for n, value in enumerate(wet.around(site)):
            masks[face_base + place(site) * 4 + n] = w * value

    def faces(site):
        return [masks[face_base + place(site) * 4 + n] for n in range(4)]

    def raw(x, h, base, ch):
        def col(j):
            if HALO <= j < HALO + cx:
                return x[ch * cx + j - HALO]
            if j < HALO:
                return h[sh.halo_tiles + ch * HALO + HALO - 1 - j]
            return h[ch * HALO + j - HALO - cx]

        return Field(sh, lane, col, lambda: strips[base + ch])

    slots = sh.cols + 1

    def stored(index):
        return Field(
            sh, lane, lambda j: fresh[index * slots + j], lambda: fresh[index * slots + sh.cols]
        )

    def store(index, site, value):
        fresh[index * slots + place(site)] = value

    def density_of(temp, salt, w):
        return (0.8 * salt - 0.2 * temp) * w

    def speeds(u, v, site, m):
        uc, vc = u.centre(site), v.centre(site)
        qe = 0.025 * (uc + u.east(site)) * m[0]
        qw = 0.025 * (uc + u.west(site)) * m[1]
        qn = 0.025 * (vc + v.north(site)) * m[2]
        qs = 0.025 * (vc + v.south(site)) * m[3]
        return qe, qw, qn, qs, (qw - qe) + (qs - qn)

    def laplacian(f, site, m, total):
        e, w, n, s = f.around(site)
        return (m[0] * e + m[1] * w) + (m[2] * n + m[3] * s) - total * f.centre(site)

    def coriolis(site):
        if site == STRIP:
            row = jnp.where(in_group < sh.half, in_group - HALO, sh.rows - HALO + in_group - sh.half)
        else:
            row = lane
        row = (row + gy * sh.rows).astype(jnp.float32)
        return mirror * (0.3 + 0.4 * row / (ny * sh.rows))

    def dynamics(d, pressure, site, heat, q, m, full):
        w = wet.centre(site)
        total = (m[0] + m[1]) + (m[2] + m[3])
        uc, vc = d[U].centre(site), d[V].centre(site)
        after = {}
        if "vel" in full:
            pc = pressure.centre(site)
            pe, pw, pn, ps = pressure.around(site)
            push_x = 0.1 * (m[0] * (pe - pc) + m[1] * (pc - pw))
            push_y = 0.1 * (m[2] * (pn - pc) + m[3] * (pc - ps))
            f = 0.2 * coriolis(site) * w
            after[U] = d[UB].centre(site) + (f * vc - push_x + 0.04 * laplacian(d[UB], site, m, total))
            after[V] = d[VB].centre(site) + (
                0.04 * laplacian(d[VB], site, m, total) - f * uc - push_y
            )
        if "tracer" in full:
            qe, qw, qn, qs, qc = q
            for now, before in ((TEMP, TB), (SALT, SB)):
                e, w_, n, s = d[now].around(site)
                carried = (qw * w_ - qe * e) + (qs * s - qn * n) + qc * d[now].centre(site)
                change = 2.0 * carried + 0.04 * laplacian(d[before], site, m, total)
                if now == TEMP:
                    change = change + 0.6 * heat
                after[now] = d[before].centre(site) + change
        return after

    def filtered(d, site, ch, after):
        w = wet.centre(site)
        now, before = d[ch].centre(site), d[ch + 4].centre(site)
        return now + 0.1 * (before - 2.0 * now + after) * w

    def optics(c2, c3, site):
        absorb = 0.08 + 0.05 * (jnp.abs(c2) + jnp.abs(c3))
        return absorb, cumulate(absorb)

    def heating(absorb, depthsum, site):
        fade = jnp.exp(-depthsum)
        above = jnp.where(level == 0, 1.0, level_roll(fade, 1))
        return irr_at(site) * wet.centre(site) * (above - fade)

    def light(absorb, depthsum, site):
        return irr_at(site) * jnp.exp(0.5 * absorb - depthsum)

    def mixing(temp, salt, site):
        rho = density_of(temp, salt, wet.centre(site))
        below = level_roll(rho, -1)
        wet_below = jnp.where(levelf + 1.0 < depth_at(site), 1.0, 0.0)
        return (0.005 + 0.1 / (1.0 + 4.0 * jnp.maximum(below - rho, 0.0))) * wet_below

    def reactions(c, temp, lit, which):
        nn, na = jnp.abs(c[0]), jnp.abs(c[1])
        base = jnp.exp(0.06 * temp) * (lit / (lit + 0.5))
        total = nn + na
        small = 0.6 * base * c[2] / (0.2 + total)
        large = 0.9 * base * c[3] / (0.8 + total)
        graze = 0.8 * c[4] / (1.0 + (jnp.abs(c[2]) + jnp.abs(c[3])))
        gs, gl = graze * c[2], graze * c[3]
        up_s, up_l = small * total, large * total
        r = {2: up_s - gs - 0.1 * c[2], 3: up_l - gl - 0.1 * c[3]}
        if len(which) > 2:
            both = small + large
            remin = 0.3 * c[5] + 0.1 * c[6]
            nitrify = 0.2 * c[1]
            r[0] = nitrify - both * nn
            r[1] = remin + 0.1 * c[4] - nitrify - both * na
            r[4] = 0.7 * (gs + gl) - 0.25 * c[4]
            r[5] = 0.1 * c[2] + 0.3 * gs - 0.3 * c[5]
            r[6] = 0.1 * c[3] + 0.15 * c[4] + 0.3 * gl - 0.1 * c[6]
            r[7] = 1.3 * (up_s + up_l) - (remin + 2.0 * nitrify)
        return r

    def tracer_step(c, site, q, m, kappa, temp, lit, which, emit):
        w = wet.centre(site)
        qe, qw, qn, qs, qc = q
        total = (m[0] + m[1]) + (m[2] + m[3])
        ke, kw = 0.02 * m[0] - qe, 0.02 * m[1] + qw
        kn, ks = 0.02 * m[2] - qn, 0.02 * m[3] + qs
        kc = (1.0 - 0.02 * total) + qc
        centre = {i: c[i].centre(site) for i in (which if len(which) > 2 else range(5))}
        r = reactions(centre, temp, lit, which)
        tenth = 0.1 * w
        for i in which:
            e, w_, n, s = c[i].around(site)
            here = centre[i]
            down = kappa * (level_roll(here, -1) - here)
            emit(
                i,
                kc * here
                + ((ke * e + kw * w_) + (kn * n + ks * s))
                + (down - level_roll(down, 1))
                + tenth * r[i],
            )

    def write(ch, k_values):
        for i in range(cx):
            out_ref[pl.ds(ch * sh.lev * cx + i, sh.lev, stride=cx), :] = jnp.where(
                odd_x, k_values[cx - 1 - i], k_values[i]
            )

    def make_pressure(d, index, all_sites):
        for site in all_sites:
            rho = density_of(d[TEMP].centre(site), d[SALT].centre(site), wet.centre(site))
            store(index, site, 0.1 * cumulate(rho))
        return stored(index)

    everywhere = list(range(sh.cols)) + [STRIP]

    @pl.when(lax.axis_index("comp") == 0)
    def _():
        d = [raw(xo, ho, 0, ch) for ch in range(FIELDS)]
        c = [raw(xp, hp, FIELDS, ch) for ch in range(FIELDS)]
        extra = FIELDS
        pressure = make_pressure(d, extra + 2, everywhere)
        for site in sites:
            m = faces(site)
            q = speeds(d[U], d[V], site, m)
            optic = optics(c[2].centre(site), c[3].centre(site), site)
            heat = heating(*optic, site)
            after = dynamics(d, pressure, site, heat, q, m, ("vel", "tracer"))
            for ch, value in after.items():
                store(ch, site, value)
                store(ch + 4, site, filtered(d, site, ch, value))
            if site in own:
                temp, salt = d[TEMP].centre(site), d[SALT].centre(site)
                tracer_step(
                    c, site, q, m, mixing(temp, salt, site), temp, light(*optic, site), (2, 3),
                    lambda i, value: store(extra + i - 2, site, value),
                )
        d = [stored(ch) for ch in range(FIELDS)]
        pressure = make_pressure(d, extra + 2, first_step + [STRIP])
        done = {}
        for site in own:
            m = faces(site)
            q = speeds(d[U], d[V], site, m)
            optic = optics(stored(extra).centre(site), stored(extra + 1).centre(site), site)
            heat = heating(*optic, site)
            after = dynamics(d, pressure, site, heat, q, m, ("vel", "tracer"))
            for ch, value in after.items():
                done[ch, site] = value
                done[ch + 4, site] = filtered(d, site, ch, value)
        for ch in range(FIELDS):
            factor = mirror if ch in VEL_X else 1.0
            write(ch, [done[ch, site] * factor if ch in VEL_X else done[ch, site] for site in own])

    @pl.when(lax.axis_index("comp") != 0)
    def _():
        d = [raw(xp, hp, FIELDS, ch) for ch in range(FIELDS)]
        c = [raw(xo, ho, 0, ch) for ch in range(FIELDS)]
        extra = FIELDS
        pressure = make_pressure(d, extra + 4, everywhere)
        for site in sites:
            m = faces(site)
            q = speeds(d[U], d[V], site, m)
            optic = optics(c[2].centre(site), c[3].centre(site), site)
            temp, salt = d[TEMP].centre(site), d[SALT].centre(site)
            inner = site in own
            heat = heating(*optic, site) if inner else None
            full = ("vel", "tracer") if inner else ("vel",)
            after = dynamics(d, pressure, site, heat, q, m, full)
            for ch, value in after.items():
                store(extra + ch, site, value)
            tracer_step(
                c, site, q, m, mixing(temp, salt, site), temp, light(*optic, site), range(FIELDS),
                lambda i, value: store(i, site, value),
            )
        c = [stored(ch) for ch in range(FIELDS)]
        d = [stored(extra + ch) for ch in range(4)]
        done = {}
        for site in own:
            m = faces(site)
            q = speeds(d[U], d[V], site, m)
            optic = optics(c[2].centre(site), c[3].centre(site), site)
            temp, salt = d[TEMP].centre(site), d[SALT].centre(site)

            def emit(i, value):
                done[i, site] = value

            tracer_step(
                c, site, q, m, mixing(temp, salt, site), temp, light(*optic, site), range(FIELDS),
                emit,
            )
        for ch in range(FIELDS):
            write(ch, [done[ch, site] for site in own])


def tiles(sh, n):
    return jax.ShapeDtypeStruct((n, sh.lev, sh.rows), jnp.float32)


def call(kernel, sh, outs, args, flops, scratch=()):
    spec = pl.BlockSpec(memory_space=pltpu.VMEM)
    size = sum(a.size for a in args) + sum(o.size for o in outs)
    return pl.pallas_call(
        lambda *refs: kernel(sh, *refs),
        out_shape=outs,
        in_specs=[spec] * len(args),
        out_specs=[spec] * len(outs),
        scratch_shapes=list(scratch),
        name=kernel.__name__,
        compiler_params=pltpu.CompilerParams(vmem_limit_bytes=16 << 20),
        cost_estimate=pl.CostEstimate(flops=flops, bytes_accessed=4 * size, transcendentals=0),
    )(*args)


def local(ocean_state, irradiance, land_mask, bottom_level):
    fields, lev, cx, rows = ocean_state.shape
    assert fields == FIELDS
    sh = Shape(lev, cx, rows)
    nx, ny = lax.axis_size("gx"), lax.axis_size("gy")
    assert nx % 2 == 0 and ny % 2 == 0
    axes = ("comp", "gy", "gx")

    def send(value, target, name):
        pairs = []
        for c in range(2):
            for y in range(ny):
                for x in range(nx):
                    tc, ty, tx = target(c, y, x)
                    pairs.append(((c * ny + y) * nx + x, (tc * ny + ty) * nx + tx))
        with jax.named_scope(name):
            return lax.ppermute(value, axes, pairs)

    def odd_pair(i, n):
        return (i + 1) % n if i % 2 else (i - 1) % n

    def x_a(v):
        return send(v, lambda c, y, x: (c, y, x ^ 1), "x_a")

    def x_b(v):
        return send(v, lambda c, y, x: (c, y, odd_pair(x, nx)), "x_b")

    def y_a(v):
        return send(v, lambda c, y, x: (c, y ^ 1, x), "y_a")

    def y_b(v):
        return send(v, lambda c, y, x: (c, odd_pair(y, ny), x), "y_b")

    def swap(v, name):
        return send(v, lambda c, y, x: (1 - c, y, x), name)

    flat = ocean_state.reshape(fields * lev * cx, rows)
    x, e0, ma, mb = call(
        pack_kernel,
        sh,
        [
            tiles(sh, fields * cx + 1),
            tiles(sh, sh.edge_tiles),
            tiles(sh, sh.halo_tiles + 1),
            tiles(sh, sh.halo_tiles + 1),
        ],
        (flat, irradiance, land_mask, bottom_level),
        100_000,
    )
    ra, rb = x_a(ma), x_b(mb)
    xp = swap(x, "swap_x")
    e1, h = call(
        merge_kernel,
        sh,
        [tiles(sh, sh.edge_tiles), tiles(sh, sh.edge_base + sh.edge_tiles)],
        (e0, ra, rb),
        100_000,
    )
    ya, yb = y_a(e1), y_b(e1)
    hp = swap(h, "swap_h")
    yap, ybp = swap(ya, "swap_a"), swap(yb, "swap_b")
    width = sh.cols + 1
    (out,) = call(
        step_kernel,
        sh,
        [jax.ShapeDtypeStruct(flat.shape, jnp.float32)],
        (x, xp, h, hp, ya, yb, yap, ybp),
        10_000_000,
        scratch=[
            pltpu.VMEM((2 * FIELDS + 2, lev, rows), jnp.float32),
            pltpu.VMEM(((FIELDS + 5) * width, lev, rows), jnp.float32),
            pltpu.VMEM((width + 4 * width, lev, rows), jnp.float32),
        ],
    )
    return out.reshape(ocean_state.shape)


def solution(mesh):
    return jax.shard_map(
        local,
        mesh=mesh,
        in_specs=(P("comp", None, "gx", "gy"), P("gx", "gy"), P("gx", "gy"), P("gx", "gy")),
        out_specs=P("comp", None, "gx", "gy"),
        check_vma=False,
    )
```

```python
import jax
import jax.numpy as jnp
from jax import lax
from jax.experimental import pallas as pl
from jax.experimental.pallas import tpu as pltpu
from jax.sharding import PartitionSpec as P


HALO = 2
FIELDS = 8
U, V, TEMP, SALT, UB, VB, TB, SB = range(FIELDS)
VEL_X = (U, UB)


def lane_roll(x, shift):
    shift %= x.shape[1]
    return pltpu.roll(x, shift, 1) if shift else x


def level_roll(x, shift):
    shift %= x.shape[0]
    return pltpu.roll(x, shift, 0) if shift else x


class Shape:
    def __init__(self, lev, cx, rows):
        self.lev, self.cx, self.rows = lev, cx, rows
        self.cols = cx + 2 * HALO
        self.group = rows // self.cols
        self.per_tile = self.group // (2 * HALO)
        self.half = self.group // 2
        self.edge_tiles = -(-FIELDS // self.per_tile) + 1
        assert self.per_tile >= 2 and self.group >= 4 * HALO and 2 * cx <= lev
        assert self.cols * self.group == rows
        self.mask_tile = FIELDS * cx
        self.halo_tiles = FIELDS * HALO
        self.edge_base = 2 * self.halo_tiles + 2

    def lanes(self):
        return lax.broadcasted_iota(jnp.int32, (self.lev, self.rows), 1)

    def levels(self):
        return lax.broadcasted_iota(jnp.int32, (self.lev, self.rows), 0)

    def row(self, ref, tile, r):
        return jnp.broadcast_to(ref[tile, r : r + 1, :], (self.lev, self.rows))

    def edge_place(self, acc, value, j, channel, lane):
        at = j * self.group + channel * 2 * HALO + HALO
        return jnp.where((lane >= at - HALO) & (lane < at + HALO), lane_roll(value, at), acc)


def pack_kernel(sh, *refs):
    sources, (x_ref, e_ref, ma_ref, mb_ref), arrived, sem = refs[:4], refs[4:8], refs[8:12], refs[12]
    copies = [
        pltpu.make_async_copy(a, b, sem.at[i]) for i, (a, b) in enumerate(zip(sources, arrived))
    ]
    for copy in copies:
        copy.start()
    for copy in copies:
        copy.wait()
    state_ref, irr_ref, land_ref, bottom_ref = arrived
    odd = lax.axis_index("gx") % 2 == 1
    flip = jnp.where(odd & (lax.axis_index("comp") == 0), -1.0, 1.0)
    lane = sh.lanes()
    cx = sh.cx
    zero = jnp.zeros((sh.lev, sh.rows), jnp.float32)
    edges = [zero] * sh.edge_tiles
    for ch in range(FIELDS):
        raw = [state_ref[pl.ds(ch * sh.lev * cx + i, sh.lev, stride=cx), :] for i in range(cx)]
        cols = [jnp.where(odd, raw[cx - 1 - k], raw[k]) for k in range(cx)]
        if ch in VEL_X:
            cols = [c * flip for c in cols]
        t, q = divmod(ch, sh.per_tile)
        for k in range(cx):
            x_ref[ch * cx + k] = cols[k]
            edges[t] = sh.edge_place(edges[t], cols[k], k + HALO, q, lane)
        for d in range(HALO):
            mb_ref[ch * HALO + d] = cols[d]
            ma_ref[ch * HALO + d] = cols[cx - 1 - d]
    depth = jnp.where(land_ref[...] == 1, bottom_ref[...], 0).astype(jnp.float32)
    irr = irr_ref[...]
    rows = []
    for value in (irr, depth):
        rows += [
            jnp.where(odd, value[cx - 1 - k : cx - k, :], value[k : k + 1, :]) for k in range(cx)
        ]
    for r, value in enumerate(rows):
        x_ref[sh.mask_tile, r : r + 1, :] = value
        mb_ref[sh.halo_tiles, r : r + 1, :] = value
        ma_ref[sh.halo_tiles, r : r + 1, :] = value
        q, k = divmod(r, cx)
        wide = jnp.broadcast_to(value, (sh.lev, sh.rows))
        edges[-1] = sh.edge_place(edges[-1], wide, k + HALO, q, lane)
    for t in range(sh.edge_tiles):
        e_ref[t] = edges[t]


def merge_kernel(sh, e_ref, ra_ref, rb_ref, eo_ref, h_ref):
    flip = jnp.where(lax.axis_index("comp") == 0, -1.0, 1.0)
    lane = sh.lanes()
    cx = sh.cx
    edges = [e_ref[t] for t in range(sh.edge_tiles)]
    sides = (
        (ra_ref, 0, lambda d: cx + HALO + d, lambda d: cx - 1 - d),
        (rb_ref, 1, lambda d: HALO - 1 - d, lambda d: d),
    )
    for ref, side, place, source in sides:
        for ch in range(FIELDS):
            t, q = divmod(ch, sh.per_tile)
            for d in range(HALO):
                value = ref[ch * HALO + d]
                if ch in VEL_X:
                    value = value * flip
                h_ref[side * sh.halo_tiles + ch * HALO + d] = value
                edges[t] = sh.edge_place(edges[t], value, place(d), q, lane)
        h_ref[2 * sh.halo_tiles + side] = ref[sh.halo_tiles]
        for q in range(2):
            for d in range(HALO):
                value = sh.row(ref, sh.halo_tiles, q * cx + source(d))
                edges[-1] = sh.edge_place(edges[-1], value, place(d), q, lane)
    for t in range(sh.edge_tiles):
        eo_ref[t] = edges[t]
        h_ref[sh.edge_base + t] = edges[t]


STRIP = "strip"


class Field:
    def __init__(self, sh, lane, col, strip):
        self.sh, self.lane, self.col, self.strip = sh, lane, col, strip

    def centre(self, site):
        return self.strip() if site == STRIP else self.col(site)

    def east(self, site):
        return lane_roll(self.strip(), -self.sh.group) if site == STRIP else self.col(site + 1)

    def west(self, site):
        return lane_roll(self.strip(), self.sh.group) if site == STRIP else self.col(site - 1)

    def north(self, site):
        if site == STRIP:
            return lane_roll(self.strip(), -1)
        sh = self.sh
        end = sh.rows - 1
        beyond = lane_roll(self.strip(), end - (site * sh.group + sh.half + HALO))
        return jnp.where(self.lane == end, beyond, lane_roll(self.col(site), -1))

    def south(self, site):
        if site == STRIP:
            return lane_roll(self.strip(), 1)
        sh = self.sh
        beyond = lane_roll(self.strip(), -(site * sh.group + HALO - 1))
        return jnp.where(self.lane == 0, beyond, lane_roll(self.col(site), 1))

    def around(self, site):
        return self.east(site), self.west(site), self.north(site), self.south(site)


def step_kernel(sh, xo, xp, ho, hp, rao, rbo, rap, rbp, out_ref, strips, fresh, masks):
    lane, level = sh.lanes(), sh.levels()
    cx, group = sh.cx, sh.group
    gy, ny = lax.axis_index("gy"), lax.axis_size("gy")
    odd_x = lax.axis_index("gx") % 2 == 1
    mirror = jnp.where(odd_x, -1.0, 1.0)
    even_y = gy % 2 == 0
    slot = lane % (2 * HALO)
    in_group = lane % group
    first_step = list(range(1, sh.cols - 1))
    own = list(range(HALO, HALO + cx))
    sites = first_step + [STRIP]
    zero = jnp.zeros((sh.lev, sh.rows), jnp.float32)

    def cumulate(x):
        reach = 1
        while reach < sh.lev:
            x = x + jnp.where(level >= reach, level_roll(x, reach), 0.0)
            reach *= 2
        return x

    def place(site):
        return sh.cols if site == STRIP else site

    def build_strips(h, ra, rb, base, tiles, channels):
        for t in tiles:
            a, b, mine = ra[t], rb[t], h[sh.edge_base + t]
            left = jnp.where(gy > 0, jnp.where(even_y, b, a), zero)
            right = jnp.where(gy < ny - 1, jnp.where(even_y, a, b), zero)
            low = jnp.where(slot < HALO, left, mine)
            high = jnp.where(slot < HALO, mine, right)
            for q in range(channels):
                at = q * 2 * HALO
                strips[base + (t - tiles[0]) * channels + q] = jnp.where(
                    in_group < sh.half, lane_roll(low, -at), lane_roll(high, sh.half - at)
                )

    field_tiles = range(sh.edge_tiles - 1)
    build_strips(ho, rao, rbo, 0, field_tiles, sh.per_tile)
    build_strips(hp, rap, rbp, FIELDS, field_tiles, sh.per_tile)
    build_strips(ho, rao, rbo, 2 * FIELDS, [sh.edge_tiles - 1], 2)

    def mask_row(kind, j):
        if HALO <= j < HALO + cx:
            return sh.row(xo, sh.mask_tile, kind * cx + j - HALO)
        if j < HALO:
            return sh.row(ho, 2 * sh.halo_tiles + 1, kind * cx + HALO - 1 - j)
        return sh.row(ho, 2 * sh.halo_tiles, kind * cx + cx - 1 - (j - HALO - cx))

    levelf = level.astype(jnp.float32)

    def depth_at(site):
        return strips[2 * FIELDS + 1] if site == STRIP else mask_row(1, site)

    def irr_at(site):
        return strips[2 * FIELDS] if site == STRIP else mask_row(0, site)

    for j in range(sh.cols):
        masks[j] = jnp.where(levelf < depth_at(j), 1.0, 0.0)
    masks[sh.cols] = jnp.where(levelf < depth_at(STRIP), 1.0, 0.0)
    wet = Field(sh, lane, lambda j: masks[j], lambda: masks[sh.cols])
    face_base = sh.cols + 1
    for site in sites:
        w = wet.centre(site)
        for n, value in enumerate(wet.around(site)):
            masks[face_base + place(site) * 4 + n] = w * value

    def faces(site):
        return [masks[face_base + place(site) * 4 + n] for n in range(4)]

    def raw(x, h, base, ch):
        def col(j):
            if HALO <= j < HALO + cx:
                return x[ch * cx + j - HALO]
            if j < HALO:
                return h[sh.halo_tiles + ch * HALO + HALO - 1 - j]
            return h[ch * HALO + j - HALO - cx]

        return Field(sh, lane, col, lambda: strips[base + ch])

    slots = sh.cols + 1

    def stored(index):
        return Field(
            sh, lane, lambda j: fresh[index * slots + j], lambda: fresh[index * slots + sh.cols]
        )

    def store(index, site, value):
        fresh[index * slots + place(site)] = value

    def density_of(temp, salt, w):
        return (0.8 * salt - 0.2 * temp) * w

    def speeds(u, v, site, m):
        uc, vc = u.centre(site), v.centre(site)
        qe = 0.025 * (uc + u.east(site)) * m[0]
        qw = 0.025 * (uc + u.west(site)) * m[1]
        qn = 0.025 * (vc + v.north(site)) * m[2]
        qs = 0.025 * (vc + v.south(site)) * m[3]
        return qe, qw, qn, qs, (qw - qe) + (qs - qn)

    def laplacian(f, site, m, total):
        e, w, n, s = f.around(site)
        return (m[0] * e + m[1] * w) + (m[2] * n + m[3] * s) - total * f.centre(site)

    def coriolis(site):
        if site == STRIP:
            row = jnp.where(in_group < sh.half, in_group - HALO, sh.rows - HALO + in_group - sh.half)
        else:
            row = lane
        row = (row + gy * sh.rows).astype(jnp.float32)
        return mirror * (0.3 + 0.4 * row / (ny * sh.rows))

    def dynamics(d, pressure, site, heat, q, m, full):
        w = wet.centre(site)
        total = (m[0] + m[1]) + (m[2] + m[3])
        uc, vc = d[U].centre(site), d[V].centre(site)
        after = {}
        if "vel" in full:
            pc = pressure.centre(site)
            pe, pw, pn, ps = pressure.around(site)
            push_x = 0.1 * (m[0] * (pe - pc) + m[1] * (pc - pw))
            push_y = 0.1 * (m[2] * (pn - pc) + m[3] * (pc - ps))
            f = 0.2 * coriolis(site) * w
            after[U] = d[UB].centre(site) + (f * vc - push_x + 0.04 * laplacian(d[UB], site, m, total))
            after[V] = d[VB].centre(site) + (
                0.04 * laplacian(d[VB], site, m, total) - f * uc - push_y
            )
        if "tracer" in full:
            qe, qw, qn, qs, qc = q
            for now, before in ((TEMP, TB), (SALT, SB)):
                e, w_, n, s = d[now].around(site)
                carried = (qw * w_ - qe * e) + (qs * s - qn * n) + qc * d[now].centre(site)
                change = 2.0 * carried + 0.04 * laplacian(d[before], site, m, total)
                if now == TEMP:
                    change = change + 0.6 * heat
                after[now] = d[before].centre(site) + change
        return after

    def filtered(d, site, ch, after):
        w = wet.centre(site)
        now, before = d[ch].centre(site), d[ch + 4].centre(site)
        return now + 0.1 * (before - 2.0 * now + after) * w

    def optics(c2, c3):
        absorb = 0.08 + 0.05 * (jnp.abs(c2) + jnp.abs(c3))
        return absorb, cumulate(absorb)

    def heating(absorb, depthsum, site):
        fade = jnp.exp(-depthsum)
        above = jnp.where(level == 0, 1.0, level_roll(fade, 1))
        return irr_at(site) * wet.centre(site) * (above - fade)

    def light(absorb, depthsum, site):
        return irr_at(site) * jnp.exp(0.5 * absorb - depthsum)

    def mixing(temp, salt, site):
        rho = density_of(temp, salt, wet.centre(site))
        below = level_roll(rho, -1)
        wet_below = jnp.where(levelf + 1.0 < depth_at(site), 1.0, 0.0)
        return (0.005 + 0.1 / (1.0 + 4.0 * jnp.maximum(below - rho, 0.0))) * wet_below

    def reactions(c, temp, lit, which):
        nn, na = jnp.abs(c[0]), jnp.abs(c[1])
        base = jnp.exp(0.06 * temp) * (lit / (lit + 0.5))
        total = nn + na
        small = 0.6 * base * c[2] / (0.2 + total)
        large = 0.9 * base * c[3] / (0.8 + total)
        graze = 0.8 * c[4] / (1.0 + (jnp.abs(c[2]) + jnp.abs(c[3])))
        gs, gl = graze * c[2], graze * c[3]
        up_s, up_l = small * total, large * total
        r = {2: up_s - gs - 0.1 * c[2], 3: up_l - gl - 0.1 * c[3]}
        if len(which) > 2:
            both = small + large
            remin = 0.3 * c[5] + 0.1 * c[6]
            nitrify = 0.2 * c[1]
            r[0] = nitrify - both * nn
            r[1] = remin + 0.1 * c[4] - nitrify - both * na
            r[4] = 0.7 * (gs + gl) - 0.25 * c[4]
            r[5] = 0.1 * c[2] + 0.3 * gs - 0.3 * c[5]
            r[6] = 0.1 * c[3] + 0.15 * c[4] + 0.3 * gl - 0.1 * c[6]
            r[7] = 1.3 * (up_s + up_l) - (remin + 2.0 * nitrify)
        return r

    def tracer_step(c, site, q, m, kappa, temp, lit, which, emit):
        w = wet.centre(site)
        qe, qw, qn, qs, qc = q
        total = (m[0] + m[1]) + (m[2] + m[3])
        ke, kw = 0.02 * m[0] - qe, 0.02 * m[1] + qw
        kn, ks = 0.02 * m[2] - qn, 0.02 * m[3] + qs
        kc = (1.0 - 0.02 * total) + qc
        centre = {i: c[i].centre(site) for i in (which if len(which) > 2 else range(5))}
        r = reactions(centre, temp, lit, which)
        tenth = 0.1 * w
        for i in which:
            e, w_, n, s = c[i].around(site)
            here = centre[i]
            down = kappa * (level_roll(here, -1) - here)
            emit(
                i,
                kc * here
                + ((ke * e + kw * w_) + (kn * n + ks * s))
                + (down - level_roll(down, 1))
                + tenth * r[i],
            )

    def write(ch, k_values):
        for i in range(cx):
            out_ref[pl.ds(ch * sh.lev * cx + i, sh.lev, stride=cx), :] = jnp.where(
                odd_x, k_values[cx - 1 - i], k_values[i]
            )

    def make_pressure(d, index, all_sites):
        for site in all_sites:
            rho = density_of(d[TEMP].centre(site), d[SALT].centre(site), wet.centre(site))
            store(index, site, 0.1 * cumulate(rho))
        return stored(index)

    everywhere = list(range(sh.cols)) + [STRIP]

    @pl.when(lax.axis_index("comp") == 0)
    def _():
        d = [raw(xo, ho, 0, ch) for ch in range(FIELDS)]
        c = [raw(xp, hp, FIELDS, ch) for ch in range(FIELDS)]
        extra = FIELDS
        pressure = make_pressure(d, extra + 2, everywhere)
        for site in sites:
            m = faces(site)
            q = speeds(d[U], d[V], site, m)
            optic = optics(c[2].centre(site), c[3].centre(site))
            heat = heating(*optic, site)
            after = dynamics(d, pressure, site, heat, q, m, ("vel", "tracer"))
            for ch, value in after.items():
                store(ch, site, value)
                store(ch + 4, site, filtered(d, site, ch, value))
            if site in own:
                temp, salt = d[TEMP].centre(site), d[SALT].centre(site)
                tracer_step(
                    c, site, q, m, mixing(temp, salt, site), temp, light(*optic, site), (2, 3),
                    lambda i, value: store(extra + i - 2, site, value),
                )
        d = [stored(ch) for ch in range(FIELDS)]
        pressure = make_pressure(d, extra + 2, first_step + [STRIP])
        done = {}
        for site in own:
            m = faces(site)
            q = speeds(d[U], d[V], site, m)
            optic = optics(stored(extra).centre(site), stored(extra + 1).centre(site))
            heat = heating(*optic, site)
            after = dynamics(d, pressure, site, heat, q, m, ("vel", "tracer"))
            for ch, value in after.items():
                done[ch, site] = value
                done[ch + 4, site] = filtered(d, site, ch, value)
        for ch in range(FIELDS):
            factor = mirror if ch in VEL_X else 1.0
            write(ch, [done[ch, site] * factor if ch in VEL_X else done[ch, site] for site in own])

    @pl.when(lax.axis_index("comp") != 0)
    def _():
        d = [raw(xp, hp, FIELDS, ch) for ch in range(FIELDS)]
        c = [raw(xo, ho, 0, ch) for ch in range(FIELDS)]
        extra = FIELDS
        pressure = make_pressure(d, extra + 4, everywhere)
        for site in sites:
            m = faces(site)
            q = speeds(d[U], d[V], site, m)
            optic = optics(c[2].centre(site), c[3].centre(site))
            temp, salt = d[TEMP].centre(site), d[SALT].centre(site)
            inner = site in own
            heat = heating(*optic, site) if inner else None
            full = ("vel", "tracer") if inner else ("vel",)
            after = dynamics(d, pressure, site, heat, q, m, full)
            for ch, value in after.items():
                store(extra + ch, site, value)
            tracer_step(
                c, site, q, m, mixing(temp, salt, site), temp, light(*optic, site), range(FIELDS),
                lambda i, value: store(i, site, value),
            )
        c = [stored(ch) for ch in range(FIELDS)]
        d = [stored(extra + ch) for ch in range(4)]
        done = {}
        for site in own:
            m = faces(site)
            q = speeds(d[U], d[V], site, m)
            optic = optics(c[2].centre(site), c[3].centre(site))
            temp, salt = d[TEMP].centre(site), d[SALT].centre(site)

            def emit(i, value):
                done[i, site] = value

            tracer_step(
                c, site, q, m, mixing(temp, salt, site), temp, light(*optic, site), range(FIELDS),
                emit,
            )
        for ch in range(FIELDS):
            write(ch, [done[ch, site] for site in own])


def tiles(sh, n):
    return jax.ShapeDtypeStruct((n, sh.lev, sh.rows), jnp.float32)


def call(kernel, sh, outs, args, flops, scratch=(), source=pltpu.VMEM):
    spec = pl.BlockSpec(memory_space=pltpu.VMEM)
    size = sum(a.size for a in args) + sum(o.size for o in outs)
    return pl.pallas_call(
        lambda *refs: kernel(sh, *refs),
        out_shape=outs,
        in_specs=[pl.BlockSpec(memory_space=source)] * len(args),
        out_specs=[spec] * len(outs),
        scratch_shapes=list(scratch),
        compiler_params=pltpu.CompilerParams(vmem_limit_bytes=16 << 20),
        cost_estimate=pl.CostEstimate(flops=flops, bytes_accessed=4 * size, transcendentals=0),
    )(*args)


def local(ocean_state, irradiance, land_mask, bottom_level):
    fields, lev, cx, rows = ocean_state.shape
    assert fields == FIELDS
    sh = Shape(lev, cx, rows)
    nx, ny = lax.axis_size("gx"), lax.axis_size("gy")
    assert nx % 2 == 0 and ny % 2 == 0
    axes = ("comp", "gy", "gx")

    def send(value, target):
        pairs = []
        for c in range(2):
            for y in range(ny):
                for x in range(nx):
                    tc, ty, tx = target(c, y, x)
                    pairs.append(((c * ny + y) * nx + x, (tc * ny + ty) * nx + tx))
        return lax.ppermute(value, axes, pairs)

    def odd_pair(i, n):
        return (i + 1) % n if i % 2 else (i - 1) % n

    def x_a(v):
        return send(v, lambda c, y, x: (c, y, x ^ 1))

    def x_b(v):
        return send(v, lambda c, y, x: (c, y, odd_pair(x, nx)))

    def y_a(v):
        return send(v, lambda c, y, x: (c, y ^ 1, x))

    def y_b(v):
        return send(v, lambda c, y, x: (c, odd_pair(y, ny), x))

    def swap(v):
        return send(v, lambda c, y, x: (1 - c, y, x))

    flat = ocean_state.reshape(fields * lev * cx, rows)
    x, e0, ma, mb = call(
        pack_kernel,
        sh,
        [
            tiles(sh, fields * cx + 1),
            tiles(sh, sh.edge_tiles),
            tiles(sh, sh.halo_tiles + 1),
            tiles(sh, sh.halo_tiles + 1),
        ],
        tuple(pltpu.with_memory_space_constraint(a, pltpu.HBM) for a in (flat, irradiance, land_mask, bottom_level)),
        100_000,
        scratch=[
            pltpu.VMEM(a.shape, a.dtype) for a in (flat, irradiance, land_mask, bottom_level)
        ]
        + [pltpu.SemaphoreType.DMA((4,))],
        source=pltpu.HBM,
    )
    ra, rb = x_a(ma), x_b(mb)
    xp = swap(x)
    e1, h = call(
        merge_kernel,
        sh,
        [tiles(sh, sh.edge_tiles), tiles(sh, sh.edge_base + sh.edge_tiles)],
        (e0, ra, rb),
        100_000,
    )
    ya, yb = y_a(e1), y_b(e1)
    hp = swap(h)
    yap, ybp = swap(ya), swap(yb)
    width = sh.cols + 1
    (out,) = call(
        step_kernel,
        sh,
        [jax.ShapeDtypeStruct(flat.shape, jnp.float32)],
        (x, xp, h, hp, ya, yb, yap, ybp),
        10_000_000,
        scratch=[
            pltpu.VMEM((2 * FIELDS + 2, lev, rows), jnp.float32),
            pltpu.VMEM(((FIELDS + 5) * width, lev, rows), jnp.float32),
            pltpu.VMEM((width + 4 * width, lev, rows), jnp.float32),
        ],
    )
    return out.reshape(ocean_state.shape)


def solution(mesh):
    return jax.shard_map(
        local,
        mesh=mesh,
        in_specs=(P("comp", None, "gx", "gy"), P("gx", "gy"), P("gx", "gy"), P("gx", "gy")),
        out_specs=P("comp", None, "gx", "gy"),
        check_vma=False,
    )
```

```python
import jax
import jax.numpy as jnp
from jax import lax
from jax.experimental import pallas as pl
from jax.experimental.pallas import tpu as pltpu
from jax.sharding import PartitionSpec as P


HALO = 2
FIELDS = 8
U, V, TEMP, SALT, UB, VB, TB, SB = range(FIELDS)
VEL_X = (U, UB)


def lane_roll(x, shift):
    shift %= x.shape[1]
    return pltpu.roll(x, shift, 1) if shift else x


def level_roll(x, shift):
    shift %= x.shape[0]
    return pltpu.roll(x, shift, 0) if shift else x


class Shape:
    def __init__(self, lev, cx, rows):
        self.lev, self.cx, self.rows = lev, cx, rows
        self.cols = cx + 2 * HALO
        self.group = rows // self.cols
        self.per_tile = self.group // (2 * HALO)
        self.half = self.group // 2
        self.field_tiles = -(-FIELDS // self.per_tile)
        self.edge_tiles = 2 * self.field_tiles + 1
        assert self.per_tile >= 2 and self.group >= 4 * HALO and 2 * cx <= lev
        assert self.cols * self.group == rows
        self.mask_tile = FIELDS * cx
        self.halo_tiles = FIELDS * HALO

    def lanes(self):
        return lax.broadcasted_iota(jnp.int32, (self.lev, self.rows), 1)

    def levels(self):
        return lax.broadcasted_iota(jnp.int32, (self.lev, self.rows), 0)

    def row(self, ref, tile, r):
        return jnp.broadcast_to(ref[tile, r : r + 1, :], (self.lev, self.rows))

    def edge_at(self, comp, ch):
        t, q = divmod(ch, self.per_tile)
        return comp * self.field_tiles + t, q

    def halo_at(self, comp, side, ch, d):
        return (self.halo_tiles if comp != side else 0) + ch * HALO + d

    def edge_place(self, acc, value, j, channel, lane):
        at = j * self.group + channel * 2 * HALO + HALO
        return jnp.where((lane >= at - HALO) & (lane < at + HALO), lane_roll(value, at), acc)


def load_kernel(sh, *refs):
    sources, x_ref, arrived, sem = refs[:4], refs[4], refs[5:9], refs[9]
    copies = [
        pltpu.make_async_copy(a, b, sem.at[i]) for i, (a, b) in enumerate(zip(sources, arrived))
    ]
    for copy in copies:
        copy.start()
    for copy in copies:
        copy.wait()
    state_ref, irr_ref, land_ref, bottom_ref = arrived
    odd = is_odd("gx")
    own_columns(sh, state_ref, x_ref, odd, first_core())
    cx = sh.cx
    depth = jnp.where(land_ref[...] == 1, bottom_ref[...], 0).astype(jnp.float32)
    for base, value in ((0, irr_ref[...]), (cx, depth)):
        for k in range(cx):
            x_ref[sh.mask_tile, base + k : base + k + 1, :] = jnp.where(
                odd, value[cx - 1 - k : cx - k, :], value[k : k + 1, :]
            )


def is_odd(axis):
    return lax.axis_index(axis) % 2 == 1


def first_core():
    return lax.axis_index("comp") == 0


def own_columns(sh, state_ref, x_ref, odd, dynamics):
    flip = jnp.where(odd & dynamics, -1.0, 1.0)
    cx = sh.cx
    for ch in range(FIELDS):
        raw = [state_ref[pl.ds(ch * sh.lev * cx + i, sh.lev, stride=cx), :] for i in range(cx)]
        for k in range(cx):
            value = jnp.where(odd, raw[cx - 1 - k], raw[k])
            x_ref[ch * cx + k] = value * flip if ch in VEL_X else value


def send_kernel(sh, state_ref, xo_ref, xp_ref, m_ref):
    core0 = first_core()
    own_columns(sh, state_ref, xp_ref, is_odd("gx"), jnp.logical_not(core0))
    cx = sh.cx
    for part, (x_ref, flip) in enumerate(
        ((xo_ref, jnp.where(core0, -1.0, 1.0)), (xp_ref, jnp.where(core0, 1.0, -1.0)))
    ):
        for ch in range(FIELDS):
            for d in range(HALO):
                value = jnp.where(core0, x_ref[ch * cx + cx - 1 - d], x_ref[ch * cx + d])
                m_ref[part * sh.halo_tiles + ch * HALO + d] = value * flip if ch in VEL_X else value
    m_ref[2 * sh.halo_tiles] = xo_ref[sh.mask_tile]


def edge_kernel(sh, xo_ref, xp_ref, e_ref):
    lane = sh.lanes()
    core0 = first_core()
    cx = sh.cx
    edges = [jnp.zeros((sh.lev, sh.rows), jnp.float32)] * sh.edge_tiles
    for comp in range(2):
        for ch in range(FIELDS):
            t, q = sh.edge_at(comp, ch)
            for k in range(cx):
                own, partner = xo_ref[ch * cx + k], xp_ref[ch * cx + k]
                value = jnp.where(core0, own, partner) if comp == 0 else jnp.where(core0, partner, own)
                edges[t] = sh.edge_place(edges[t], value, k + HALO, q, lane)
    for q in range(2):
        for k in range(cx):
            value = sh.row(xo_ref, sh.mask_tile, q * cx + k)
            edges[-1] = sh.edge_place(edges[-1], value, k + HALO, q, lane)
    for t in range(sh.edge_tiles):
        e_ref[t] = edges[t]


def merge_kernel(sh, e_ref, rx_ref, rp_ref, eo_ref):
    lane = sh.lanes()
    core0 = first_core()
    cx = sh.cx
    edges = [e_ref[t] for t in range(sh.edge_tiles)]
    sides = (
        (rx_ref, rp_ref, 0, lambda d: cx + HALO + d, lambda d: cx - 1 - d),
        (rp_ref, rx_ref, 1, lambda d: HALO - 1 - d, lambda d: d),
    )
    for on_first, on_second, side, place, source in sides:
        for comp in range(2):
            for ch in range(FIELDS):
                t, q = sh.edge_at(comp, ch)
                for d in range(HALO):
                    at = sh.halo_at(comp, side, ch, d)
                    value = jnp.where(core0, on_first[at], on_second[at])
                    edges[t] = sh.edge_place(edges[t], value, place(d), q, lane)
        for q in range(2):
            for d in range(HALO):
                at = q * cx + source(d)
                value = jnp.where(
                    core0,
                    sh.row(on_first, 2 * sh.halo_tiles, at),
                    sh.row(on_second, 2 * sh.halo_tiles, at),
                )
                edges[-1] = sh.edge_place(edges[-1], value, place(d), q, lane)
    for t in range(sh.edge_tiles):
        eo_ref[t] = edges[t]


STRIP = "strip"


class Field:
    def __init__(self, sh, lane, col, strip):
        self.sh, self.lane, self.col, self.strip = sh, lane, col, strip

    def centre(self, site):
        return self.strip() if site == STRIP else self.col(site)

    def east(self, site):
        return lane_roll(self.strip(), -self.sh.group) if site == STRIP else self.col(site + 1)

    def west(self, site):
        return lane_roll(self.strip(), self.sh.group) if site == STRIP else self.col(site - 1)

    def north(self, site):
        if site == STRIP:
            return lane_roll(self.strip(), -1)
        sh = self.sh
        end = sh.rows - 1
        beyond = lane_roll(self.strip(), end - (site * sh.group + sh.half + HALO))
        return jnp.where(self.lane == end, beyond, lane_roll(self.col(site), -1))

    def south(self, site):
        if site == STRIP:
            return lane_roll(self.strip(), 1)
        sh = self.sh
        beyond = lane_roll(self.strip(), -(site * sh.group + HALO - 1))
        return jnp.where(self.lane == 0, beyond, lane_roll(self.col(site), 1))

    def around(self, site):
        return self.east(site), self.west(site), self.north(site), self.south(site)


def step_kernel(sh, xo, xp, rx, rp, edges, y, yp, out_ref, strips, fresh, masks):
    core0 = first_core()
    lane, level = sh.lanes(), sh.levels()
    cx, group = sh.cx, sh.group
    gy, ny = lax.axis_index("gy"), lax.axis_size("gy")
    odd_x = lax.axis_index("gx") % 2 == 1
    mirror = jnp.where(odd_x, -1.0, 1.0)
    even_y = gy % 2 == 0
    slot = lane % (2 * HALO)
    in_group = lane % group
    first_step = list(range(1, sh.cols - 1))
    own = list(range(HALO, HALO + cx))
    sites = first_step + [STRIP]
    zero = jnp.zeros((sh.lev, sh.rows), jnp.float32)

    def cumulate(x):
        reach = 1
        while reach < sh.lev:
            x = x + jnp.where(level >= reach, level_roll(x, reach), 0.0)
            reach *= 2
        return x

    def place(site):
        return sh.cols if site == STRIP else site

    def build_strips(base, tiles, channels):
        for t in tiles:
            a, b = jnp.where(core0, y[t], yp[t]), jnp.where(core0, yp[t], y[t])
            mine = edges[t]
            left = jnp.where(gy > 0, jnp.where(even_y, b, a), zero)
            right = jnp.where(gy < ny - 1, jnp.where(even_y, a, b), zero)
            low = jnp.where(slot < HALO, left, mine)
            high = jnp.where(slot < HALO, mine, right)
            for q in range(channels):
                at = q * 2 * HALO
                strips[base + (t - tiles[0]) * sh.per_tile + q] = jnp.where(
                    in_group < sh.half, lane_roll(low, -at), lane_roll(high, sh.half - at)
                )

    build_strips(0, range(2 * sh.field_tiles), sh.per_tile)
    build_strips(2 * FIELDS, [sh.edge_tiles - 1], 2)

    def mask_row(kind, j):
        if HALO <= j < HALO + cx:
            return sh.row(xo, sh.mask_tile, kind * cx + j - HALO)
        if j < HALO:
            first, second, at = rp, rx, HALO - 1 - j
        else:
            first, second, at = rx, rp, cx - 1 - (j - HALO - cx)
        tile = 2 * sh.halo_tiles
        return jnp.where(
            core0, sh.row(first, tile, kind * cx + at), sh.row(second, tile, kind * cx + at)
        )

    levelf = level.astype(jnp.float32)

    def depth_at(site):
        return strips[2 * FIELDS + 1] if site == STRIP else mask_row(1, site)

    def irr_at(site):
        return strips[2 * FIELDS] if site == STRIP else mask_row(0, site)

    for j in range(sh.cols):
        masks[j] = jnp.where(levelf < depth_at(j), 1.0, 0.0)
    masks[sh.cols] = jnp.where(levelf < depth_at(STRIP), 1.0, 0.0)
    wet = Field(sh, lane, lambda j: masks[j], lambda: masks[sh.cols])
    face_base = sh.cols + 1
    for site in sites:
        w = wet.centre(site)
        for n, value in enumerate(wet.around(site)):
            masks[face_base + place(site) * 4 + n] = w * value

    def faces(site):
        return [masks[face_base + place(site) * 4 + n] for n in range(4)]

    def raw(x, sides, comp, ch):
        def col(j):
            if HALO <= j < HALO + cx:
                return x[ch * cx + j - HALO]
            if j < HALO:
                return sides[1][sh.halo_at(comp, 1, ch, HALO - 1 - j)]
            return sides[0][sh.halo_at(comp, 0, ch, j - HALO - cx)]

        return Field(sh, lane, col, lambda: strips[comp * FIELDS + ch])

    slots = sh.cols + 1

    def stored(index):
        return Field(
            sh, lane, lambda j: fresh[index * slots + j], lambda: fresh[index * slots + sh.cols]
        )

    def store(index, site, value):
        fresh[index * slots + place(site)] = value

    def density_of(temp, salt, w):
        return (0.8 * salt - 0.2 * temp) * w

    def speeds(u, v, site, m):
        uc, vc = u.centre(site), v.centre(site)
        qe = 0.025 * (uc + u.east(site)) * m[0]
        qw = 0.025 * (uc + u.west(site)) * m[1]
        qn = 0.025 * (vc + v.north(site)) * m[2]
        qs = 0.025 * (vc + v.south(site)) * m[3]
        return qe, qw, qn, qs, (qw - qe) + (qs - qn)

    def laplacian(f, site, m, total):
        e, w, n, s = f.around(site)
        return (m[0] * e + m[1] * w) + (m[2] * n + m[3] * s) - total * f.centre(site)

    def coriolis(site):
        if site == STRIP:
            row = jnp.where(in_group < sh.half, in_group - HALO, sh.rows - HALO + in_group - sh.half)
        else:
            row = lane
        row = (row + gy * sh.rows).astype(jnp.float32)
        return mirror * (0.3 + 0.4 * row / (ny * sh.rows))

    def dynamics(d, pressure, site, heat, q, m, full):
        w = wet.centre(site)
        total = (m[0] + m[1]) + (m[2] + m[3])
        uc, vc = d[U].centre(site), d[V].centre(site)
        after = {}
        if "vel" in full:
            pc = pressure.centre(site)
            pe, pw, pn, ps = pressure.around(site)
            push_x = 0.1 * (m[0] * (pe - pc) + m[1] * (pc - pw))
            push_y = 0.1 * (m[2] * (pn - pc) + m[3] * (pc - ps))
            f = 0.2 * coriolis(site) * w
            after[U] = d[UB].centre(site) + (f * vc - push_x + 0.04 * laplacian(d[UB], site, m, total))
            after[V] = d[VB].centre(site) + (
                0.04 * laplacian(d[VB], site, m, total) - f * uc - push_y
            )
        if "tracer" in full:
            qe, qw, qn, qs, qc = q
            for now, before in ((TEMP, TB), (SALT, SB)):
                e, w_, n, s = d[now].around(site)
                carried = (qw * w_ - qe * e) + (qs * s - qn * n) + qc * d[now].centre(site)
                change = 2.0 * carried + 0.04 * laplacian(d[before], site, m, total)
                if now == TEMP:
                    change = change + 0.6 * heat
                after[now] = d[before].centre(site) + change
        return after

    def filtered(d, site, ch, after):
        w = wet.centre(site)
        now, before = d[ch].centre(site), d[ch + 4].centre(site)
        return now + 0.1 * (before - 2.0 * now + after) * w

    def optics(c2, c3):
        absorb = 0.08 + 0.05 * (jnp.abs(c2) + jnp.abs(c3))
        return absorb, cumulate(absorb)

    def heating(absorb, depthsum, site):
        fade = jnp.exp(-depthsum)
        above = jnp.where(level == 0, 1.0, level_roll(fade, 1))
        return irr_at(site) * wet.centre(site) * (above - fade)

    def light(absorb, depthsum, site):
        return irr_at(site) * jnp.exp(0.5 * absorb - depthsum)

    def mixing(temp, salt, site):
        rho = density_of(temp, salt, wet.centre(site))
        below = level_roll(rho, -1)
        wet_below = jnp.where(levelf + 1.0 < depth_at(site), 1.0, 0.0)
        return (0.005 + 0.1 / (1.0 + 4.0 * jnp.maximum(below - rho, 0.0))) * wet_below

    def reactions(c, temp, lit, which):
        nn, na = jnp.abs(c[0]), jnp.abs(c[1])
        base = jnp.exp(0.06 * temp) * (lit / (lit + 0.5))
        total = nn + na
        small = 0.6 * base * c[2] / (0.2 + total)
        large = 0.9 * base * c[3] / (0.8 + total)
        graze = 0.8 * c[4] / (1.0 + (jnp.abs(c[2]) + jnp.abs(c[3])))
        gs, gl = graze * c[2], graze * c[3]
        up_s, up_l = small * total, large * total
        r = {2: up_s - gs - 0.1 * c[2], 3: up_l - gl - 0.1 * c[3]}
        if len(which) > 2:
            both = small + large
            remin = 0.3 * c[5] + 0.1 * c[6]
            nitrify = 0.2 * c[1]
            r[0] = nitrify - both * nn
            r[1] = remin + 0.1 * c[4] - nitrify - both * na
            r[4] = 0.7 * (gs + gl) - 0.25 * c[4]
            r[5] = 0.1 * c[2] + 0.3 * gs - 0.3 * c[5]
            r[6] = 0.1 * c[3] + 0.15 * c[4] + 0.3 * gl - 0.1 * c[6]
            r[7] = 1.3 * (up_s + up_l) - (remin + 2.0 * nitrify)
        return r

    def tracer_step(c, site, q, m, kappa, temp, lit, which, emit):
        w = wet.centre(site)
        qe, qw, qn, qs, qc = q
        total = (m[0] + m[1]) + (m[2] + m[3])
        ke, kw = 0.02 * m[0] - qe, 0.02 * m[1] + qw
        kn, ks = 0.02 * m[2] - qn, 0.02 * m[3] + qs
        kc = (1.0 - 0.02 * total) + qc
        centre = {i: c[i].centre(site) for i in (which if len(which) > 2 else range(5))}
        r = reactions(centre, temp, lit, which)
        tenth = 0.1 * w
        for i in which:
            e, w_, n, s = c[i].around(site)
            here = centre[i]
            down = kappa * (level_roll(here, -1) - here)
            emit(
                i,
                kc * here
                + ((ke * e + kw * w_) + (kn * n + ks * s))
                + (down - level_roll(down, 1))
                + tenth * r[i],
            )

    def write(ch, k_values):
        for i in range(cx):
            out_ref[pl.ds(ch * sh.lev * cx + i, sh.lev, stride=cx), :] = jnp.where(
                odd_x, k_values[cx - 1 - i], k_values[i]
            )

    def make_pressure(d, index, all_sites):
        for site in all_sites:
            rho = density_of(d[TEMP].centre(site), d[SALT].centre(site), wet.centre(site))
            store(index, site, 0.1 * cumulate(rho))
        return stored(index)

    everywhere = list(range(sh.cols)) + [STRIP]

    @pl.when(lax.axis_index("comp") == 0)
    def _():
        d = [raw(xo, (rx, rp), 0, ch) for ch in range(FIELDS)]
        c = [raw(xp, (rx, rp), 1, ch) for ch in range(FIELDS)]
        extra = FIELDS
        pressure = make_pressure(d, extra + 2, everywhere)
        for site in sites:
            m = faces(site)
            q = speeds(d[U], d[V], site, m)
            optic = optics(c[2].centre(site), c[3].centre(site))
            heat = heating(*optic, site)
            after = dynamics(d, pressure, site, heat, q, m, ("vel", "tracer"))
            for ch, value in after.items():
                store(ch, site, value)
                store(ch + 4, site, filtered(d, site, ch, value))
            if site in own:
                temp, salt = d[TEMP].centre(site), d[SALT].centre(site)
                tracer_step(
                    c, site, q, m, mixing(temp, salt, site), temp, light(*optic, site), (2, 3),
                    lambda i, value: store(extra + i - 2, site, value),
                )
        d = [stored(ch) for ch in range(FIELDS)]
        pressure = make_pressure(d, extra + 2, first_step + [STRIP])
        done = {}
        for site in own:
            m = faces(site)
            q = speeds(d[U], d[V], site, m)
            optic = optics(stored(extra).centre(site), stored(extra + 1).centre(site))
            heat = heating(*optic, site)
            after = dynamics(d, pressure, site, heat, q, m, ("vel", "tracer"))
            for ch, value in after.items():
                done[ch, site] = value
                done[ch + 4, site] = filtered(d, site, ch, value)
        for ch in range(FIELDS):
            factor = mirror if ch in VEL_X else 1.0
            write(ch, [done[ch, site] * factor if ch in VEL_X else done[ch, site] for site in own])

    @pl.when(lax.axis_index("comp") != 0)
    def _():
        d = [raw(xp, (rp, rx), 0, ch) for ch in range(FIELDS)]
        c = [raw(xo, (rp, rx), 1, ch) for ch in range(FIELDS)]
        extra = FIELDS
        pressure = make_pressure(d, extra + 4, everywhere)
        for site in sites:
            m = faces(site)
            q = speeds(d[U], d[V], site, m)
            optic = optics(c[2].centre(site), c[3].centre(site))
            temp, salt = d[TEMP].centre(site), d[SALT].centre(site)
            inner = site in own
            heat = heating(*optic, site) if inner else None
            full = ("vel", "tracer") if inner else ("vel",)
            after = dynamics(d, pressure, site, heat, q, m, full)
            for ch, value in after.items():
                store(extra + ch, site, value)
            tracer_step(
                c, site, q, m, mixing(temp, salt, site), temp, light(*optic, site), range(FIELDS),
                lambda i, value: store(i, site, value),
            )
        c = [stored(ch) for ch in range(FIELDS)]
        d = [stored(extra + ch) for ch in range(4)]
        done = {}
        for site in own:
            m = faces(site)
            q = speeds(d[U], d[V], site, m)
            optic = optics(c[2].centre(site), c[3].centre(site))
            temp, salt = d[TEMP].centre(site), d[SALT].centre(site)

            def emit(i, value):
                done[i, site] = value

            tracer_step(
                c, site, q, m, mixing(temp, salt, site), temp, light(*optic, site), range(FIELDS),
                emit,
            )
        for ch in range(FIELDS):
            write(ch, [done[ch, site] for site in own])


def tiles(sh, n):
    return jax.ShapeDtypeStruct((n, sh.lev, sh.rows), jnp.float32)


def call(kernel, sh, outs, args, flops, scratch=(), source=pltpu.VMEM):
    spec = pl.BlockSpec(memory_space=pltpu.VMEM)
    size = sum(a.size for a in args) + sum(o.size for o in outs)
    return pl.pallas_call(
        lambda *refs: kernel(sh, *refs),
        out_shape=outs,
        in_specs=[pl.BlockSpec(memory_space=source)] * len(args),
        out_specs=[spec] * len(outs),
        scratch_shapes=list(scratch),
        compiler_params=pltpu.CompilerParams(vmem_limit_bytes=16 << 20),
        cost_estimate=pl.CostEstimate(flops=flops, bytes_accessed=4 * size, transcendentals=0),
    )(*args)


def local(ocean_state, irradiance, land_mask, bottom_level):
    fields, lev, cx, rows = ocean_state.shape
    assert fields == FIELDS
    sh = Shape(lev, cx, rows)
    nx, ny = lax.axis_size("gx"), lax.axis_size("gy")
    assert nx % 2 == 0 and ny % 2 == 0
    axes = ("comp", "gy", "gx")

    def send(value, target):
        pairs = []
        for c in range(2):
            for y in range(ny):
                for x in range(nx):
                    tc, ty, tx = target(c, y, x)
                    pairs.append(((c * ny + y) * nx + x, (tc * ny + ty) * nx + tx))
        return lax.ppermute(value, axes, pairs)

    def odd_pair(i, n):
        return (i + 1) % n if i % 2 else (i - 1) % n

    def pair(i, n, core):
        return i ^ 1 if core == 0 else odd_pair(i, n)

    def along_x(v):
        return send(v, lambda c, y, x: (c, y, pair(x, nx, c)))

    def along_y(v):
        return send(v, lambda c, y, x: (c, pair(y, ny, c), x))

    def swap(v):
        return send(v, lambda c, y, x: (1 - c, y, x))

    flat = ocean_state.reshape(fields * lev * cx, rows)
    partner = swap(flat)
    inputs = (flat, irradiance, land_mask, bottom_level)
    (xo,) = call(
        load_kernel,
        sh,
        [tiles(sh, fields * cx + 1)],
        tuple(pltpu.with_memory_space_constraint(a, pltpu.HBM) for a in inputs),
        100_000,
        scratch=[pltpu.VMEM(a.shape, a.dtype) for a in inputs] + [pltpu.SemaphoreType.DMA((4,))],
        source=pltpu.HBM,
    )
    message = 2 * sh.halo_tiles + 1
    xp, m = call(
        send_kernel, sh, [tiles(sh, fields * cx), tiles(sh, message)], (partner, xo), 100_000
    )
    rx = along_x(m)
    (e0,) = call(edge_kernel, sh, [tiles(sh, sh.edge_tiles)], (xo, xp), 100_000)
    rp = swap(rx)
    (e1,) = call(merge_kernel, sh, [tiles(sh, sh.edge_tiles)], (e0, rx, rp), 100_000)
    y = along_y(e1)
    yp = swap(y)
    width = sh.cols + 1
    (out,) = call(
        step_kernel,
        sh,
        [jax.ShapeDtypeStruct(flat.shape, jnp.float32)],
        (xo, xp, rx, rp, e1, y, yp),
        10_000_000,
        scratch=[
            pltpu.VMEM((2 * FIELDS + 2, lev, rows), jnp.float32),
            pltpu.VMEM(((FIELDS + 5) * width, lev, rows), jnp.float32),
            pltpu.VMEM((width + 4 * width, lev, rows), jnp.float32),
        ],
    )
    return out.reshape(ocean_state.shape)


def solution(mesh):
    return jax.shard_map(
        local,
        mesh=mesh,
        in_specs=(P("comp", None, "gx", "gy"), P("gx", "gy"), P("gx", "gy"), P("gx", "gy")),
        out_specs=P("comp", None, "gx", "gy"),
        check_vma=False,
    )
```

```python
import jax
import jax.numpy as jnp
from jax import lax
from jax.experimental import pallas as pl
from jax.experimental.pallas import tpu as pltpu
from jax.sharding import PartitionSpec as P


HALO = 2
FIELDS = 8
U, V, TEMP, SALT, UB, VB, TB, SB = range(FIELDS)
VEL_X = (U, UB)


def lane_roll(x, shift):
    shift %= x.shape[1]
    return pltpu.roll(x, shift, 1) if shift else x


def level_roll(x, shift):
    shift %= x.shape[0]
    return pltpu.roll(x, shift, 0) if shift else x


class Shape:
    def __init__(self, lev, cx, rows):
        self.lev, self.cx, self.rows = lev, cx, rows
        self.cols = cx + 2 * HALO
        self.group = rows // self.cols
        self.per_tile = self.group // (2 * HALO)
        self.half = self.group // 2
        self.field_tiles = -(-FIELDS // self.per_tile)
        self.edge_tiles = 2 * self.field_tiles + 1
        assert self.per_tile >= 2 and self.group >= 4 * HALO and 2 * cx <= lev
        assert self.cols * self.group == rows
        self.mask_tile = FIELDS * cx
        self.halo_tiles = FIELDS * HALO

    def lanes(self):
        return lax.broadcasted_iota(jnp.int32, (self.lev, self.rows), 1)

    def levels(self):
        return lax.broadcasted_iota(jnp.int32, (self.lev, self.rows), 0)

    def row(self, ref, tile, r):
        return jnp.broadcast_to(ref[tile, r : r + 1, :], (self.lev, self.rows))

    def edge_at(self, comp, ch):
        t, q = divmod(ch, self.per_tile)
        return comp * self.field_tiles + t, q

    def halo_at(self, comp, side, ch, d):
        return (self.halo_tiles if comp == side else 0) + ch * HALO + d

    def edge_place(self, acc, value, j, channel, lane):
        at = j * self.group + channel * 2 * HALO + HALO
        return jnp.where((lane >= at - HALO) & (lane < at + HALO), lane_roll(value, at), acc)


def load_kernel(sh, *refs):
    sources, x_ref, e_ref, arrived, sem = refs[:4], refs[4], refs[5], refs[6:10], refs[10]
    copies = [
        pltpu.make_async_copy(a, b, sem.at[i]) for i, (a, b) in enumerate(zip(sources, arrived))
    ]
    for copy in copies:
        copy.start()
    for copy in copies:
        copy.wait()
    state_ref, irr_ref, land_ref, bottom_ref = arrived
    odd = is_odd("gx")
    edges = own_columns(sh, state_ref, x_ref, odd, first_core())
    cx = sh.cx
    lane = sh.lanes()
    depth = jnp.where(land_ref[...] == 1, bottom_ref[...], 0).astype(jnp.float32)
    last = jnp.zeros((sh.lev, sh.rows), jnp.float32)
    for q, value in enumerate((irr_ref[...], depth)):
        for k in range(cx):
            row = jnp.where(odd, value[cx - 1 - k : cx - k, :], value[k : k + 1, :])
            x_ref[sh.mask_tile, q * cx + k : q * cx + k + 1, :] = row
            wide = jnp.broadcast_to(row, (sh.lev, sh.rows))
            last = sh.edge_place(last, wide, k + HALO, q, lane)
    for t, edge in enumerate(edges + [last]):
        e_ref[t] = edge


def is_odd(axis):
    return lax.axis_index(axis) % 2 == 1


def first_core():
    return lax.axis_index("comp") == 0


def own_columns(sh, state_ref, x_ref, odd, dynamics):
    flip = jnp.where(odd & dynamics, -1.0, 1.0)
    cx = sh.cx
    lane = sh.lanes()
    edges = [jnp.zeros((sh.lev, sh.rows), jnp.float32)] * sh.field_tiles
    for ch in range(FIELDS):
        raw = [state_ref[pl.ds(ch * sh.lev * cx + i, sh.lev, stride=cx), :] for i in range(cx)]
        t, q = sh.edge_at(0, ch)
        for k in range(cx):
            value = jnp.where(odd, raw[cx - 1 - k], raw[k])
            if ch in VEL_X:
                value = value * flip
            x_ref[ch * cx + k] = value
            edges[t] = sh.edge_place(edges[t], value, k + HALO, q, lane)
    return edges


def send_kernel(sh, state_ref, xo_ref, eo_ref, xp_ref, e_ref, m_ref):
    core0 = first_core()
    edges = own_columns(sh, state_ref, xp_ref, is_odd("gx"), jnp.logical_not(core0))
    cx = sh.cx
    for t in range(sh.field_tiles):
        own = eo_ref[t]
        e_ref[t] = jnp.where(core0, own, edges[t])
        e_ref[sh.field_tiles + t] = jnp.where(core0, edges[t], own)
    e_ref[sh.edge_tiles - 1] = eo_ref[sh.field_tiles]
    for part, (x_ref, flip) in enumerate(
        ((xo_ref, jnp.where(core0, -1.0, 1.0)), (xp_ref, jnp.where(core0, 1.0, -1.0)))
    ):
        for ch in range(FIELDS):
            for d in range(HALO):
                value = jnp.where(core0, x_ref[ch * cx + d], x_ref[ch * cx + cx - 1 - d])
                m_ref[part * sh.halo_tiles + ch * HALO + d] = value * flip if ch in VEL_X else value
    m_ref[2 * sh.halo_tiles] = xo_ref[sh.mask_tile]


def merge_kernel(sh, e_ref, a_ref, b_ref, eo_ref):
    lane = sh.lanes()
    core0 = first_core()
    column, place = lane // sh.group, lane % sh.group // (2 * HALO)
    for t in range(sh.edge_tiles):
        got = a_ref[t], b_ref[t]
        after, before = jnp.where(core0, got[0], got[1]), jnp.where(core0, got[1], got[0])
        for ch in VEL_X:
            if sh.edge_at(0, ch)[0] == t:
                flip = jnp.where(place == sh.edge_at(0, ch)[1], -1.0, 1.0)
                after, before = after * flip, before * flip
        edge = e_ref[t]
        for d in range(HALO):
            shift = (2 * d + 1) * sh.group
            edge = jnp.where(column == sh.cx + HALO + d, lane_roll(after, shift), edge)
            edge = jnp.where(column == HALO - 1 - d, lane_roll(before, -shift), edge)
        eo_ref[t] = edge


STRIP = "strip"


class Field:
    def __init__(self, sh, lane, col, strip):
        self.sh, self.lane, self.col, self.strip = sh, lane, col, strip

    def centre(self, site):
        return self.strip() if site == STRIP else self.col(site)

    def east(self, site):
        return lane_roll(self.strip(), -self.sh.group) if site == STRIP else self.col(site + 1)

    def west(self, site):
        return lane_roll(self.strip(), self.sh.group) if site == STRIP else self.col(site - 1)

    def north(self, site):
        if site == STRIP:
            return lane_roll(self.strip(), -1)
        sh = self.sh
        end = sh.rows - 1
        beyond = lane_roll(self.strip(), end - (site * sh.group + sh.half + HALO))
        return jnp.where(self.lane == end, beyond, lane_roll(self.col(site), -1))

    def south(self, site):
        if site == STRIP:
            return lane_roll(self.strip(), 1)
        sh = self.sh
        beyond = lane_roll(self.strip(), -(site * sh.group + HALO - 1))
        return jnp.where(self.lane == 0, beyond, lane_roll(self.col(site), 1))

    def around(self, site):
        return self.east(site), self.west(site), self.north(site), self.south(site)


def step_kernel(sh, xo, xp, rx, rp, edges, y, yp, out_ref, strips, fresh, masks):
    core0 = first_core()
    lane, level = sh.lanes(), sh.levels()
    cx, group = sh.cx, sh.group
    gy, ny = lax.axis_index("gy"), lax.axis_size("gy")
    odd_x = lax.axis_index("gx") % 2 == 1
    mirror = jnp.where(odd_x, -1.0, 1.0)
    even_y = gy % 2 == 0
    slot = lane % (2 * HALO)
    in_group = lane % group
    first_step = list(range(1, sh.cols - 1))
    own = list(range(HALO, HALO + cx))
    sites = first_step + [STRIP]
    zero = jnp.zeros((sh.lev, sh.rows), jnp.float32)

    def cumulate(x):
        reach = 1
        while reach < sh.lev:
            x = x + jnp.where(level >= reach, level_roll(x, reach), 0.0)
            reach *= 2
        return x

    def place(site):
        return sh.cols if site == STRIP else site

    def build_strips(base, tiles, channels):
        for t in tiles:
            a, b = jnp.where(core0, y[t], yp[t]), jnp.where(core0, yp[t], y[t])
            mine = edges[t]
            left = jnp.where(gy > 0, jnp.where(even_y, b, a), zero)
            right = jnp.where(gy < ny - 1, jnp.where(even_y, a, b), zero)
            low = jnp.where(slot < HALO, left, mine)
            high = jnp.where(slot < HALO, mine, right)
            for q in range(channels):
                at = q * 2 * HALO
                strips[base + (t - tiles[0]) * sh.per_tile + q] = jnp.where(
                    in_group < sh.half, lane_roll(low, -at), lane_roll(high, sh.half - at)
                )

    build_strips(0, range(2 * sh.field_tiles), sh.per_tile)
    build_strips(2 * FIELDS, [sh.edge_tiles - 1], 2)

    def mask_row(kind, j):
        if HALO <= j < HALO + cx:
            return sh.row(xo, sh.mask_tile, kind * cx + j - HALO)
        if j < HALO:
            first, second, at = rx, rp, HALO - 1 - j
        else:
            first, second, at = rp, rx, cx - 1 - (j - HALO - cx)
        tile = 2 * sh.halo_tiles
        return jnp.where(
            core0, sh.row(first, tile, kind * cx + at), sh.row(second, tile, kind * cx + at)
        )

    levelf = level.astype(jnp.float32)

    def depth_at(site):
        return strips[2 * FIELDS + 1] if site == STRIP else mask_row(1, site)

    def irr_at(site):
        return strips[2 * FIELDS] if site == STRIP else mask_row(0, site)

    for j in range(sh.cols):
        masks[j] = jnp.where(levelf < depth_at(j), 1.0, 0.0)
    masks[sh.cols] = jnp.where(levelf < depth_at(STRIP), 1.0, 0.0)
    wet = Field(sh, lane, lambda j: masks[j], lambda: masks[sh.cols])
    face_base = sh.cols + 1
    for site in sites:
        w = wet.centre(site)
        for n, value in enumerate(wet.around(site)):
            masks[face_base + place(site) * 4 + n] = w * value

    def faces(site):
        return [masks[face_base + place(site) * 4 + n] for n in range(4)]

    def raw(x, sides, comp, ch):
        def col(j):
            if HALO <= j < HALO + cx:
                return x[ch * cx + j - HALO]
            if j < HALO:
                return sides[1][sh.halo_at(comp, 1, ch, HALO - 1 - j)]
            return sides[0][sh.halo_at(comp, 0, ch, j - HALO - cx)]

        return Field(sh, lane, col, lambda: strips[comp * FIELDS + ch])

    slots = sh.cols + 1

    def stored(index):
        return Field(
            sh, lane, lambda j: fresh[index * slots + j], lambda: fresh[index * slots + sh.cols]
        )

    def store(index, site, value):
        fresh[index * slots + place(site)] = value

    def density_of(temp, salt, w):
        return (0.8 * salt - 0.2 * temp) * w

    def speeds(u, v, site, m):
        uc, vc = u.centre(site), v.centre(site)
        qe = 0.025 * (uc + u.east(site)) * m[0]
        qw = 0.025 * (uc + u.west(site)) * m[1]
        qn = 0.025 * (vc + v.north(site)) * m[2]
        qs = 0.025 * (vc + v.south(site)) * m[3]
        return qe, qw, qn, qs, (qw - qe) + (qs - qn)

    def laplacian(f, site, m, total):
        e, w, n, s = f.around(site)
        return (m[0] * e + m[1] * w) + (m[2] * n + m[3] * s) - total * f.centre(site)

    def coriolis(site):
        if site == STRIP:
            row = jnp.where(in_group < sh.half, in_group - HALO, sh.rows - HALO + in_group - sh.half)
        else:
            row = lane
        row = (row + gy * sh.rows).astype(jnp.float32)
        return mirror * (0.3 + 0.4 * row / (ny * sh.rows))

    def dynamics(d, pressure, site, heat, q, m, full):
        w = wet.centre(site)
        total = (m[0] + m[1]) + (m[2] + m[3])
        uc, vc = d[U].centre(site), d[V].centre(site)
        after = {}
        if "vel" in full:
            pc = pressure.centre(site)
            pe, pw, pn, ps = pressure.around(site)
            push_x = 0.1 * (m[0] * (pe - pc) + m[1] * (pc - pw))
            push_y = 0.1 * (m[2] * (pn - pc) + m[3] * (pc - ps))
            f = 0.2 * coriolis(site) * w
            after[U] = d[UB].centre(site) + (f * vc - push_x + 0.04 * laplacian(d[UB], site, m, total))
            after[V] = d[VB].centre(site) + (
                0.04 * laplacian(d[VB], site, m, total) - f * uc - push_y
            )
        if "tracer" in full:
            qe, qw, qn, qs, qc = q
            for now, before in ((TEMP, TB), (SALT, SB)):
                e, w_, n, s = d[now].around(site)
                carried = (qw * w_ - qe * e) + (qs * s - qn * n) + qc * d[now].centre(site)
                change = 2.0 * carried + 0.04 * laplacian(d[before], site, m, total)
                if now == TEMP:
                    change = change + 0.6 * heat
                after[now] = d[before].centre(site) + change
        return after

    def filtered(d, site, ch, after):
        w = wet.centre(site)
        now, before = d[ch].centre(site), d[ch + 4].centre(site)
        return now + 0.1 * (before - 2.0 * now + after) * w

    def optics(c2, c3):
        absorb = 0.08 + 0.05 * (jnp.abs(c2) + jnp.abs(c3))
        return absorb, cumulate(absorb)

    def heating(absorb, depthsum, site):
        fade = jnp.exp(-depthsum)
        above = jnp.where(level == 0, 1.0, level_roll(fade, 1))
        return irr_at(site) * wet.centre(site) * (above - fade)

    def light(absorb, depthsum, site):
        return irr_at(site) * jnp.exp(0.5 * absorb - depthsum)

    def mixing(temp, salt, site):
        rho = density_of(temp, salt, wet.centre(site))
        below = level_roll(rho, -1)
        wet_below = jnp.where(levelf + 1.0 < depth_at(site), 1.0, 0.0)
        return (0.005 + 0.1 / (1.0 + 4.0 * jnp.maximum(below - rho, 0.0))) * wet_below

    def reactions(c, temp, lit, which):
        nn, na = jnp.abs(c[0]), jnp.abs(c[1])
        base = jnp.exp(0.06 * temp) * (lit / (lit + 0.5))
        total = nn + na
        small = 0.6 * base * c[2] / (0.2 + total)
        large = 0.9 * base * c[3] / (0.8 + total)
        graze = 0.8 * c[4] / (1.0 + (jnp.abs(c[2]) + jnp.abs(c[3])))
        gs, gl = graze * c[2], graze * c[3]
        up_s, up_l = small * total, large * total
        r = {2: up_s - gs - 0.1 * c[2], 3: up_l - gl - 0.1 * c[3]}
        if len(which) > 2:
            both = small + large
            remin = 0.3 * c[5] + 0.1 * c[6]
            nitrify = 0.2 * c[1]
            r[0] = nitrify - both * nn
            r[1] = remin + 0.1 * c[4] - nitrify - both * na
            r[4] = 0.7 * (gs + gl) - 0.25 * c[4]
            r[5] = 0.1 * c[2] + 0.3 * gs - 0.3 * c[5]
            r[6] = 0.1 * c[3] + 0.15 * c[4] + 0.3 * gl - 0.1 * c[6]
            r[7] = 1.3 * (up_s + up_l) - (remin + 2.0 * nitrify)
        return r

    def tracer_step(c, site, q, m, kappa, temp, lit, which, emit):
        w = wet.centre(site)
        qe, qw, qn, qs, qc = q
        total = (m[0] + m[1]) + (m[2] + m[3])
        ke, kw = 0.02 * m[0] - qe, 0.02 * m[1] + qw
        kn, ks = 0.02 * m[2] - qn, 0.02 * m[3] + qs
        kc = (1.0 - 0.02 * total) + qc
        centre = {i: c[i].centre(site) for i in (which if len(which) > 2 else range(5))}
        r = reactions(centre, temp, lit, which)
        tenth = 0.1 * w
        for i in which:
            e, w_, n, s = c[i].around(site)
            here = centre[i]
            down = kappa * (level_roll(here, -1) - here)
            emit(
                i,
                kc * here
                + ((ke * e + kw * w_) + (kn * n + ks * s))
                + (down - level_roll(down, 1))
                + tenth * r[i],
            )

    def write(ch, k_values):
        for i in range(cx):
            out_ref[pl.ds(ch * sh.lev * cx + i, sh.lev, stride=cx), :] = jnp.where(
                odd_x, k_values[cx - 1 - i], k_values[i]
            )

    def make_pressure(d, index, all_sites):
        for site in all_sites:
            rho = density_of(d[TEMP].centre(site), d[SALT].centre(site), wet.centre(site))
            store(index, site, 0.1 * cumulate(rho))
        return stored(index)

    everywhere = list(range(sh.cols)) + [STRIP]

    @pl.when(lax.axis_index("comp") == 0)
    def _():
        d = [raw(xo, (rp, rx), 0, ch) for ch in range(FIELDS)]
        c = [raw(xp, (rp, rx), 1, ch) for ch in range(FIELDS)]
        extra = FIELDS
        pressure = make_pressure(d, extra + 2, everywhere)
        for site in sites:
            m = faces(site)
            q = speeds(d[U], d[V], site, m)
            optic = optics(c[2].centre(site), c[3].centre(site))
            heat = heating(*optic, site)
            after = dynamics(d, pressure, site, heat, q, m, ("vel", "tracer"))
            for ch, value in after.items():
                store(ch, site, value)
                store(ch + 4, site, filtered(d, site, ch, value))
            if site in own:
                temp, salt = d[TEMP].centre(site), d[SALT].centre(site)
                tracer_step(
                    c, site, q, m, mixing(temp, salt, site), temp, light(*optic, site), (2, 3),
                    lambda i, value: store(extra + i - 2, site, value),
                )
        d = [stored(ch) for ch in range(FIELDS)]
        pressure = make_pressure(d, extra + 2, first_step + [STRIP])
        done = {}
        for site in own:
            m = faces(site)
            q = speeds(d[U], d[V], site, m)
            optic = optics(stored(extra).centre(site), stored(extra + 1).centre(site))
            heat = heating(*optic, site)
            after = dynamics(d, pressure, site, heat, q, m, ("vel", "tracer"))
            for ch, value in after.items():
                done[ch, site] = value
                done[ch + 4, site] = filtered(d, site, ch, value)
        for ch in range(FIELDS):
            factor = mirror if ch in VEL_X else 1.0
            write(ch, [done[ch, site] * factor if ch in VEL_X else done[ch, site] for site in own])

    @pl.when(lax.axis_index("comp") != 0)
    def _():
        d = [raw(xp, (rx, rp), 0, ch) for ch in range(FIELDS)]
        c = [raw(xo, (rx, rp), 1, ch) for ch in range(FIELDS)]
        extra = FIELDS
        pressure = make_pressure(d, extra + 4, everywhere)
        for site in sites:
            m = faces(site)
            q = speeds(d[U], d[V], site, m)
            optic = optics(c[2].centre(site), c[3].centre(site))
            temp, salt = d[TEMP].centre(site), d[SALT].centre(site)
            inner = site in own
            heat = heating(*optic, site) if inner else None
            full = ("vel", "tracer") if inner else ("vel",)
            after = dynamics(d, pressure, site, heat, q, m, full)
            for ch, value in after.items():
                store(extra + ch, site, value)
            tracer_step(
                c, site, q, m, mixing(temp, salt, site), temp, light(*optic, site), range(FIELDS),
                lambda i, value: store(i, site, value),
            )
        c = [stored(ch) for ch in range(FIELDS)]
        d = [stored(extra + ch) for ch in range(4)]
        done = {}
        for site in own:
            m = faces(site)
            q = speeds(d[U], d[V], site, m)
            optic = optics(c[2].centre(site), c[3].centre(site))
            temp, salt = d[TEMP].centre(site), d[SALT].centre(site)

            def emit(i, value):
                done[i, site] = value

            tracer_step(
                c, site, q, m, mixing(temp, salt, site), temp, light(*optic, site), range(FIELDS),
                emit,
            )
        for ch in range(FIELDS):
            write(ch, [done[ch, site] for site in own])


def tiles(sh, n):
    return jax.ShapeDtypeStruct((n, sh.lev, sh.rows), jnp.float32)


def call(kernel, sh, outs, args, flops, scratch=(), source=pltpu.VMEM):
    spec = pl.BlockSpec(memory_space=pltpu.VMEM)
    size = sum(a.size for a in args) + sum(o.size for o in outs)
    return pl.pallas_call(
        lambda *refs: kernel(sh, *refs),
        out_shape=outs,
        in_specs=[pl.BlockSpec(memory_space=source)] * len(args),
        out_specs=[spec] * len(outs),
        scratch_shapes=list(scratch),
        compiler_params=pltpu.CompilerParams(vmem_limit_bytes=16 << 20),
        cost_estimate=pl.CostEstimate(flops=flops, bytes_accessed=4 * size, transcendentals=0),
    )(*args)


def local(ocean_state, irradiance, land_mask, bottom_level):
    fields, lev, cx, rows = ocean_state.shape
    assert fields == FIELDS
    sh = Shape(lev, cx, rows)
    nx, ny = lax.axis_size("gx"), lax.axis_size("gy")
    assert nx % 2 == 0 and ny % 2 == 0
    axes = ("comp", "gy", "gx")

    def send(value, target):
        pairs = []
        for c in range(2):
            for y in range(ny):
                for x in range(nx):
                    tc, ty, tx = target(c, y, x)
                    pairs.append(((c * ny + y) * nx + x, (tc * ny + ty) * nx + tx))
        return lax.ppermute(value, axes, pairs)

    def odd_pair(i, n):
        return (i + 1) % n if i % 2 else (i - 1) % n

    def pair(i, n, core):
        return i ^ 1 if core == 0 else odd_pair(i, n)

    def edges_x(v):
        return send(v, lambda c, y, x: (c, y, pair(x, nx, c)))

    def bulk_x(v):
        return send(v, lambda c, y, x: (c, y, pair(x, nx, 1 - c)))

    def along_y(v):
        return send(v, lambda c, y, x: (c, pair(y, ny, c), x))

    def swap(v):
        return send(v, lambda c, y, x: (1 - c, y, x))

    flat = ocean_state.reshape(fields * lev * cx, rows)
    partner = swap(flat)
    inputs = (flat, irradiance, land_mask, bottom_level)
    xo, eo = call(
        load_kernel,
        sh,
        [tiles(sh, fields * cx + 1), tiles(sh, sh.field_tiles + 1)],
        tuple(pltpu.with_memory_space_constraint(a, pltpu.HBM) for a in inputs),
        100_000,
        scratch=[pltpu.VMEM(a.shape, a.dtype) for a in inputs] + [pltpu.SemaphoreType.DMA((4,))],
        source=pltpu.HBM,
    )
    edge, message = tiles(sh, sh.edge_tiles), tiles(sh, 2 * sh.halo_tiles + 1)
    xp, e0, m = call(
        send_kernel, sh, [tiles(sh, fields * cx), edge, message], (partner, xo, eo), 100_000
    )
    ex = edges_x(e0)
    rx = bulk_x(m)
    ep = swap(ex)
    (e1,) = call(merge_kernel, sh, [edge], (e0, ex, ep), 10_000)
    y = along_y(e1)
    rp = swap(rx)
    yp = swap(y)
    width = sh.cols + 1
    (out,) = call(
        step_kernel,
        sh,
        [jax.ShapeDtypeStruct(flat.shape, jnp.float32)],
        (xo, xp, rx, rp, e1, y, yp),
        10_000_000,
        scratch=[
            pltpu.VMEM((2 * FIELDS + 2, lev, rows), jnp.float32),
            pltpu.VMEM(((FIELDS + 5) * width, lev, rows), jnp.float32),
            pltpu.VMEM((width + 4 * width, lev, rows), jnp.float32),
        ],
    )
    return out.reshape(ocean_state.shape)


def solution(mesh):
    return jax.shard_map(
        local,
        mesh=mesh,
        in_specs=(P("comp", None, "gx", "gy"), P("gx", "gy"), P("gx", "gy"), P("gx", "gy")),
        out_specs=P("comp", None, "gx", "gy"),
        check_vma=False,
    )
```

```python
import jax
import jax.numpy as jnp
from jax import lax
from jax.experimental import pallas as pl
from jax.experimental.pallas import tpu as pltpu
from jax.sharding import PartitionSpec as P


HALO = 2
FIELDS = 8
U, V, TEMP, SALT, UB, VB, TB, SB = range(FIELDS)
VEL_X = (U, UB)


def lane_roll(x, shift):
    shift %= x.shape[1]
    return pltpu.roll(x, shift, 1) if shift else x


def level_roll(x, shift):
    shift %= x.shape[0]
    return pltpu.roll(x, shift, 0) if shift else x


class Shape:
    def __init__(self, lev, cx, rows):
        self.lev, self.cx, self.rows = lev, cx, rows
        self.cols = cx + 2 * HALO
        self.group = rows // self.cols
        self.per_tile = self.group // (2 * HALO)
        self.half = self.group // 2
        self.field_tiles = -(-FIELDS // self.per_tile)
        self.edge_tiles = 2 * self.field_tiles + 1
        assert self.per_tile >= 2 and self.group >= 4 * HALO and 2 * cx <= lev
        assert self.cols * self.group == rows
        self.mask_tile = FIELDS * cx
        self.halo_tiles = FIELDS * HALO

    def lanes(self):
        return lax.broadcasted_iota(jnp.int32, (self.lev, self.rows), 1)

    def levels(self):
        return lax.broadcasted_iota(jnp.int32, (self.lev, self.rows), 0)

    def row(self, ref, tile, r):
        return jnp.broadcast_to(ref[tile, r : r + 1, :], (self.lev, self.rows))

    def edge_at(self, comp, ch):
        t, q = divmod(ch, self.per_tile)
        return comp * self.field_tiles + t, q

    def halo_at(self, comp, side, ch, d):
        return (self.halo_tiles if comp == side else 0) + ch * HALO + d

    def edge_place(self, acc, value, j, channel, lane):
        at = j * self.group + channel * 2 * HALO + HALO
        return jnp.where((lane >= at - HALO) & (lane < at + HALO), lane_roll(value, at), acc)


def load_kernel(sh, *refs):
    sources, x_ref, e_ref, arrived, sem = refs[:4], refs[4], refs[5], refs[6:10], refs[10]
    copies = [
        pltpu.make_async_copy(a, b, sem.at[i]) for i, (a, b) in enumerate(zip(sources, arrived))
    ]
    for copy in copies:
        copy.start()
    for copy in copies:
        copy.wait()
    state_ref, irr_ref, land_ref, bottom_ref = arrived
    odd = is_odd("gx")
    edges = own_columns(sh, state_ref, x_ref, odd, first_core())
    cx = sh.cx
    lane = sh.lanes()
    depth = jnp.where(land_ref[...] == 1, bottom_ref[...], 0).astype(jnp.float32)
    last = jnp.zeros((sh.lev, sh.rows), jnp.float32)
    for q, value in enumerate((irr_ref[...], depth)):
        for k in range(cx):
            row = jnp.where(odd, value[cx - 1 - k : cx - k, :], value[k : k + 1, :])
            x_ref[sh.mask_tile, q * cx + k : q * cx + k + 1, :] = row
            wide = jnp.broadcast_to(row, (sh.lev, sh.rows))
            last = sh.edge_place(last, wide, k + HALO, q, lane)
    for t, edge in enumerate(edges + [last]):
        e_ref[t] = edge


def is_odd(axis):
    return lax.axis_index(axis) % 2 == 1


def first_core():
    return lax.axis_index("comp") == 0


def own_columns(sh, state_ref, x_ref, odd, dynamics):
    flip = jnp.where(odd & dynamics, -1.0, 1.0)
    cx = sh.cx
    lane = sh.lanes()
    edges = [jnp.zeros((sh.lev, sh.rows), jnp.float32)] * sh.field_tiles
    for ch in range(FIELDS):
        raw = [state_ref[pl.ds(ch * sh.lev * cx + i, sh.lev, stride=cx), :] for i in range(cx)]
        t, q = sh.edge_at(0, ch)
        for k in range(cx):
            value = jnp.where(odd, raw[cx - 1 - k], raw[k])
            if ch in VEL_X:
                value = value * flip
            x_ref[ch * cx + k] = value
            edges[t] = sh.edge_place(edges[t], value, k + HALO, q, lane)
    return edges


def send_kernel(sh, state_ref, xo_ref, eo_ref, xp_ref, e_ref, m_ref):
    core0 = first_core()
    edges = own_columns(sh, state_ref, xp_ref, is_odd("gx"), jnp.logical_not(core0))
    cx = sh.cx
    for t in range(sh.field_tiles):
        own = eo_ref[t]
        e_ref[t] = jnp.where(core0, own, edges[t])
        e_ref[sh.field_tiles + t] = jnp.where(core0, edges[t], own)
    e_ref[sh.edge_tiles - 1] = eo_ref[sh.field_tiles]
    for part, (x_ref, flip) in enumerate(
        ((xo_ref, jnp.where(core0, -1.0, 1.0)), (xp_ref, jnp.where(core0, 1.0, -1.0)))
    ):
        for ch in range(FIELDS):
            for d in range(HALO):
                value = jnp.where(core0, x_ref[ch * cx + d], x_ref[ch * cx + cx - 1 - d])
                m_ref[part * sh.halo_tiles + ch * HALO + d] = value * flip if ch in VEL_X else value
    m_ref[2 * sh.halo_tiles] = xo_ref[sh.mask_tile]


def merge_kernel(sh, e_ref, a_ref, b_ref, eo_ref):
    lane = sh.lanes()
    core0 = first_core()
    column, place = lane // sh.group, lane % sh.group // (2 * HALO)
    for t in range(sh.edge_tiles):
        got = a_ref[t], b_ref[t]
        after, before = jnp.where(core0, got[0], got[1]), jnp.where(core0, got[1], got[0])
        for ch in VEL_X:
            if sh.edge_at(0, ch)[0] == t:
                flip = jnp.where(place == sh.edge_at(0, ch)[1], -1.0, 1.0)
                after, before = after * flip, before * flip
        edge = e_ref[t]
        for d in range(HALO):
            shift = (2 * d + 1) * sh.group
            edge = jnp.where(column == sh.cx + HALO + d, lane_roll(after, shift), edge)
            edge = jnp.where(column == HALO - 1 - d, lane_roll(before, -shift), edge)
        eo_ref[t] = edge


STRIP = "strip"


class Field:
    def __init__(self, sh, lane, col=None, strip=None, seam=None, rough=None):
        self.sh, self.lane, self.col, self.strip = sh, lane, col, strip
        self.seam, self.rough = seam, rough

    def centre(self, site):
        return self.strip() if site == STRIP else self.col(site)

    def east(self, site):
        return lane_roll(self.strip(), -self.sh.group) if site == STRIP else self.col(site + 1)

    def west(self, site):
        return lane_roll(self.strip(), self.sh.group) if site == STRIP else self.col(site - 1)

    def along_rows(self, site):
        inner = site == STRIP or self.rough is None
        value = self.centre(site) if inner else self.rough(site)
        north, south = lane_roll(value, -1), lane_roll(value, 1)
        if site == STRIP or self.seam is None:
            return north, south
        beyond = self.seam(site)
        more = 0 if inner else 1
        last = self.lane >= self.sh.rows - 1 - more
        return jnp.where(last, beyond, north), jnp.where(self.lane <= more, beyond, south)

    def around(self, site):
        return (self.east(site), self.west(site)) + self.along_rows(site)


GRAZED = (FIELDS, FIELDS + 1)
FLOW = tuple(FIELDS + ch for ch in (U, V, TEMP, SALT))
PRESSURE = FIELDS + 2
FRESH = FIELDS + 4


class Model:
    def __init__(self, sh):
        self.sh = sh
        self.lane, self.level = sh.lanes(), sh.levels()
        self.levelf = self.level.astype(jnp.float32)
        self.in_group = self.lane % sh.group
        self.core0 = first_core()
        self.odd_x = is_odd("gx")
        self.mirror = jnp.where(self.odd_x, -1.0, 1.0)
        self.gy, self.ny = lax.axis_index("gy"), lax.axis_size("gy")
        self.first_step = list(range(1, sh.cols - 1))
        self.own = list(range(HALO, HALO + sh.cx))
        self.n_sites = len(self.first_step)

    def fresh_at(self, index, site):
        return index * self.n_sites + site - 1

    def cumulate(self, x):
        reach = 1
        while reach < self.sh.lev:
            x = x + jnp.where(self.level >= reach, level_roll(x, reach), 0.0)
            reach *= 2
        return x

    def wet_of(self, depth):
        return jnp.where(self.levelf < depth, 1.0, 0.0)

    def faces(self, site):
        w = self.wet.centre(site)
        return [w * value for value in self.wet.around(site)]

    def density(self, d, site):
        rho = 0.8 * d[SALT].centre(site) - 0.2 * d[TEMP].centre(site)
        return rho * self.wet.centre(site)

    def pressure(self, d, site):
        return 0.1 * self.cumulate(self.density(d, site))

    def speeds(self, u, v, site, m):
        uc, vc = u.centre(site), v.centre(site)
        north, south = v.along_rows(site)
        qe = 0.025 * (uc + u.east(site)) * m[0]
        qw = 0.025 * (uc + u.west(site)) * m[1]
        qn = 0.025 * (vc + north) * m[2]
        qs = 0.025 * (vc + south) * m[3]
        return qe, qw, qn, qs, (qw - qe) + (qs - qn)

    def laplacian(self, f, site, m, total):
        e, w, n, s = f.around(site)
        return (m[0] * e + m[1] * w) + (m[2] * n + m[3] * s) - total * f.centre(site)

    def coriolis(self, site):
        sh, at = self.sh, self.in_group
        row = self.lane
        if site == STRIP:
            row = jnp.where(at < sh.half, at - HALO, sh.rows - HALO + at - sh.half)
        row = (row + self.gy * sh.rows).astype(jnp.float32)
        return self.mirror * (0.3 + 0.4 * row / (self.ny * sh.rows))

    def dynamics(self, d, pressure, site, heat, q, m):
        w = self.wet.centre(site)
        total = (m[0] + m[1]) + (m[2] + m[3])
        uc, vc = d[U].centre(site), d[V].centre(site)
        pc = pressure.centre(site)
        pe, pw, pn, ps = pressure.around(site)
        push_x = 0.1 * (m[0] * (pe - pc) + m[1] * (pc - pw))
        push_y = 0.1 * (m[2] * (pn - pc) + m[3] * (pc - ps))
        f = 0.2 * self.coriolis(site) * w
        spread = {ch: 0.04 * self.laplacian(d[ch], site, m, total) for ch in (UB, VB)}
        after = {
            U: d[UB].centre(site) + (f * vc - push_x + spread[UB]),
            V: d[VB].centre(site) + (spread[VB] - f * uc - push_y),
        }
        if heat is None:
            return after
        qe, qw, qn, qs, qc = q
        for now, before in ((TEMP, TB), (SALT, SB)):
            e, w_, n, s = d[now].around(site)
            carried = (qw * w_ - qe * e) + (qs * s - qn * n) + qc * d[now].centre(site)
            change = 2.0 * carried + 0.04 * self.laplacian(d[before], site, m, total)
            if now == TEMP:
                change = change + 0.6 * heat
            after[now] = d[before].centre(site) + change
        return after

    def filtered(self, d, site, ch, after):
        now, before = d[ch].centre(site), d[ch + 4].centre(site)
        return now + 0.1 * (before - 2.0 * now + after) * self.wet.centre(site)

    def optics(self, c, site):
        absorb = 0.08 + 0.05 * (jnp.abs(c[2].centre(site)) + jnp.abs(c[3].centre(site)))
        return absorb, self.cumulate(absorb)

    def heating(self, absorb, depthsum, site):
        fade = jnp.exp(-depthsum)
        above = jnp.where(self.level == 0, 1.0, level_roll(fade, 1))
        return self.irr_at(site) * self.wet.centre(site) * (above - fade)

    def light(self, absorb, depthsum, site):
        return self.irr_at(site) * jnp.exp(0.5 * absorb - depthsum)

    def mixing(self, d, site):
        rho = self.density(d, site)
        below = level_roll(rho, -1)
        wet_below = jnp.where(self.levelf + 1.0 < self.depth_at(site), 1.0, 0.0)
        return (0.005 + 0.1 / (1.0 + 4.0 * jnp.maximum(below - rho, 0.0))) * wet_below

    def reactions(self, c, temp, lit, which):
        nn, na = jnp.abs(c[0]), jnp.abs(c[1])
        base = jnp.exp(0.06 * temp) * (lit / (lit + 0.5))
        total = nn + na
        small = 0.6 * base * c[2] / (0.2 + total)
        large = 0.9 * base * c[3] / (0.8 + total)
        graze = 0.8 * c[4] / (1.0 + (jnp.abs(c[2]) + jnp.abs(c[3])))
        gs, gl = graze * c[2], graze * c[3]
        up_s, up_l = small * total, large * total
        r = {2: up_s - gs - 0.1 * c[2], 3: up_l - gl - 0.1 * c[3]}
        if len(which) > 2:
            both = small + large
            remin = 0.3 * c[5] + 0.1 * c[6]
            nitrify = 0.2 * c[1]
            r[0] = nitrify - both * nn
            r[1] = remin + 0.1 * c[4] - nitrify - both * na
            r[4] = 0.7 * (gs + gl) - 0.25 * c[4]
            r[5] = 0.1 * c[2] + 0.3 * gs - 0.3 * c[5]
            r[6] = 0.1 * c[3] + 0.15 * c[4] + 0.3 * gl - 0.1 * c[6]
            r[7] = 1.3 * (up_s + up_l) - (remin + 2.0 * nitrify)
        return r

    def tracers(self, c, d, site, q, m, lit, which):
        w = self.wet.centre(site)
        qe, qw, qn, qs, qc = q
        total = (m[0] + m[1]) + (m[2] + m[3])
        ke, kw = 0.02 * m[0] - qe, 0.02 * m[1] + qw
        kn, ks = 0.02 * m[2] - qn, 0.02 * m[3] + qs
        kc = (1.0 - 0.02 * total) + qc
        kappa = self.mixing(d, site)
        centre = {i: c[i].centre(site) for i in (which if len(which) > 2 else range(5))}
        r = self.reactions(centre, d[TEMP].centre(site), lit, which)
        tenth = 0.1 * w
        for i in which:
            e, w_, n, s = c[i].around(site)
            here = centre[i]
            down = kappa * (level_roll(here, -1) - here)
            moved = (ke * e + kw * w_) + (kn * n + ks * s)
            yield i, kc * here + moved + (down - level_roll(down, 1)) + tenth * r[i]

    def first_core_site(self, d, c, pressure, site, store, plankton):
        m = self.faces(site)
        q = self.speeds(d[U], d[V], site, m)
        optic = self.optics(c, site)
        after = self.dynamics(d, pressure, site, self.heating(*optic, site), q, m)
        for ch, value in after.items():
            store(ch, site, value)
            store(ch + 4, site, self.filtered(d, site, ch, value))
        if plankton:
            for i, value in self.tracers(c, d, site, q, m, self.light(*optic, site), (2, 3)):
                store(GRAZED[i - 2], site, value)

    def second_core_site(self, d, c, pressure, site, store, heated):
        m = self.faces(site)
        q = self.speeds(d[U], d[V], site, m)
        optic = self.optics(c, site)
        if pressure is not None:
            heat = self.heating(*optic, site) if heated else None
            for ch, value in self.dynamics(d, pressure, site, heat, q, m).items():
                store(FLOW[ch], site, value)
        lit = self.light(*optic, site)
        for i, value in self.tracers(c, d, site, q, m, lit, range(FIELDS)):
            store(i, site, value)


def column_kernel(sh, xo, xp, rx, rp, fresh, wet_ref, press):
    md = Model(sh)
    cx = sh.cx

    def mask_row(kind, j):
        if HALO <= j < HALO + cx:
            return sh.row(xo, sh.mask_tile, kind * cx + j - HALO)
        if j < HALO:
            first, second, at = rx, rp, HALO - 1 - j
        else:
            first, second, at = rp, rx, cx - 1 - (j - HALO - cx)
        tile = 2 * sh.halo_tiles
        return jnp.where(
            md.core0, sh.row(first, tile, kind * cx + at), sh.row(second, tile, kind * cx + at)
        )

    md.irr_at = lambda site: mask_row(0, site)
    md.depth_at = lambda site: mask_row(1, site)
    for j in range(sh.cols):
        wet_ref[j] = md.wet_of(mask_row(1, j))
    md.wet = Field(sh, md.lane, lambda j: wet_ref[j])

    def raw(x, sides, comp, ch):
        def col(j):
            if HALO <= j < HALO + cx:
                return x[ch * cx + j - HALO]
            if j < HALO:
                return sides[1][sh.halo_at(comp, 1, ch, HALO - 1 - j)]
            return sides[0][sh.halo_at(comp, 0, ch, j - HALO - cx)]

        return Field(sh, md.lane, col)

    def store(index, site, value):
        fresh[md.fresh_at(index, site)] = value

    def fields(x, sides, comp):
        return [raw(x, sides, comp, ch) for ch in range(FIELDS)]

    def pressure_of(d):
        for j in range(sh.cols):
            press[j] = md.pressure(d, j)
        return Field(sh, md.lane, lambda j: press[j])

    @pl.when(md.core0)
    def _():
        d, c = fields(xo, (rp, rx), 0), fields(xp, (rp, rx), 1)
        pressure = pressure_of(d)
        for site in md.first_step:
            md.first_core_site(d, c, pressure, site, store, site in md.own)
        d = [
            Field(sh, md.lane, lambda j, ch=ch: fresh[md.fresh_at(ch, j)]) for ch in range(FIELDS)
        ]
        for site in md.first_step:
            store(PRESSURE, site, md.pressure(d, site))

    @pl.when(jnp.logical_not(md.core0))
    def _():
        d, c = fields(xp, (rx, rp), 0), fields(xo, (rx, rp), 1)
        pressure = pressure_of(d)
        for site in md.first_step:
            md.second_core_site(d, c, pressure, site, store, site in md.own)


def step_kernel(sh, xo, wet_ref, fresh, edges, y, yp, out_ref, strips, cols, rims, seams):
    md = Model(sh)
    cx, lane, in_group = sh.cx, md.lane, md.in_group
    end = sh.rows - 1
    even_y = md.gy % 2 == 0
    slot = lane % (2 * HALO)
    zero = jnp.zeros((sh.lev, sh.rows), jnp.float32)

    def build_strips(base, tiles, channels):
        for t in tiles:
            a, b = jnp.where(md.core0, y[t], yp[t]), jnp.where(md.core0, yp[t], y[t])
            mine = edges[t]
            left = jnp.where(md.gy > 0, jnp.where(even_y, b, a), zero)
            right = jnp.where(md.gy < md.ny - 1, jnp.where(even_y, a, b), zero)
            low = jnp.where(slot < HALO, left, mine)
            high = jnp.where(slot < HALO, mine, right)
            for q in range(channels):
                at = q * 2 * HALO
                strips[base + (t - tiles[0]) * sh.per_tile + q] = jnp.where(
                    in_group < sh.half, lane_roll(low, -at), lane_roll(high, sh.half - at)
                )

    build_strips(0, range(2 * sh.field_tiles), sh.per_tile)
    build_strips(2 * FIELDS, [sh.edge_tiles - 1], 2)

    def mask_at(kind, site):
        if site == STRIP:
            return strips[2 * FIELDS + kind]
        return sh.row(xo, sh.mask_tile, kind * cx + site - HALO)

    md.irr_at = lambda site: mask_at(0, site)
    md.depth_at = lambda site: mask_at(1, site)

    def beside(strip, low, high):
        at = sh.half + high
        return jnp.where(in_group > at, lane_roll(strip, at + 1 - low), strip)

    def to_ends(pair, site, high):
        return lane_roll(pair, end - (site * sh.group + sh.half + high))

    def seam_of(ref, index):
        return lambda site: to_ends(ref[index], site, HALO)

    wet_strip = md.wet_of(strips[2 * FIELDS + 1])
    wet_pair = beside(wet_strip, HALO - 1, HALO)
    md.wet = Field(
        sh, lane, lambda j: wet_ref[j], lambda: wet_strip, lambda site: to_ends(wet_pair, site, HALO)
    )

    def strip_field(index):
        return Field(sh, lane, strip=lambda: strips[index])

    def rim(index, site, value):
        rims[index] = value

    def renewed(index, sites):
        value = rims[index]
        seams[index] = beside(value, HALO - 1, HALO)
        ends = beside(value, HALO, HALO - 1)
        for site in sites:
            cols[md.fresh_at(index, site)] = jnp.where(
                (lane == 0) | (lane == end),
                to_ends(ends, site, HALO - 1),
                fresh[md.fresh_at(index, site)],
            )
        return stored(index)

    def stored(index):
        return Field(
            sh,
            lane,
            lambda j: cols[md.fresh_at(index, j)],
            lambda: rims[index],
            seam_of(seams, index),
            lambda j: fresh[md.fresh_at(index, j)],
        )

    def write(ch, k_values):
        for i in range(cx):
            out_ref[pl.ds(ch * sh.lev * cx + i, sh.lev, stride=cx), :] = jnp.where(
                md.odd_x, k_values[cx - 1 - i], k_values[i]
            )

    d = [strip_field(ch) for ch in range(FIELDS)]
    c = [strip_field(FIELDS + ch) for ch in range(FIELDS)]
    strip_pressure = md.pressure(d, STRIP)
    pressure = Field(sh, lane, strip=lambda: strip_pressure)
    done = {}

    def keep(ch, site, value):
        done[ch, site] = value

    @pl.when(md.core0)
    def _():
        md.first_core_site(d, c, pressure, STRIP, rim, True)
        d1 = [renewed(ch, md.own if ch == V else md.first_step) for ch in range(FIELDS)]
        c1 = {i: renewed(GRAZED[i - 2], md.own) for i in (2, 3)}
        rim(PRESSURE, STRIP, md.pressure(d1, STRIP))
        pressure1 = renewed(PRESSURE, md.first_step)
        for site in md.own:
            md.first_core_site(d1, c1, pressure1, site, keep, False)
        for ch in range(FIELDS):
            values = [done[ch, site] for site in md.own]
            write(ch, [v * md.mirror for v in values] if ch in VEL_X else values)

    @pl.when(jnp.logical_not(md.core0))
    def _():
        md.second_core_site(d, c, pressure, STRIP, rim, True)
        c1 = [renewed(ch, md.first_step) for ch in range(FIELDS)]
        d1 = [renewed(FLOW[ch], md.first_step if ch == U else md.own) for ch in range(4)]
        for site in md.own:
            md.second_core_site(d1, c1, None, site, keep, False)
        for ch in range(FIELDS):
            write(ch, [done[ch, site] for site in md.own])


def tiles(sh, n):
    return jax.ShapeDtypeStruct((n, sh.lev, sh.rows), jnp.float32)


def call(kernel, sh, outs, args, flops, scratch=(), source=pltpu.VMEM):
    spec = pl.BlockSpec(memory_space=pltpu.VMEM)
    size = sum(a.size for a in args) + sum(o.size for o in outs)
    return pl.pallas_call(
        lambda *refs: kernel(sh, *refs),
        out_shape=outs,
        in_specs=[pl.BlockSpec(memory_space=source)] * len(args),
        out_specs=[spec] * len(outs),
        scratch_shapes=list(scratch),
        compiler_params=pltpu.CompilerParams(vmem_limit_bytes=16 << 20),
        cost_estimate=pl.CostEstimate(flops=flops, bytes_accessed=4 * size, transcendentals=0),
    )(*args)


def local(ocean_state, irradiance, land_mask, bottom_level):
    fields, lev, cx, rows = ocean_state.shape
    assert fields == FIELDS
    sh = Shape(lev, cx, rows)
    nx, ny = lax.axis_size("gx"), lax.axis_size("gy")
    assert nx % 2 == 0 and ny % 2 == 0
    axes = ("comp", "gy", "gx")

    def send(value, target):
        pairs = []
        for c in range(2):
            for y in range(ny):
                for x in range(nx):
                    tc, ty, tx = target(c, y, x)
                    pairs.append(((c * ny + y) * nx + x, (tc * ny + ty) * nx + tx))
        return lax.ppermute(value, axes, pairs)

    def odd_pair(i, n):
        return (i + 1) % n if i % 2 else (i - 1) % n

    def pair(i, n, core):
        return i ^ 1 if core == 0 else odd_pair(i, n)

    def edges_x(v):
        return send(v, lambda c, y, x: (c, y, pair(x, nx, c)))

    def bulk_x(v):
        return send(v, lambda c, y, x: (c, y, pair(x, nx, 1 - c)))

    def along_y(v):
        return send(v, lambda c, y, x: (c, pair(y, ny, c), x))

    def swap(v):
        return send(v, lambda c, y, x: (1 - c, y, x))

    flat = ocean_state.reshape(fields * lev * cx, rows)
    partner = swap(flat)
    inputs = (flat, irradiance, land_mask, bottom_level)
    xo, eo = call(
        load_kernel,
        sh,
        [tiles(sh, fields * cx + 1), tiles(sh, sh.field_tiles + 1)],
        tuple(pltpu.with_memory_space_constraint(a, pltpu.HBM) for a in inputs),
        100_000,
        scratch=[pltpu.VMEM(a.shape, a.dtype) for a in inputs] + [pltpu.SemaphoreType.DMA((4,))],
        source=pltpu.HBM,
    )
    edge, message = tiles(sh, sh.edge_tiles), tiles(sh, 2 * sh.halo_tiles + 1)
    xp, e0, m = call(
        send_kernel, sh, [tiles(sh, fields * cx), edge, message], (partner, xo, eo), 100_000
    )
    ex = edges_x(e0)
    rx = bulk_x(m)
    ep = swap(ex)
    (e1,) = call(merge_kernel, sh, [edge], (e0, ex, ep), 10_000)
    y = along_y(e1)
    rp = swap(rx)
    yp = swap(y)
    n_sites = sh.cols - 2
    fresh, wet = call(
        column_kernel,
        sh,
        [tiles(sh, FRESH * n_sites), tiles(sh, sh.cols)],
        (xo, xp, rx, rp),
        1_000_000,
        scratch=[pltpu.VMEM((sh.cols, lev, rows), jnp.float32)],
    )
    (out,) = call(
        step_kernel,
        sh,
        [jax.ShapeDtypeStruct(flat.shape, jnp.float32)],
        (xo, wet, fresh, e1, y, yp),
        1_000_000,
        scratch=[
            pltpu.VMEM((2 * FIELDS + 2, lev, rows), jnp.float32),
            pltpu.VMEM((FRESH * n_sites, lev, rows), jnp.float32),
            pltpu.VMEM((FRESH, lev, rows), jnp.float32),
            pltpu.VMEM((FRESH, lev, rows), jnp.float32),
        ],
    )
    return out.reshape(ocean_state.shape)


def solution(mesh):
    return jax.shard_map(
        local,
        mesh=mesh,
        in_specs=(P("comp", None, "gx", "gy"), P("gx", "gy"), P("gx", "gy"), P("gx", "gy")),
        out_specs=P("comp", None, "gx", "gy"),
        check_vma=False,
    )
```

```python
import jax
import jax.numpy as jnp
from jax import lax
from jax.experimental import pallas as pl
from jax.experimental.pallas import tpu as pltpu
from jax.sharding import PartitionSpec as P


HALO = 2
FIELDS = 8
U, V, TEMP, SALT, UB, VB, TB, SB = range(FIELDS)
VEL_X = (U, UB)


def lane_roll(x, shift):
    shift %= x.shape[1]
    return pltpu.roll(x, shift, 1) if shift else x


def level_roll(x, shift):
    shift %= x.shape[0]
    return pltpu.roll(x, shift, 0) if shift else x


class Shape:
    def __init__(self, lev, cx, rows):
        self.lev, self.cx, self.rows = lev, cx, rows
        self.cols = cx + 2 * HALO
        self.group = rows // self.cols
        self.per_tile = self.group // (2 * HALO)
        self.half = self.group // 2
        self.field_tiles = -(-FIELDS // self.per_tile)
        self.edge_tiles = 2 * self.field_tiles + 1
        assert self.per_tile >= 2 and self.group >= 4 * HALO and 2 * cx <= lev
        assert self.cols * self.group == rows
        self.mask_tile = FIELDS * cx
        self.halo_tiles = FIELDS * HALO

    def lanes(self):
        return lax.broadcasted_iota(jnp.int32, (self.lev, self.rows), 1)

    def levels(self):
        return lax.broadcasted_iota(jnp.int32, (self.lev, self.rows), 0)

    def row(self, ref, tile, r):
        return jnp.broadcast_to(ref[tile, r : r + 1, :], (self.lev, self.rows))

    def edge_at(self, comp, ch):
        t, q = divmod(ch, self.per_tile)
        return comp * self.field_tiles + t, q

    def halo_at(self, comp, side, ch, d):
        return (self.halo_tiles if comp == side else 0) + ch * HALO + d

    def edge_place(self, acc, value, j, channel, lane):
        at = j * self.group + channel * 2 * HALO + HALO
        return jnp.where((lane >= at - HALO) & (lane < at + HALO), lane_roll(value, at), acc)


def load_kernel(sh, *refs):
    sources, x_ref, e_ref, arrived, sem = refs[:4], refs[4], refs[5], refs[6:10], refs[10]
    copies = [
        pltpu.make_async_copy(a, b, sem.at[i]) for i, (a, b) in enumerate(zip(sources, arrived))
    ]
    for copy in copies:
        copy.start()
    for copy in copies:
        copy.wait()
    state_ref, irr_ref, land_ref, bottom_ref = arrived
    odd = is_odd("gx")
    edges = own_columns(sh, state_ref, x_ref, odd, first_core())
    cx = sh.cx
    lane = sh.lanes()
    depth = jnp.where(land_ref[...] == 1, bottom_ref[...], 0).astype(jnp.float32)
    last = jnp.zeros((sh.lev, sh.rows), jnp.float32)
    for q, value in enumerate((irr_ref[...], depth)):
        for k in range(cx):
            row = jnp.where(odd, value[cx - 1 - k : cx - k, :], value[k : k + 1, :])
            x_ref[sh.mask_tile, q * cx + k : q * cx + k + 1, :] = row
            wide = jnp.broadcast_to(row, (sh.lev, sh.rows))
            last = sh.edge_place(last, wide, k + HALO, q, lane)
    for t, edge in enumerate(edges + [last]):
        e_ref[t] = edge


def is_odd(axis):
    return lax.axis_index(axis) % 2 == 1


def first_core():
    return lax.axis_index("comp") == 0


def own_columns(sh, state_ref, x_ref, odd, dynamics):
    flip = jnp.where(odd & dynamics, -1.0, 1.0)
    cx = sh.cx
    lane = sh.lanes()
    edges = [jnp.zeros((sh.lev, sh.rows), jnp.float32)] * sh.field_tiles
    for ch in range(FIELDS):
        raw = [state_ref[pl.ds(ch * sh.lev * cx + i, sh.lev, stride=cx), :] for i in range(cx)]
        t, q = sh.edge_at(0, ch)
        for k in range(cx):
            value = jnp.where(odd, raw[cx - 1 - k], raw[k])
            if ch in VEL_X:
                value = value * flip
            x_ref[ch * cx + k] = value
            edges[t] = sh.edge_place(edges[t], value, k + HALO, q, lane)
    return edges


def send_kernel(sh, state_ref, xo_ref, eo_ref, xp_ref, e_ref, m_ref):
    core0 = first_core()
    edges = own_columns(sh, state_ref, xp_ref, is_odd("gx"), jnp.logical_not(core0))
    cx = sh.cx
    for t in range(sh.field_tiles):
        own = eo_ref[t]
        e_ref[t] = jnp.where(core0, own, edges[t])
        e_ref[sh.field_tiles + t] = jnp.where(core0, edges[t], own)
    e_ref[sh.edge_tiles - 1] = eo_ref[sh.field_tiles]
    for part, (x_ref, flip) in enumerate(
        ((xo_ref, jnp.where(core0, -1.0, 1.0)), (xp_ref, jnp.where(core0, 1.0, -1.0)))
    ):
        for ch in range(FIELDS):
            for d in range(HALO):
                value = jnp.where(core0, x_ref[ch * cx + d], x_ref[ch * cx + cx - 1 - d])
                m_ref[part * sh.halo_tiles + ch * HALO + d] = value * flip if ch in VEL_X else value
    m_ref[2 * sh.halo_tiles] = xo_ref[sh.mask_tile]


def merge_kernel(sh, e_ref, a_ref, b_ref, eo_ref):
    lane = sh.lanes()
    core0 = first_core()
    column, place = lane // sh.group, lane % sh.group // (2 * HALO)
    for t in range(sh.edge_tiles):
        got = a_ref[t], b_ref[t]
        after, before = jnp.where(core0, got[0], got[1]), jnp.where(core0, got[1], got[0])
        for ch in VEL_X:
            if sh.edge_at(0, ch)[0] == t:
                flip = jnp.where(place == sh.edge_at(0, ch)[1], -1.0, 1.0)
                after, before = after * flip, before * flip
        edge = e_ref[t]
        for d in range(HALO):
            shift = (2 * d + 1) * sh.group
            edge = jnp.where(column == sh.cx + HALO + d, lane_roll(after, shift), edge)
            edge = jnp.where(column == HALO - 1 - d, lane_roll(before, -shift), edge)
        eo_ref[t] = edge


STRIP = "strip"


class Field:
    def __init__(self, sh, lane, col=None, strip=None, seam=None, rough=None):
        self.sh, self.lane, self.col, self.strip = sh, lane, col, strip
        self.seam, self.rough = seam, rough

    def centre(self, site):
        return self.strip() if site == STRIP else self.col(site)

    def east(self, site):
        return lane_roll(self.strip(), -self.sh.group) if site == STRIP else self.col(site + 1)

    def west(self, site):
        return lane_roll(self.strip(), self.sh.group) if site == STRIP else self.col(site - 1)

    def along_rows(self, site):
        inner = site == STRIP or self.rough is None
        value = self.centre(site) if inner else self.rough(site)
        north, south = lane_roll(value, -1), lane_roll(value, 1)
        if site == STRIP or self.seam is None:
            return north, south
        beyond = self.seam(site)
        more = 0 if inner else 1
        last = self.lane >= self.sh.rows - 1 - more
        return jnp.where(last, beyond, north), jnp.where(self.lane <= more, beyond, south)

    def around(self, site):
        return (self.east(site), self.west(site)) + self.along_rows(site)


GRAZED = (FIELDS, FIELDS + 1)
FLOW = tuple(FIELDS + ch for ch in (U, V, TEMP, SALT))
PRESSURE = FIELDS + 2
FRESH = FIELDS + 4


class Model:
    def __init__(self, sh):
        self.sh = sh
        self.lane, self.level = sh.lanes(), sh.levels()
        self.levelf = self.level.astype(jnp.float32)
        self.in_group = self.lane % sh.group
        self.core0 = first_core()
        self.odd_x = is_odd("gx")
        self.mirror = jnp.where(self.odd_x, -1.0, 1.0)
        self.gy, self.ny = lax.axis_index("gy"), lax.axis_size("gy")
        self.first_step = list(range(1, sh.cols - 1))
        self.own = list(range(HALO, HALO + sh.cx))
        self.n_sites = len(self.first_step)

    def fresh_at(self, index, site):
        return index * self.n_sites + site - 1

    def cumulate(self, x):
        reach = 1
        while reach < self.sh.lev:
            x = x + jnp.where(self.level >= reach, level_roll(x, reach), 0.0)
            reach *= 2
        return x

    def wet_of(self, depth):
        return jnp.where(self.levelf < depth, 1.0, 0.0)

    def faces(self, site):
        w = self.wet.centre(site)
        return [w * value for value in self.wet.around(site)]

    def density(self, d, site):
        rho = 0.8 * d[SALT].centre(site) - 0.2 * d[TEMP].centre(site)
        return rho * self.wet.centre(site)

    def pressure(self, d, site):
        return 0.1 * self.cumulate(self.density(d, site))

    def speeds(self, u, v, site, m):
        uc, vc = u.centre(site), v.centre(site)
        north, south = v.along_rows(site)
        qe = 0.025 * (uc + u.east(site)) * m[0]
        qw = 0.025 * (uc + u.west(site)) * m[1]
        qn = 0.025 * (vc + north) * m[2]
        qs = 0.025 * (vc + south) * m[3]
        return qe, qw, qn, qs, (qw - qe) + (qs - qn)

    def laplacian(self, f, site, m, total):
        e, w, n, s = f.around(site)
        return (m[0] * e + m[1] * w) + (m[2] * n + m[3] * s) - total * f.centre(site)

    def coriolis(self, site):
        sh, at = self.sh, self.in_group
        row = self.lane
        if site == STRIP:
            row = jnp.where(at < sh.half, at - HALO, sh.rows - HALO + at - sh.half)
        row = (row + self.gy * sh.rows).astype(jnp.float32)
        return self.mirror * (0.3 + 0.4 * row / (self.ny * sh.rows))

    def dynamics(self, d, pressure, site, heat, q, m):
        w = self.wet.centre(site)
        total = (m[0] + m[1]) + (m[2] + m[3])
        uc, vc = d[U].centre(site), d[V].centre(site)
        pc = pressure.centre(site)
        pe, pw, pn, ps = pressure.around(site)
        push_x = 0.1 * (m[0] * (pe - pc) + m[1] * (pc - pw))
        push_y = 0.1 * (m[2] * (pn - pc) + m[3] * (pc - ps))
        f = 0.2 * self.coriolis(site) * w
        spread = {ch: 0.04 * self.laplacian(d[ch], site, m, total) for ch in (UB, VB)}
        after = {
            U: d[UB].centre(site) + (f * vc - push_x + spread[UB]),
            V: d[VB].centre(site) + (spread[VB] - f * uc - push_y),
        }
        if heat is None:
            return after
        qe, qw, qn, qs, qc = q
        for now, before in ((TEMP, TB), (SALT, SB)):
            e, w_, n, s = d[now].around(site)
            carried = (qw * w_ - qe * e) + (qs * s - qn * n) + qc * d[now].centre(site)
            change = 2.0 * carried + 0.04 * self.laplacian(d[before], site, m, total)
            if now == TEMP:
                change = change + 0.6 * heat
            after[now] = d[before].centre(site) + change
        return after

    def filtered(self, d, site, ch, after):
        now, before = d[ch].centre(site), d[ch + 4].centre(site)
        return now + 0.1 * (before - 2.0 * now + after) * self.wet.centre(site)

    def optics(self, c, site):
        absorb = 0.08 + 0.05 * (jnp.abs(c[2].centre(site)) + jnp.abs(c[3].centre(site)))
        return absorb, self.cumulate(absorb)

    def heating(self, absorb, depthsum, site):
        fade = jnp.exp(-depthsum)
        above = jnp.where(self.level == 0, 1.0, level_roll(fade, 1))
        return self.irr_at(site) * self.wet.centre(site) * (above - fade)

    def light(self, absorb, depthsum, site):
        return self.irr_at(site) * jnp.exp(0.5 * absorb - depthsum)

    def mixing(self, d, site):
        rho = self.density(d, site)
        below = level_roll(rho, -1)
        wet_below = jnp.where(self.levelf + 1.0 < self.depth_at(site), 1.0, 0.0)
        return (0.005 + 0.1 / (1.0 + 4.0 * jnp.maximum(below - rho, 0.0))) * wet_below

    def reactions(self, c, temp, lit, which):
        nn, na = jnp.abs(c[0]), jnp.abs(c[1])
        base = jnp.exp(0.06 * temp) * (lit / (lit + 0.5))
        total = nn + na
        small = 0.6 * base * c[2] / (0.2 + total)
        large = 0.9 * base * c[3] / (0.8 + total)
        graze = 0.8 * c[4] / (1.0 + (jnp.abs(c[2]) + jnp.abs(c[3])))
        gs, gl = graze * c[2], graze * c[3]
        up_s, up_l = small * total, large * total
        r = {2: up_s - gs - 0.1 * c[2], 3: up_l - gl - 0.1 * c[3]}
        if len(which) > 2:
            both = small + large
            remin = 0.3 * c[5] + 0.1 * c[6]
            nitrify = 0.2 * c[1]
            r[0] = nitrify - both * nn
            r[1] = remin + 0.1 * c[4] - nitrify - both * na
            r[4] = 0.7 * (gs + gl) - 0.25 * c[4]
            r[5] = 0.1 * c[2] + 0.3 * gs - 0.3 * c[5]
            r[6] = 0.1 * c[3] + 0.15 * c[4] + 0.3 * gl - 0.1 * c[6]
            r[7] = 1.3 * (up_s + up_l) - (remin + 2.0 * nitrify)
        return r

    def tracers(self, c, d, site, q, m, lit, which):
        w = self.wet.centre(site)
        qe, qw, qn, qs, qc = q
        total = (m[0] + m[1]) + (m[2] + m[3])
        ke, kw = 0.02 * m[0] - qe, 0.02 * m[1] + qw
        kn, ks = 0.02 * m[2] - qn, 0.02 * m[3] + qs
        kc = (1.0 - 0.02 * total) + qc
        kappa = self.mixing(d, site)
        centre = {i: c[i].centre(site) for i in (which if len(which) > 2 else range(5))}
        r = self.reactions(centre, d[TEMP].centre(site), lit, which)
        tenth = 0.1 * w
        for i in which:
            e, w_, n, s = c[i].around(site)
            here = centre[i]
            down = kappa * (level_roll(here, -1) - here)
            moved = (ke * e + kw * w_) + (kn * n + ks * s)
            yield i, kc * here + moved + (down - level_roll(down, 1)) + tenth * r[i]

    def first_core_site(self, d, c, pressure, site, store, plankton):
        m = self.faces(site)
        q = self.speeds(d[U], d[V], site, m)
        optic = self.optics(c, site)
        after = self.dynamics(d, pressure, site, self.heating(*optic, site), q, m)
        for ch, value in after.items():
            store(ch, site, value)
            store(ch + 4, site, self.filtered(d, site, ch, value))
        if plankton:
            for i, value in self.tracers(c, d, site, q, m, self.light(*optic, site), (2, 3)):
                store(GRAZED[i - 2], site, value)

    def second_core_site(self, d, c, pressure, site, store, heated):
        m = self.faces(site)
        q = self.speeds(d[U], d[V], site, m)
        optic = self.optics(c, site)
        if pressure is not None:
            heat = self.heating(*optic, site) if heated else None
            for ch, value in self.dynamics(d, pressure, site, heat, q, m).items():
                store(FLOW[ch], site, value)
        lit = self.light(*optic, site)
        for i, value in self.tracers(c, d, site, q, m, lit, range(FIELDS)):
            store(i, site, value)


def column_kernel(sh, xo, xp, rx, rp, fresh, wet_ref, press):
    md = Model(sh)
    cx = sh.cx

    def mask_row(kind, j):
        if HALO <= j < HALO + cx:
            return sh.row(xo, sh.mask_tile, kind * cx + j - HALO)
        if j < HALO:
            first, second, at = rx, rp, HALO - 1 - j
        else:
            first, second, at = rp, rx, cx - 1 - (j - HALO - cx)
        tile = 2 * sh.halo_tiles
        return jnp.where(
            md.core0, sh.row(first, tile, kind * cx + at), sh.row(second, tile, kind * cx + at)
        )

    md.irr_at = lambda site: mask_row(0, site)
    md.depth_at = lambda site: mask_row(1, site)
    for j in range(sh.cols):
        wet_ref[j] = md.wet_of(mask_row(1, j))
    md.wet = Field(sh, md.lane, lambda j: wet_ref[j])

    def raw(x, sides, comp, ch):
        def col(j):
            if HALO <= j < HALO + cx:
                return x[ch * cx + j - HALO]
            if j < HALO:
                return sides[1][sh.halo_at(comp, 1, ch, HALO - 1 - j)]
            return sides[0][sh.halo_at(comp, 0, ch, j - HALO - cx)]

        return Field(sh, md.lane, col)

    def store(index, site, value):
        fresh[md.fresh_at(index, site)] = value

    def fields(x, sides, comp):
        return [raw(x, sides, comp, ch) for ch in range(FIELDS)]

    def pressure_of(d):
        for j in range(sh.cols):
            press[j] = md.pressure(d, j)
        return Field(sh, md.lane, lambda j: press[j])

    @pl.when(md.core0)
    def _():
        d, c = fields(xo, (rp, rx), 0), fields(xp, (rp, rx), 1)
        pressure = pressure_of(d)
        for site in md.first_step:
            md.first_core_site(d, c, pressure, site, store, site in md.own)
        d = [
            Field(sh, md.lane, lambda j, ch=ch: fresh[md.fresh_at(ch, j)]) for ch in range(FIELDS)
        ]
        for site in md.first_step:
            store(PRESSURE, site, md.pressure(d, site))

    @pl.when(jnp.logical_not(md.core0))
    def _():
        d, c = fields(xp, (rx, rp), 0), fields(xo, (rx, rp), 1)
        pressure = pressure_of(d)
        for site in md.first_step:
            md.second_core_site(d, c, pressure, site, store, site in md.own)


def step_kernel(sh, xo, wet_ref, fresh, edges, y, yp, out_ref, strips, cols, rims, seams):
    md = Model(sh)
    cx, lane, in_group = sh.cx, md.lane, md.in_group
    end = sh.rows - 1
    even_y = md.gy % 2 == 0
    slot = lane % (2 * HALO)
    zero = jnp.zeros((sh.lev, sh.rows), jnp.float32)

    def build_strips():
        strips_of(2 * FIELDS, [sh.edge_tiles - 1], 2)
        strips_of(0, range(2 * sh.field_tiles), sh.per_tile)

    def strips_of(base, tiles, channels):
        for t in tiles:
            a, b = jnp.where(md.core0, y[t], yp[t]), jnp.where(md.core0, yp[t], y[t])
            mine = edges[t]
            left = jnp.where(md.gy > 0, jnp.where(even_y, b, a), zero)
            right = jnp.where(md.gy < md.ny - 1, jnp.where(even_y, a, b), zero)
            low = jnp.where(slot < HALO, left, mine)
            high = jnp.where(slot < HALO, mine, right)
            for q in range(channels):
                at = q * 2 * HALO
                strips[base + (t - tiles[0]) * sh.per_tile + q] = jnp.where(
                    in_group < sh.half, lane_roll(low, -at), lane_roll(high, sh.half - at)
                )

    def mask_at(kind, site):
        if site == STRIP:
            return strips[2 * FIELDS + kind]
        return sh.row(xo, sh.mask_tile, kind * cx + site - HALO)

    md.irr_at = lambda site: mask_at(0, site)
    md.depth_at = lambda site: mask_at(1, site)

    def beside(strip, low, high):
        at = sh.half + high
        return jnp.where(in_group > at, lane_roll(strip, at + 1 - low), strip)

    def to_ends(pair, site, high):
        return lane_roll(pair, end - (site * sh.group + sh.half + high))

    def seam_of(ref, index):
        return lambda site: to_ends(ref[index], site, HALO)

    def prepare():
        build_strips()
        wet_strip = md.wet_of(strips[2 * FIELDS + 1])
        wet_pair = beside(wet_strip, HALO - 1, HALO)
        md.wet = Field(
            sh,
            lane,
            lambda j: wet_ref[j],
            lambda: wet_strip,
            lambda site: to_ends(wet_pair, site, HALO),
        )
        d = [strip_field(ch) for ch in range(FIELDS)]
        c = [strip_field(FIELDS + ch) for ch in range(FIELDS)]
        pressure = md.pressure(d, STRIP)
        return d, c, Field(sh, lane, strip=lambda: pressure)

    def strip_field(index):
        return Field(sh, lane, strip=lambda: strips[index])

    def rim(index, site, value):
        rims[index] = value

    def renewed(index, sites):
        value = rims[index]
        seams[index] = beside(value, HALO - 1, HALO)
        ends = beside(value, HALO, HALO - 1)
        for site in sites:
            cols[md.fresh_at(index, site)] = jnp.where(
                (lane == 0) | (lane == end),
                to_ends(ends, site, HALO - 1),
                fresh[md.fresh_at(index, site)],
            )
        return stored(index)

    def stored(index):
        return Field(
            sh,
            lane,
            lambda j: cols[md.fresh_at(index, j)],
            lambda: rims[index],
            seam_of(seams, index),
            lambda j: fresh[md.fresh_at(index, j)],
        )

    def write(ch, k_values):
        for i in range(cx):
            out_ref[pl.ds(ch * sh.lev * cx + i, sh.lev, stride=cx), :] = jnp.where(
                md.odd_x, k_values[cx - 1 - i], k_values[i]
            )

    done = {}

    def keep(ch, site, value):
        done[ch, site] = value

    @pl.when(md.core0)
    def _():
        d, c, pressure = prepare()
        md.first_core_site(d, c, pressure, STRIP, rim, True)
        d1 = [renewed(ch, md.own if ch == V else md.first_step) for ch in range(FIELDS)]
        c1 = {i: renewed(GRAZED[i - 2], md.own) for i in (2, 3)}
        rim(PRESSURE, STRIP, md.pressure(d1, STRIP))
        pressure1 = renewed(PRESSURE, md.first_step)
        for site in md.own:
            md.first_core_site(d1, c1, pressure1, site, keep, False)
        for ch in range(FIELDS):
            values = [done[ch, site] for site in md.own]
            write(ch, [v * md.mirror for v in values] if ch in VEL_X else values)

    @pl.when(jnp.logical_not(md.core0))
    def _():
        d, c, pressure = prepare()
        md.second_core_site(d, c, pressure, STRIP, rim, True)
        c1 = [renewed(ch, md.first_step) for ch in range(FIELDS)]
        d1 = [renewed(FLOW[ch], md.first_step if ch == U else md.own) for ch in range(4)]
        for site in md.own:
            md.second_core_site(d1, c1, None, site, keep, False)
        for ch in range(FIELDS):
            write(ch, [done[ch, site] for site in md.own])


def tiles(sh, n):
    return jax.ShapeDtypeStruct((n, sh.lev, sh.rows), jnp.float32)


def call(kernel, sh, outs, args, flops, scratch=(), source=pltpu.VMEM):
    spec = pl.BlockSpec(memory_space=pltpu.VMEM)
    size = sum(a.size for a in args) + sum(o.size for o in outs)
    return pl.pallas_call(
        lambda *refs: kernel(sh, *refs),
        out_shape=outs,
        in_specs=[pl.BlockSpec(memory_space=source)] * len(args),
        out_specs=[spec] * len(outs),
        scratch_shapes=list(scratch),
        compiler_params=pltpu.CompilerParams(vmem_limit_bytes=16 << 20),
        cost_estimate=pl.CostEstimate(flops=flops, bytes_accessed=4 * size, transcendentals=0),
    )(*args)


def local(ocean_state, irradiance, land_mask, bottom_level):
    fields, lev, cx, rows = ocean_state.shape
    assert fields == FIELDS
    sh = Shape(lev, cx, rows)
    nx, ny = lax.axis_size("gx"), lax.axis_size("gy")
    assert nx % 2 == 0 and ny % 2 == 0
    axes = ("comp", "gy", "gx")

    def send(value, target):
        pairs = []
        for c in range(2):
            for y in range(ny):
                for x in range(nx):
                    tc, ty, tx = target(c, y, x)
                    pairs.append(((c * ny + y) * nx + x, (tc * ny + ty) * nx + tx))
        return lax.ppermute(value, axes, pairs)

    def odd_pair(i, n):
        return (i + 1) % n if i % 2 else (i - 1) % n

    def pair(i, n, core):
        return i ^ 1 if core == 0 else odd_pair(i, n)

    def edges_x(v):
        return send(v, lambda c, y, x: (c, y, pair(x, nx, c)))

    def bulk_x(v):
        return send(v, lambda c, y, x: (c, y, pair(x, nx, 1 - c)))

    def along_y(v):
        return send(v, lambda c, y, x: (c, pair(y, ny, c), x))

    def swap(v):
        return send(v, lambda c, y, x: (1 - c, y, x))

    flat = ocean_state.reshape(fields * lev * cx, rows)
    partner = swap(flat)
    inputs = (flat, irradiance, land_mask, bottom_level)
    xo, eo = call(
        load_kernel,
        sh,
        [tiles(sh, fields * cx + 1), tiles(sh, sh.field_tiles + 1)],
        tuple(pltpu.with_memory_space_constraint(a, pltpu.HBM) for a in inputs),
        100_000,
        scratch=[pltpu.VMEM(a.shape, a.dtype) for a in inputs] + [pltpu.SemaphoreType.DMA((4,))],
        source=pltpu.HBM,
    )
    edge, message = tiles(sh, sh.edge_tiles), tiles(sh, 2 * sh.halo_tiles + 1)
    xp, e0, m = call(
        send_kernel, sh, [tiles(sh, fields * cx), edge, message], (partner, xo, eo), 100_000
    )
    ex = edges_x(e0)
    rx = bulk_x(m)
    ep = swap(ex)
    (e1,) = call(merge_kernel, sh, [edge], (e0, ex, ep), 10_000)
    y = along_y(e1)
    rp = swap(rx)
    yp = swap(y)
    n_sites = sh.cols - 2
    fresh, wet = call(
        column_kernel,
        sh,
        [tiles(sh, FRESH * n_sites), tiles(sh, sh.cols)],
        (xo, xp, rx, rp),
        1_000_000,
        scratch=[pltpu.VMEM((sh.cols, lev, rows), jnp.float32)],
    )
    (out,) = call(
        step_kernel,
        sh,
        [jax.ShapeDtypeStruct(flat.shape, jnp.float32)],
        (xo, wet, fresh, e1, y, yp),
        1_000_000,
        scratch=[
            pltpu.VMEM((2 * FIELDS + 2, lev, rows), jnp.float32),
            pltpu.VMEM((FRESH * n_sites, lev, rows), jnp.float32),
            pltpu.VMEM((FRESH, lev, rows), jnp.float32),
            pltpu.VMEM((FRESH, lev, rows), jnp.float32),
        ],
    )
    return out.reshape(ocean_state.shape)


def solution(mesh):
    return jax.shard_map(
        local,
        mesh=mesh,
        in_specs=(P("comp", None, "gx", "gy"), P("gx", "gy"), P("gx", "gy"), P("gx", "gy")),
        out_specs=P("comp", None, "gx", "gy"),
        check_vma=False,
    )
```

```python
import jax
import jax.numpy as jnp
from jax import lax
from jax.experimental import pallas as pl
from jax.experimental.pallas import tpu as pltpu
from jax.sharding import PartitionSpec as P


HALO = 2
FIELDS = 8
U, V, TEMP, SALT, UB, VB, TB, SB = range(FIELDS)
VEL_X = (U, UB)


def lane_roll(x, shift):
    shift %= x.shape[1]
    return pltpu.roll(x, shift, 1) if shift else x


def level_roll(x, shift):
    shift %= x.shape[0]
    return pltpu.roll(x, shift, 0) if shift else x


class Shape:
    def __init__(self, lev, cx, rows):
        self.lev, self.cx, self.rows = lev, cx, rows
        self.cols = cx + 2 * HALO
        self.group = rows // self.cols
        self.per_tile = self.group // (2 * HALO)
        self.half = self.group // 2
        self.field_tiles = -(-FIELDS // self.per_tile)
        self.edge_tiles = 2 * self.field_tiles + 1
        assert self.per_tile >= 2 and self.group >= 4 * HALO and 2 * cx <= lev
        assert self.cols * self.group == rows and HALO * 2 * self.field_tiles <= self.cols
        self.mask_tile = FIELDS * cx
        self.halo_tiles = FIELDS * HALO

    def lanes(self):
        return lax.broadcasted_iota(jnp.int32, (self.lev, self.rows), 1)

    def levels(self):
        return lax.broadcasted_iota(jnp.int32, (self.lev, self.rows), 0)

    def row(self, ref, tile, r):
        return jnp.broadcast_to(ref[tile, r : r + 1, :], (self.lev, self.rows))

    def edge_at(self, comp, ch):
        t, q = divmod(ch, self.per_tile)
        return comp * self.field_tiles + t, q

    def halo_at(self, comp, side, ch, d):
        return (self.halo_tiles if comp == side else 0) + ch * HALO + d

    def near_block(self, part, t, d):
        return (d * 2 + part) * self.field_tiles + t

    def edge_place(self, acc, value, j, channel, lane):
        at = (j * self.group + channel * 2 * HALO + HALO) % self.rows
        return jnp.where((lane >= at - HALO) & (lane < at + HALO), lane_roll(value, at), acc)


def load_kernel(sh, *refs):
    sources, x_ref, near_ref, arrived, sem = refs[:4], refs[4], refs[5], refs[6:10], refs[10]
    copies = [
        pltpu.make_async_copy(a, b, sem.at[i]) for i, (a, b) in enumerate(zip(sources, arrived))
    ]
    for copy in copies:
        copy.start()
    for copy in copies:
        copy.wait()
    state_ref, irr_ref, land_ref, bottom_ref = arrived
    odd, core0 = is_odd("gx"), first_core()
    zero = jnp.zeros((sh.lev, sh.rows), jnp.float32)
    own_columns(sh, state_ref, x_ref, odd, core0)
    near_ref[0] = near_edges(sh, x_ref, 0, core0, zero)
    cx = sh.cx
    lane = sh.lanes()
    depth = jnp.where(land_ref[...] == 1, bottom_ref[...], 0).astype(jnp.float32)
    masks = zero
    for q, value in enumerate((irr_ref[...], depth)):
        rows = [
            jnp.where(odd, value[cx - 1 - k : cx - k, :], value[k : k + 1, :]) for k in range(cx)
        ]
        for k in range(cx):
            x_ref[sh.mask_tile, q * cx + k : q * cx + k + 1, :] = rows[k]
        for d in range(HALO):
            row = jnp.where(core0, rows[cx - 1 - d], rows[d])
            wide = jnp.broadcast_to(row, (sh.lev, sh.rows))
            masks = sh.edge_place(masks, wide, d, q, lane)
    near_ref[1] = masks


def near_edges(sh, x_ref, part, core0, acc):
    lane = sh.lanes()
    flip = turned(part, core0)
    for ch in range(FIELDS):
        t, q = sh.edge_at(0, ch)
        for d in range(HALO):
            value = jnp.where(core0, x_ref[ch * sh.cx + sh.cx - 1 - d], x_ref[ch * sh.cx + d])
            if ch in VEL_X:
                value = value * flip
            acc = sh.edge_place(acc, value, sh.near_block(part, t, d), q, lane)
    return acc


def turned(part, core0):
    return jnp.where(core0, -1.0, 1.0) if part == 0 else jnp.where(core0, 1.0, -1.0)


def is_odd(axis):
    return lax.axis_index(axis) % 2 == 1


def first_core():
    return lax.axis_index("comp") == 0


def own_columns(sh, state_ref, x_ref, odd, dynamics):
    flip = jnp.where(odd & dynamics, -1.0, 1.0)
    cx = sh.cx
    for ch in range(FIELDS):
        raw = [state_ref[pl.ds(ch * sh.lev * cx + i, sh.lev, stride=cx), :] for i in range(cx)]
        for k in range(cx):
            value = jnp.where(odd, raw[cx - 1 - k], raw[k])
            x_ref[ch * cx + k] = value * flip if ch in VEL_X else value


def send_kernel(sh, state_ref, xo_ref, own_ref, xp_ref, near_ref, m_ref):
    core0 = first_core()
    own_columns(sh, state_ref, xp_ref, is_odd("gx"), jnp.logical_not(core0))
    near_ref[0] = near_edges(sh, xp_ref, 1, core0, own_ref[0])
    near_ref[1] = own_ref[1]
    cx = sh.cx
    for part, x_ref in enumerate((xo_ref, xp_ref)):
        for ch in range(FIELDS):
            for d in range(HALO):
                value = jnp.where(core0, x_ref[ch * cx + d], x_ref[ch * cx + cx - 1 - d])
                if ch in VEL_X:
                    value = value * turned(part, core0)
                m_ref[part * sh.halo_tiles + ch * HALO + d] = value
    m_ref[2 * sh.halo_tiles] = xo_ref[sh.mask_tile]


def edge_kernel(sh, xo_ref, xp_ref, e_ref):
    lane = sh.lanes()
    core0 = first_core()
    cx = sh.cx
    edges = [jnp.zeros((sh.lev, sh.rows), jnp.float32)] * sh.edge_tiles
    for comp in range(2):
        for ch in range(FIELDS):
            t, q = sh.edge_at(comp, ch)
            for k in range(cx):
                pair = xo_ref[ch * cx + k], xp_ref[ch * cx + k]
                value = jnp.where(core0, pair[comp], pair[1 - comp])
                edges[t] = sh.edge_place(edges[t], value, k + HALO, q, lane)
    for q in range(2):
        for k in range(cx):
            value = sh.row(xo_ref, sh.mask_tile, q * cx + k)
            edges[-1] = sh.edge_place(edges[-1], value, k + HALO, q, lane)
    for t in range(sh.edge_tiles):
        e_ref[t] = edges[t]


def merge_kernel(sh, e_ref, a_ref, b_ref, eo_ref):
    core0 = first_core()
    column = sh.lanes() // sh.group
    got = [
        (jnp.where(core0, a_ref[i], b_ref[i]), jnp.where(core0, b_ref[i], a_ref[i]))
        for i in range(2)
    ]
    for tile in range(sh.edge_tiles):
        edge = e_ref[tile]
        comp, t = divmod(tile, sh.field_tiles)
        for side in range(2):
            for d in range(HALO):
                place = sh.cx + HALO + d if side == 0 else HALO - 1 - d
                if tile == sh.edge_tiles - 1:
                    source, block = got[1][side], d
                else:
                    source, block = got[0][side], sh.near_block(int(comp != side), t, d)
                edge = jnp.where(column == place, lane_roll(source, (place - block) * sh.group), edge)
        eo_ref[tile] = edge


STRIP = "strip"


class Field:
    def __init__(self, sh, lane, col=None, strip=None, seam=None, rough=None):
        self.sh, self.lane, self.col, self.strip = sh, lane, col, strip
        self.seam, self.rough = seam, rough

    def centre(self, site):
        return self.strip() if site == STRIP else self.col(site)

    def east(self, site):
        return lane_roll(self.strip(), -self.sh.group) if site == STRIP else self.col(site + 1)

    def west(self, site):
        return lane_roll(self.strip(), self.sh.group) if site == STRIP else self.col(site - 1)

    def along_rows(self, site):
        inner = site == STRIP or self.rough is None
        value = self.centre(site) if inner else self.rough(site)
        north, south = lane_roll(value, -1), lane_roll(value, 1)
        if site == STRIP or self.seam is None:
            return north, south
        beyond = self.seam(site)
        more = 0 if inner else 1
        last = self.lane >= self.sh.rows - 1 - more
        return jnp.where(last, beyond, north), jnp.where(self.lane <= more, beyond, south)

    def around(self, site):
        return (self.east(site), self.west(site)) + self.along_rows(site)


GRAZED = (FIELDS, FIELDS + 1)
FLOW = tuple(FIELDS + ch for ch in (U, V, TEMP, SALT))
PRESSURE = FIELDS + 2
FRESH = FIELDS + 4


class Model:
    def __init__(self, sh):
        self.sh = sh
        self.lane, self.level = sh.lanes(), sh.levels()
        self.levelf = self.level.astype(jnp.float32)
        self.in_group = self.lane % sh.group
        self.core0 = first_core()
        self.odd_x = is_odd("gx")
        self.mirror = jnp.where(self.odd_x, -1.0, 1.0)
        self.gy, self.ny = lax.axis_index("gy"), lax.axis_size("gy")
        self.first_step = list(range(1, sh.cols - 1))
        self.own = list(range(HALO, HALO + sh.cx))
        self.n_sites = len(self.first_step)

    def fresh_at(self, index, site):
        return index * self.n_sites + site - 1

    def cumulate(self, x):
        reach = 1
        while reach < self.sh.lev:
            x = x + jnp.where(self.level >= reach, level_roll(x, reach), 0.0)
            reach *= 2
        return x

    def wet_of(self, depth):
        return jnp.where(self.levelf < depth, 1.0, 0.0)

    def faces(self, site):
        w = self.wet.centre(site)
        return [w * value for value in self.wet.around(site)]

    def density(self, d, site):
        rho = 0.8 * d[SALT].centre(site) - 0.2 * d[TEMP].centre(site)
        return rho * self.wet.centre(site)

    def pressure(self, d, site):
        return 0.1 * self.cumulate(self.density(d, site))

    def speeds(self, u, v, site, m):
        uc, vc = u.centre(site), v.centre(site)
        north, south = v.along_rows(site)
        qe = 0.025 * (uc + u.east(site)) * m[0]
        qw = 0.025 * (uc + u.west(site)) * m[1]
        qn = 0.025 * (vc + north) * m[2]
        qs = 0.025 * (vc + south) * m[3]
        return qe, qw, qn, qs, (qw - qe) + (qs - qn)

    def laplacian(self, f, site, m, total):
        e, w, n, s = f.around(site)
        return (m[0] * e + m[1] * w) + (m[2] * n + m[3] * s) - total * f.centre(site)

    def coriolis(self, site):
        sh, at = self.sh, self.in_group
        row = self.lane
        if site == STRIP:
            row = jnp.where(at < sh.half, at - HALO, sh.rows - HALO + at - sh.half)
        row = (row + self.gy * sh.rows).astype(jnp.float32)
        return self.mirror * (0.3 + 0.4 * row / (self.ny * sh.rows))

    def dynamics(self, d, pressure, site, heat, q, m):
        w = self.wet.centre(site)
        total = (m[0] + m[1]) + (m[2] + m[3])
        uc, vc = d[U].centre(site), d[V].centre(site)
        pc = pressure.centre(site)
        pe, pw, pn, ps = pressure.around(site)
        push_x = 0.1 * (m[0] * (pe - pc) + m[1] * (pc - pw))
        push_y = 0.1 * (m[2] * (pn - pc) + m[3] * (pc - ps))
        f = 0.2 * self.coriolis(site) * w
        spread = {ch: 0.04 * self.laplacian(d[ch], site, m, total) for ch in (UB, VB)}
        after = {
            U: d[UB].centre(site) + (f * vc - push_x + spread[UB]),
            V: d[VB].centre(site) + (spread[VB] - f * uc - push_y),
        }
        if heat is None:
            return after
        qe, qw, qn, qs, qc = q
        for now, before in ((TEMP, TB), (SALT, SB)):
            e, w_, n, s = d[now].around(site)
            carried = (qw * w_ - qe * e) + (qs * s - qn * n) + qc * d[now].centre(site)
            change = 2.0 * carried + 0.04 * self.laplacian(d[before], site, m, total)
            if now == TEMP:
                change = change + 0.6 * heat
            after[now] = d[before].centre(site) + change
        return after

    def filtered(self, d, site, ch, after):
        now, before = d[ch].centre(site), d[ch + 4].centre(site)
        return now + 0.1 * (before - 2.0 * now + after) * self.wet.centre(site)

    def optics(self, c, site):
        absorb = 0.08 + 0.05 * (jnp.abs(c[2].centre(site)) + jnp.abs(c[3].centre(site)))
        return absorb, self.cumulate(absorb)

    def heating(self, absorb, depthsum, site):
        fade = jnp.exp(-depthsum)
        above = jnp.where(self.level == 0, 1.0, level_roll(fade, 1))
        return self.irr_at(site) * self.wet.centre(site) * (above - fade)

    def light(self, absorb, depthsum, site):
        return self.irr_at(site) * jnp.exp(0.5 * absorb - depthsum)

    def mixing(self, d, site):
        rho = self.density(d, site)
        below = level_roll(rho, -1)
        wet_below = jnp.where(self.levelf + 1.0 < self.depth_at(site), 1.0, 0.0)
        return (0.005 + 0.1 / (1.0 + 4.0 * jnp.maximum(below - rho, 0.0))) * wet_below

    def reactions(self, c, temp, lit, which):
        nn, na = jnp.abs(c[0]), jnp.abs(c[1])
        base = jnp.exp(0.06 * temp) * (lit / (lit + 0.5))
        total = nn + na
        small = 0.6 * base * c[2] / (0.2 + total)
        large = 0.9 * base * c[3] / (0.8 + total)
        graze = 0.8 * c[4] / (1.0 + (jnp.abs(c[2]) + jnp.abs(c[3])))
        gs, gl = graze * c[2], graze * c[3]
        up_s, up_l = small * total, large * total
        r = {2: up_s - gs - 0.1 * c[2], 3: up_l - gl - 0.1 * c[3]}
        if len(which) > 2:
            both = small + large
            remin = 0.3 * c[5] + 0.1 * c[6]
            nitrify = 0.2 * c[1]
            r[0] = nitrify - both * nn
            r[1] = remin + 0.1 * c[4] - nitrify - both * na
            r[4] = 0.7 * (gs + gl) - 0.25 * c[4]
            r[5] = 0.1 * c[2] + 0.3 * gs - 0.3 * c[5]
            r[6] = 0.1 * c[3] + 0.15 * c[4] + 0.3 * gl - 0.1 * c[6]
            r[7] = 1.3 * (up_s + up_l) - (remin + 2.0 * nitrify)
        return r

    def tracers(self, c, d, site, q, m, lit, which):
        w = self.wet.centre(site)
        qe, qw, qn, qs, qc = q
        total = (m[0] + m[1]) + (m[2] + m[3])
        ke, kw = 0.02 * m[0] - qe, 0.02 * m[1] + qw
        kn, ks = 0.02 * m[2] - qn, 0.02 * m[3] + qs
        kc = (1.0 - 0.02 * total) + qc
        kappa = self.mixing(d, site)
        centre = {i: c[i].centre(site) for i in (which if len(which) > 2 else range(5))}
        r = self.reactions(centre, d[TEMP].centre(site), lit, which)
        tenth = 0.1 * w
        for i in which:
            e, w_, n, s = c[i].around(site)
            here = centre[i]
            down = kappa * (level_roll(here, -1) - here)
            moved = (ke * e + kw * w_) + (kn * n + ks * s)
            yield i, kc * here + moved + (down - level_roll(down, 1)) + tenth * r[i]

    def first_core_site(self, d, c, pressure, site, store, plankton):
        m = self.faces(site)
        q = self.speeds(d[U], d[V], site, m)
        optic = self.optics(c, site)
        after = self.dynamics(d, pressure, site, self.heating(*optic, site), q, m)
        for ch, value in after.items():
            store(ch, site, value)
            store(ch + 4, site, self.filtered(d, site, ch, value))
        if plankton:
            for i, value in self.tracers(c, d, site, q, m, self.light(*optic, site), (2, 3)):
                store(GRAZED[i - 2], site, value)

    def second_core_site(self, d, c, pressure, site, store, heated):
        m = self.faces(site)
        q = self.speeds(d[U], d[V], site, m)
        optic = self.optics(c, site)
        if pressure is not None:
            heat = self.heating(*optic, site) if heated else None
            for ch, value in self.dynamics(d, pressure, site, heat, q, m).items():
                store(FLOW[ch], site, value)
        lit = self.light(*optic, site)
        for i, value in self.tracers(c, d, site, q, m, lit, range(FIELDS)):
            store(i, site, value)


def column_kernel(sh, xo, xp, rx, rp, fresh, wet_ref, press):
    md = Model(sh)
    cx = sh.cx

    def mask_row(kind, j):
        if HALO <= j < HALO + cx:
            return sh.row(xo, sh.mask_tile, kind * cx + j - HALO)
        if j < HALO:
            first, second, at = rx, rp, HALO - 1 - j
        else:
            first, second, at = rp, rx, cx - 1 - (j - HALO - cx)
        tile = 2 * sh.halo_tiles
        return jnp.where(
            md.core0, sh.row(first, tile, kind * cx + at), sh.row(second, tile, kind * cx + at)
        )

    md.irr_at = lambda site: mask_row(0, site)
    md.depth_at = lambda site: mask_row(1, site)
    for j in range(sh.cols):
        wet_ref[j] = md.wet_of(mask_row(1, j))
    md.wet = Field(sh, md.lane, lambda j: wet_ref[j])

    def raw(x, sides, comp, ch):
        def col(j):
            if HALO <= j < HALO + cx:
                return x[ch * cx + j - HALO]
            if j < HALO:
                return sides[1][sh.halo_at(comp, 1, ch, HALO - 1 - j)]
            return sides[0][sh.halo_at(comp, 0, ch, j - HALO - cx)]

        return Field(sh, md.lane, col)

    def store(index, site, value):
        fresh[md.fresh_at(index, site)] = value

    def fields(x, sides, comp):
        return [raw(x, sides, comp, ch) for ch in range(FIELDS)]

    def pressure_of(d):
        for j in range(sh.cols):
            press[j] = md.pressure(d, j)
        return Field(sh, md.lane, lambda j: press[j])

    @pl.when(md.core0)
    def _():
        d, c = fields(xo, (rp, rx), 0), fields(xp, (rp, rx), 1)
        pressure = pressure_of(d)
        for site in md.first_step:
            md.first_core_site(d, c, pressure, site, store, site in md.own)
        d = [
            Field(sh, md.lane, lambda j, ch=ch: fresh[md.fresh_at(ch, j)]) for ch in range(FIELDS)
        ]
        for site in md.first_step:
            store(PRESSURE, site, md.pressure(d, site))

    @pl.when(jnp.logical_not(md.core0))
    def _():
        d, c = fields(xp, (rx, rp), 0), fields(xo, (rx, rp), 1)
        pressure = pressure_of(d)
        for site in md.first_step:
            md.second_core_site(d, c, pressure, site, store, site in md.own)


def step_kernel(sh, xo, wet_ref, fresh, edges, y, yp, out_ref, strips, cols, rims, seams):
    md = Model(sh)
    cx, lane, in_group = sh.cx, md.lane, md.in_group
    end = sh.rows - 1
    even_y = md.gy % 2 == 0
    slot = lane % (2 * HALO)
    zero = jnp.zeros((sh.lev, sh.rows), jnp.float32)

    def build_strips():
        strips_of(2 * FIELDS, [sh.edge_tiles - 1], 2)
        strips_of(0, range(2 * sh.field_tiles), sh.per_tile)

    def strips_of(base, tiles, channels):
        for t in tiles:
            a, b = jnp.where(md.core0, y[t], yp[t]), jnp.where(md.core0, yp[t], y[t])
            mine = edges[t]
            left = jnp.where(md.gy > 0, jnp.where(even_y, b, a), zero)
            right = jnp.where(md.gy < md.ny - 1, jnp.where(even_y, a, b), zero)
            low = jnp.where(slot < HALO, left, mine)
            high = jnp.where(slot < HALO, mine, right)
            for q in range(channels):
                at = q * 2 * HALO
                strips[base + (t - tiles[0]) * sh.per_tile + q] = jnp.where(
                    in_group < sh.half, lane_roll(low, -at), lane_roll(high, sh.half - at)
                )

    def mask_at(kind, site):
        if site == STRIP:
            return strips[2 * FIELDS + kind]
        return sh.row(xo, sh.mask_tile, kind * cx + site - HALO)

    md.irr_at = lambda site: mask_at(0, site)
    md.depth_at = lambda site: mask_at(1, site)

    def beside(strip, low, high):
        at = sh.half + high
        return jnp.where(in_group > at, lane_roll(strip, at + 1 - low), strip)

    def to_ends(pair, site, high):
        return lane_roll(pair, end - (site * sh.group + sh.half + high))

    def seam_of(ref, index):
        return lambda site: to_ends(ref[index], site, HALO)

    def prepare():
        build_strips()
        wet_strip = md.wet_of(strips[2 * FIELDS + 1])
        wet_pair = beside(wet_strip, HALO - 1, HALO)
        md.wet = Field(
            sh,
            lane,
            lambda j: wet_ref[j],
            lambda: wet_strip,
            lambda site: to_ends(wet_pair, site, HALO),
        )
        d = [strip_field(ch) for ch in range(FIELDS)]
        c = [strip_field(FIELDS + ch) for ch in range(FIELDS)]
        pressure = md.pressure(d, STRIP)
        return d, c, Field(sh, lane, strip=lambda: pressure)

    def strip_field(index):
        return Field(sh, lane, strip=lambda: strips[index])

    def rim(index, site, value):
        rims[index] = value

    def renewed(index, sites):
        value = rims[index]
        seams[index] = beside(value, HALO - 1, HALO)
        ends = beside(value, HALO, HALO - 1)
        for site in sites:
            cols[md.fresh_at(index, site)] = jnp.where(
                (lane == 0) | (lane == end),
                to_ends(ends, site, HALO - 1),
                fresh[md.fresh_at(index, site)],
            )
        return stored(index)

    def stored(index):
        return Field(
            sh,
            lane,
            lambda j: cols[md.fresh_at(index, j)],
            lambda: rims[index],
            seam_of(seams, index),
            lambda j: fresh[md.fresh_at(index, j)],
        )

    def write(ch, k_values):
        for i in range(cx):
            out_ref[pl.ds(ch * sh.lev * cx + i, sh.lev, stride=cx), :] = jnp.where(
                md.odd_x, k_values[cx - 1 - i], k_values[i]
            )

    done = {}

    def keep(ch, site, value):
        done[ch, site] = value

    @pl.when(md.core0)
    def _():
        d, c, pressure = prepare()
        md.first_core_site(d, c, pressure, STRIP, rim, True)
        d1 = [renewed(ch, md.own if ch == V else md.first_step) for ch in range(FIELDS)]
        c1 = {i: renewed(GRAZED[i - 2], md.own) for i in (2, 3)}
        rim(PRESSURE, STRIP, md.pressure(d1, STRIP))
        pressure1 = renewed(PRESSURE, md.first_step)
        for site in md.own:
            md.first_core_site(d1, c1, pressure1, site, keep, False)
        for ch in range(FIELDS):
            values = [done[ch, site] for site in md.own]
            write(ch, [v * md.mirror for v in values] if ch in VEL_X else values)

    @pl.when(jnp.logical_not(md.core0))
    def _():
        d, c, pressure = prepare()
        md.second_core_site(d, c, pressure, STRIP, rim, True)
        c1 = [renewed(ch, md.first_step) for ch in range(FIELDS)]
        d1 = [renewed(FLOW[ch], md.first_step if ch == U else md.own) for ch in range(4)]
        for site in md.own:
            md.second_core_site(d1, c1, None, site, keep, False)
        for ch in range(FIELDS):
            write(ch, [done[ch, site] for site in md.own])


def tiles(sh, n):
    return jax.ShapeDtypeStruct((n, sh.lev, sh.rows), jnp.float32)


def call(kernel, sh, outs, args, flops, scratch=(), source=pltpu.VMEM):
    spec = pl.BlockSpec(memory_space=pltpu.VMEM)
    size = sum(a.size for a in args) + sum(o.size for o in outs)
    return pl.pallas_call(
        lambda *refs: kernel(sh, *refs),
        out_shape=outs,
        in_specs=[pl.BlockSpec(memory_space=source)] * len(args),
        out_specs=[spec] * len(outs),
        scratch_shapes=list(scratch),
        compiler_params=pltpu.CompilerParams(vmem_limit_bytes=16 << 20),
        cost_estimate=pl.CostEstimate(flops=flops, bytes_accessed=4 * size, transcendentals=0),
    )(*args)


def local(ocean_state, irradiance, land_mask, bottom_level):
    fields, lev, cx, rows = ocean_state.shape
    assert fields == FIELDS
    sh = Shape(lev, cx, rows)
    nx, ny = lax.axis_size("gx"), lax.axis_size("gy")
    assert nx % 2 == 0 and ny % 2 == 0
    axes = ("comp", "gy", "gx")

    def send(value, target):
        pairs = []
        for c in range(2):
            for y in range(ny):
                for x in range(nx):
                    tc, ty, tx = target(c, y, x)
                    pairs.append(((c * ny + y) * nx + x, (tc * ny + ty) * nx + tx))
        return lax.ppermute(value, axes, pairs)

    def odd_pair(i, n):
        return (i + 1) % n if i % 2 else (i - 1) % n

    def pair(i, n, core):
        return i ^ 1 if core == 0 else odd_pair(i, n)

    def edges_x(v):
        return send(v, lambda c, y, x: (c, y, pair(x, nx, c)))

    def bulk_x(v):
        return send(v, lambda c, y, x: (c, y, pair(x, nx, 1 - c)))

    def along_y(v):
        return send(v, lambda c, y, x: (c, pair(y, ny, c), x))

    def swap(v):
        return send(v, lambda c, y, x: (1 - c, y, x))

    flat = ocean_state.reshape(fields * lev * cx, rows)
    partner = swap(flat)
    inputs = (flat, irradiance, land_mask, bottom_level)
    near = tiles(sh, 2)
    xo, own_near = call(
        load_kernel,
        sh,
        [tiles(sh, fields * cx + 1), near],
        tuple(pltpu.with_memory_space_constraint(a, pltpu.HBM) for a in inputs),
        100_000,
        scratch=[pltpu.VMEM(a.shape, a.dtype) for a in inputs] + [pltpu.SemaphoreType.DMA((4,))],
        source=pltpu.HBM,
    )
    edge, message = tiles(sh, sh.edge_tiles), tiles(sh, 2 * sh.halo_tiles + 1)
    xp, nx_edges, m = call(
        send_kernel, sh, [tiles(sh, fields * cx), near, message], (partner, xo, own_near), 100_000
    )
    ex = edges_x(nx_edges)
    rx = bulk_x(m)
    ep = swap(ex)
    (e0,) = call(edge_kernel, sh, [edge], (xo, xp), 100_000)
    (e1,) = call(merge_kernel, sh, [edge], (e0, ex, ep), 10_000)
    y = along_y(e1)
    rp = swap(rx)
    yp = swap(y)
    n_sites = sh.cols - 2
    fresh, wet = call(
        column_kernel,
        sh,
        [tiles(sh, FRESH * n_sites), tiles(sh, sh.cols)],
        (xo, xp, rx, rp),
        1_000_000,
        scratch=[pltpu.VMEM((sh.cols, lev, rows), jnp.float32)],
    )
    (out,) = call(
        step_kernel,
        sh,
        [jax.ShapeDtypeStruct(flat.shape, jnp.float32)],
        (xo, wet, fresh, e1, y, yp),
        1_000_000,
        scratch=[
            pltpu.VMEM((2 * FIELDS + 2, lev, rows), jnp.float32),
            pltpu.VMEM((FRESH * n_sites, lev, rows), jnp.float32),
            pltpu.VMEM((FRESH, lev, rows), jnp.float32),
            pltpu.VMEM((FRESH, lev, rows), jnp.float32),
        ],
    )
    return out.reshape(ocean_state.shape)


def solution(mesh):
    return jax.shard_map(
        local,
        mesh=mesh,
        in_specs=(P("comp", None, "gx", "gy"), P("gx", "gy"), P("gx", "gy"), P("gx", "gy")),
        out_specs=P("comp", None, "gx", "gy"),
        check_vma=False,
    )
```

```python
import jax
import jax.numpy as jnp
from jax import lax
from jax.experimental import pallas as pl
from jax.experimental.pallas import tpu as pltpu
from jax.sharding import PartitionSpec as P


HALO = 2
FIELDS = 8
U, V, TEMP, SALT, UB, VB, TB, SB = range(FIELDS)
VEL_X = (U, UB)


def lane_roll(x, shift):
    shift %= x.shape[1]
    return pltpu.roll(x, shift, 1) if shift else x


def level_roll(x, shift):
    shift %= x.shape[0]
    return pltpu.roll(x, shift, 0) if shift else x


class Shape:
    def __init__(self, lev, cx, rows):
        self.lev, self.cx, self.rows = lev, cx, rows
        self.cols = cx + 2 * HALO
        self.group = rows // self.cols
        self.per_tile = self.group // (2 * HALO)
        self.half = self.group // 2
        self.field_tiles = -(-FIELDS // self.per_tile)
        self.edge_tiles = 2 * self.field_tiles + 1
        assert self.per_tile >= 2 and self.group >= 4 * HALO and 2 * cx <= lev
        assert self.cols * self.group == rows and HALO * 2 * self.field_tiles <= self.cols
        self.mask_tile = FIELDS * cx
        self.halo_tiles = FIELDS * HALO

    def lanes(self):
        return lax.broadcasted_iota(jnp.int32, (self.lev, self.rows), 1)

    def levels(self):
        return lax.broadcasted_iota(jnp.int32, (self.lev, self.rows), 0)

    def row(self, ref, tile, r):
        return jnp.broadcast_to(ref[tile, r : r + 1, :], (self.lev, self.rows))

    def edge_at(self, comp, ch):
        t, q = divmod(ch, self.per_tile)
        return comp * self.field_tiles + t, q

    def halo_at(self, comp, side, ch, d):
        return (self.halo_tiles if comp == side else 0) + ch * HALO + d

    def near_block(self, part, t, d):
        return (d * 2 + part) * self.field_tiles + t

    def edge_place(self, acc, value, j, channel, lane):
        at = (j * self.group + channel * 2 * HALO + HALO) % self.rows
        return jnp.where((lane >= at - HALO) & (lane < at + HALO), lane_roll(value, at), acc)


def load_kernel(sh, *refs):
    sources, x_ref, near_ref, arrived, sem = refs[:4], refs[4], refs[5], refs[6:10], refs[10]
    copies = [
        pltpu.make_async_copy(a, b, sem.at[i]) for i, (a, b) in enumerate(zip(sources, arrived))
    ]
    for copy in copies:
        copy.start()
    for copy in copies:
        copy.wait()
    state_ref, irr_ref, land_ref, bottom_ref = arrived
    odd, core0 = is_odd("gx"), first_core()
    zero = jnp.zeros((sh.lev, sh.rows), jnp.float32)
    own_columns(sh, state_ref, x_ref, odd, core0)
    near_ref[0] = near_edges(sh, x_ref, 0, core0, zero)
    cx = sh.cx
    lane = sh.lanes()
    depth = jnp.where(land_ref[...] == 1, bottom_ref[...], 0).astype(jnp.float32)
    masks = zero
    for q, value in enumerate((irr_ref[...], depth)):
        rows = [
            jnp.where(odd, value[cx - 1 - k : cx - k, :], value[k : k + 1, :]) for k in range(cx)
        ]
        for k in range(cx):
            x_ref[sh.mask_tile, q * cx + k : q * cx + k + 1, :] = rows[k]
        for d in range(HALO):
            row = jnp.where(core0, rows[cx - 1 - d], rows[d])
            wide = jnp.broadcast_to(row, (sh.lev, sh.rows))
            masks = sh.edge_place(masks, wide, d, q, lane)
    near_ref[1] = masks


def near_edges(sh, x_ref, part, core0, acc):
    lane = sh.lanes()
    flip = turned(part, core0)
    for ch in range(FIELDS):
        t, q = sh.edge_at(0, ch)
        for d in range(HALO):
            value = jnp.where(core0, x_ref[ch * sh.cx + sh.cx - 1 - d], x_ref[ch * sh.cx + d])
            if ch in VEL_X:
                value = value * flip
            acc = sh.edge_place(acc, value, sh.near_block(part, t, d), q, lane)
    return acc


def turned(part, core0):
    return jnp.where(core0, -1.0, 1.0) if part == 0 else jnp.where(core0, 1.0, -1.0)


def is_odd(axis):
    return lax.axis_index(axis) & 1 == 1


def first_core():
    return lax.axis_index("comp") == 0


def own_columns(sh, state_ref, x_ref, odd, dynamics):
    flip = jnp.where(odd & dynamics, -1.0, 1.0)
    cx = sh.cx
    for ch in range(FIELDS):
        raw = [state_ref[pl.ds(ch * sh.lev * cx + i, sh.lev, stride=cx), :] for i in range(cx)]
        for k in range(cx):
            value = jnp.where(odd, raw[cx - 1 - k], raw[k])
            x_ref[ch * cx + k] = value * flip if ch in VEL_X else value


def send_kernel(sh, state_ref, xo_ref, own_ref, xp_ref, near_ref, m_ref):
    core0 = first_core()
    own_columns(sh, state_ref, xp_ref, is_odd("gx"), jnp.logical_not(core0))
    near_ref[0] = near_edges(sh, xp_ref, 1, core0, own_ref[0])
    near_ref[1] = own_ref[1]
    cx = sh.cx
    for part, x_ref in enumerate((xo_ref, xp_ref)):
        for ch in range(FIELDS):
            for d in range(HALO):
                value = jnp.where(core0, x_ref[ch * cx + d], x_ref[ch * cx + cx - 1 - d])
                if ch in VEL_X:
                    value = value * turned(part, core0)
                m_ref[part * sh.halo_tiles + ch * HALO + d] = value
    m_ref[2 * sh.halo_tiles] = xo_ref[sh.mask_tile]


def edge_kernel(sh, xo_ref, xp_ref, e_ref):
    lane = sh.lanes()
    core0 = first_core()
    cx = sh.cx
    edges = [jnp.zeros((sh.lev, sh.rows), jnp.float32)] * sh.edge_tiles
    for comp in range(2):
        for ch in range(FIELDS):
            t, q = sh.edge_at(comp, ch)
            for k in range(cx):
                pair = xo_ref[ch * cx + k], xp_ref[ch * cx + k]
                value = jnp.where(core0, pair[comp], pair[1 - comp])
                edges[t] = sh.edge_place(edges[t], value, k + HALO, q, lane)
    for q in range(2):
        for k in range(cx):
            value = sh.row(xo_ref, sh.mask_tile, q * cx + k)
            edges[-1] = sh.edge_place(edges[-1], value, k + HALO, q, lane)
    for t in range(sh.edge_tiles):
        e_ref[t] = edges[t]


def merge_kernel(sh, e_ref, a_ref, b_ref, eo_ref):
    core0 = first_core()
    column = sh.lanes() // sh.group
    got = [
        (jnp.where(core0, a_ref[i], b_ref[i]), jnp.where(core0, b_ref[i], a_ref[i]))
        for i in range(2)
    ]
    for tile in range(sh.edge_tiles):
        edge = e_ref[tile]
        comp, t = divmod(tile, sh.field_tiles)
        for side in range(2):
            for d in range(HALO):
                place = sh.cx + HALO + d if side == 0 else HALO - 1 - d
                if tile == sh.edge_tiles - 1:
                    source, block = got[1][side], d
                else:
                    source, block = got[0][side], sh.near_block(int(comp != side), t, d)
                edge = jnp.where(column == place, lane_roll(source, (place - block) * sh.group), edge)
        eo_ref[tile] = edge


STRIP = "strip"


class Field:
    def __init__(self, sh, lane, col=None, strip=None, seam=None, rough=None):
        self.sh, self.lane, self.col, self.strip = sh, lane, col, strip
        self.seam, self.rough = seam, rough

    def centre(self, site):
        return self.strip() if site == STRIP else self.col(site)

    def east(self, site):
        return lane_roll(self.strip(), -self.sh.group) if site == STRIP else self.col(site + 1)

    def west(self, site):
        return lane_roll(self.strip(), self.sh.group) if site == STRIP else self.col(site - 1)

    def along_rows(self, site):
        inner = site == STRIP or self.rough is None
        value = self.centre(site) if inner else self.rough(site)
        north, south = lane_roll(value, -1), lane_roll(value, 1)
        if site == STRIP or self.seam is None:
            return north, south
        beyond = self.seam(site)
        more = 0 if inner else 1
        last = self.lane >= self.sh.rows - 1 - more
        return jnp.where(last, beyond, north), jnp.where(self.lane <= more, beyond, south)

    def around(self, site):
        return (self.east(site), self.west(site)) + self.along_rows(site)


GRAZED = (FIELDS, FIELDS + 1)
FLOW = tuple(FIELDS + ch for ch in (U, V, TEMP, SALT))
PRESSURE = FIELDS + 2
FRESH = FIELDS + 4


class Model:
    def __init__(self, sh):
        self.sh = sh
        self.lane, self.level = sh.lanes(), sh.levels()
        self.levelf = self.level.astype(jnp.float32)
        self.in_group = self.lane % sh.group
        self.core0 = first_core()
        self.odd_x = is_odd("gx")
        self.mirror = jnp.where(self.odd_x, -1.0, 1.0)
        self.gy, self.ny = lax.axis_index("gy"), lax.axis_size("gy")
        self.first_step = list(range(1, sh.cols - 1))
        self.own = list(range(HALO, HALO + sh.cx))
        self.n_sites = len(self.first_step)

    def fresh_at(self, index, site):
        return index * self.n_sites + site - 1

    def cumulate(self, x):
        reach = 1
        while reach < self.sh.lev:
            x = x + jnp.where(self.level >= reach, level_roll(x, reach), 0.0)
            reach *= 2
        return x

    def wet_of(self, depth):
        return jnp.where(self.levelf < depth, 1.0, 0.0)

    def faces(self, site):
        w = self.wet.centre(site)
        return [w * value for value in self.wet.around(site)]

    def density(self, d, site):
        rho = 0.8 * d[SALT].centre(site) - 0.2 * d[TEMP].centre(site)
        return rho * self.wet.centre(site)

    def pressure(self, d, site):
        return 0.1 * self.cumulate(self.density(d, site))

    def speeds(self, u, v, site, m):
        uc, vc = u.centre(site), v.centre(site)
        north, south = v.along_rows(site)
        qe = 0.025 * (uc + u.east(site)) * m[0]
        qw = 0.025 * (uc + u.west(site)) * m[1]
        qn = 0.025 * (vc + north) * m[2]
        qs = 0.025 * (vc + south) * m[3]
        return qe, qw, qn, qs, (qw - qe) + (qs - qn)

    def laplacian(self, f, site, m, total):
        e, w, n, s = f.around(site)
        return (m[0] * e + m[1] * w) + (m[2] * n + m[3] * s) - total * f.centre(site)

    def coriolis(self, site):
        sh, at = self.sh, self.in_group
        row = self.lane
        if site == STRIP:
            row = jnp.where(at < sh.half, at - HALO, sh.rows - HALO + at - sh.half)
        row = (row + self.gy * sh.rows).astype(jnp.float32)
        return self.mirror * (0.3 + 0.4 * row / (self.ny * sh.rows))

    def dynamics(self, d, pressure, site, heat, q, m):
        w = self.wet.centre(site)
        total = (m[0] + m[1]) + (m[2] + m[3])
        uc, vc = d[U].centre(site), d[V].centre(site)
        pc = pressure.centre(site)
        pe, pw, pn, ps = pressure.around(site)
        push_x = 0.1 * (m[0] * (pe - pc) + m[1] * (pc - pw))
        push_y = 0.1 * (m[2] * (pn - pc) + m[3] * (pc - ps))
        f = 0.2 * self.coriolis(site) * w
        spread = {ch: 0.04 * self.laplacian(d[ch], site, m, total) for ch in (UB, VB)}
        after = {
            U: d[UB].centre(site) + (f * vc - push_x + spread[UB]),
            V: d[VB].centre(site) + (spread[VB] - f * uc - push_y),
        }
        if heat is None:
            return after
        qe, qw, qn, qs, qc = q
        for now, before in ((TEMP, TB), (SALT, SB)):
            e, w_, n, s = d[now].around(site)
            carried = (qw * w_ - qe * e) + (qs * s - qn * n) + qc * d[now].centre(site)
            change = 2.0 * carried + 0.04 * self.laplacian(d[before], site, m, total)
            if now == TEMP:
                change = change + 0.6 * heat
            after[now] = d[before].centre(site) + change
        return after

    def filtered(self, d, site, ch, after):
        now, before = d[ch].centre(site), d[ch + 4].centre(site)
        return now + 0.1 * (before - 2.0 * now + after) * self.wet.centre(site)

    def optics(self, c, site):
        absorb = 0.08 + 0.05 * (jnp.abs(c[2].centre(site)) + jnp.abs(c[3].centre(site)))
        return absorb, self.cumulate(absorb)

    def heating(self, absorb, depthsum, site):
        fade = jnp.exp(-depthsum)
        above = jnp.where(self.level == 0, 1.0, level_roll(fade, 1))
        return self.irr_at(site) * self.wet.centre(site) * (above - fade)

    def light(self, absorb, depthsum, site):
        return self.irr_at(site) * jnp.exp(0.5 * absorb - depthsum)

    def mixing(self, d, site):
        rho = self.density(d, site)
        below = level_roll(rho, -1)
        wet_below = jnp.where(self.levelf + 1.0 < self.depth_at(site), 1.0, 0.0)
        return (0.005 + 0.1 / (1.0 + 4.0 * jnp.maximum(below - rho, 0.0))) * wet_below

    def reactions(self, c, temp, lit, which):
        nn, na = jnp.abs(c[0]), jnp.abs(c[1])
        base = jnp.exp(0.06 * temp) * (lit / (lit + 0.5))
        total = nn + na
        small = 0.6 * base * c[2] / (0.2 + total)
        large = 0.9 * base * c[3] / (0.8 + total)
        graze = 0.8 * c[4] / (1.0 + (jnp.abs(c[2]) + jnp.abs(c[3])))
        gs, gl = graze * c[2], graze * c[3]
        up_s, up_l = small * total, large * total
        r = {2: up_s - gs - 0.1 * c[2], 3: up_l - gl - 0.1 * c[3]}
        if len(which) > 2:
            both = small + large
            remin = 0.3 * c[5] + 0.1 * c[6]
            nitrify = 0.2 * c[1]
            r[0] = nitrify - both * nn
            r[1] = remin + 0.1 * c[4] - nitrify - both * na
            r[4] = 0.7 * (gs + gl) - 0.25 * c[4]
            r[5] = 0.1 * c[2] + 0.3 * gs - 0.3 * c[5]
            r[6] = 0.1 * c[3] + 0.15 * c[4] + 0.3 * gl - 0.1 * c[6]
            r[7] = 1.3 * (up_s + up_l) - (remin + 2.0 * nitrify)
        return r

    def tracers(self, c, d, site, q, m, lit, which):
        w = self.wet.centre(site)
        qe, qw, qn, qs, qc = q
        total = (m[0] + m[1]) + (m[2] + m[3])
        ke, kw = 0.02 * m[0] - qe, 0.02 * m[1] + qw
        kn, ks = 0.02 * m[2] - qn, 0.02 * m[3] + qs
        kc = (1.0 - 0.02 * total) + qc
        kappa = self.mixing(d, site)
        centre = {i: c[i].centre(site) for i in (which if len(which) > 2 else range(5))}
        r = self.reactions(centre, d[TEMP].centre(site), lit, which)
        tenth = 0.1 * w
        for i in which:
            e, w_, n, s = c[i].around(site)
            here = centre[i]
            down = kappa * (level_roll(here, -1) - here)
            moved = (ke * e + kw * w_) + (kn * n + ks * s)
            yield i, kc * here + moved + (down - level_roll(down, 1)) + tenth * r[i]

    def first_core_site(self, d, c, pressure, site, store, plankton):
        m = self.faces(site)
        q = self.speeds(d[U], d[V], site, m)
        optic = self.optics(c, site)
        after = self.dynamics(d, pressure, site, self.heating(*optic, site), q, m)
        for ch, value in after.items():
            store(ch, site, value)
            store(ch + 4, site, self.filtered(d, site, ch, value))
        if plankton:
            for i, value in self.tracers(c, d, site, q, m, self.light(*optic, site), (2, 3)):
                store(GRAZED[i - 2], site, value)

    def second_core_site(self, d, c, pressure, site, store, heated):
        m = self.faces(site)
        q = self.speeds(d[U], d[V], site, m)
        optic = self.optics(c, site)
        if pressure is not None:
            heat = self.heating(*optic, site) if heated else None
            for ch, value in self.dynamics(d, pressure, site, heat, q, m).items():
                store(FLOW[ch], site, value)
        lit = self.light(*optic, site)
        for i, value in self.tracers(c, d, site, q, m, lit, range(FIELDS)):
            store(i, site, value)


def column_kernel(sh, xo, xp, rx, rp, fresh, wet_ref, press):
    md = Model(sh)
    cx = sh.cx

    def mask_row(kind, j):
        if HALO <= j < HALO + cx:
            return sh.row(xo, sh.mask_tile, kind * cx + j - HALO)
        if j < HALO:
            first, second, at = rx, rp, HALO - 1 - j
        else:
            first, second, at = rp, rx, cx - 1 - (j - HALO - cx)
        tile = 2 * sh.halo_tiles
        return jnp.where(
            md.core0, sh.row(first, tile, kind * cx + at), sh.row(second, tile, kind * cx + at)
        )

    md.irr_at = lambda site: mask_row(0, site)
    md.depth_at = lambda site: mask_row(1, site)
    for j in range(sh.cols):
        wet_ref[j] = md.wet_of(mask_row(1, j))
    md.wet = Field(sh, md.lane, lambda j: wet_ref[j])

    def raw(x, sides, comp, ch):
        def col(j):
            if HALO <= j < HALO + cx:
                return x[ch * cx + j - HALO]
            if j < HALO:
                return sides[1][sh.halo_at(comp, 1, ch, HALO - 1 - j)]
            return sides[0][sh.halo_at(comp, 0, ch, j - HALO - cx)]

        return Field(sh, md.lane, col)

    def store(index, site, value):
        fresh[md.fresh_at(index, site)] = value

    def fields(x, sides, comp):
        return [raw(x, sides, comp, ch) for ch in range(FIELDS)]

    def pressure_of(d):
        for j in range(sh.cols):
            press[j] = md.pressure(d, j)
        return Field(sh, md.lane, lambda j: press[j])

    @pl.when(md.core0)
    def _():
        d, c = fields(xo, (rp, rx), 0), fields(xp, (rp, rx), 1)
        pressure = pressure_of(d)
        for site in md.first_step:
            md.first_core_site(d, c, pressure, site, store, site in md.own)
        d = [
            Field(sh, md.lane, lambda j, ch=ch: fresh[md.fresh_at(ch, j)]) for ch in range(FIELDS)
        ]
        for site in md.first_step:
            store(PRESSURE, site, md.pressure(d, site))

    @pl.when(jnp.logical_not(md.core0))
    def _():
        d, c = fields(xp, (rx, rp), 0), fields(xo, (rx, rp), 1)
        pressure = pressure_of(d)
        for site in md.first_step:
            md.second_core_site(d, c, pressure, site, store, site in md.own)


def step_kernel(sh, xo, wet_ref, fresh, edges, y, yp, out_ref, strips, cols, rims, seams):
    md = Model(sh)
    cx, lane, in_group = sh.cx, md.lane, md.in_group
    end = sh.rows - 1
    even_y = md.gy & 1 == 0
    slot = lane % (2 * HALO)
    zero = jnp.zeros((sh.lev, sh.rows), jnp.float32)

    def build_strips(tracers):
        strips_of(2 * FIELDS, [sh.edge_tiles - 1], 2)
        strips_of(0, range(2 * sh.field_tiles), FIELDS + tracers)

    def strips_of(base, tiles, channels):
        for t in tiles:
            a, b = jnp.where(md.core0, y[t], yp[t]), jnp.where(md.core0, yp[t], y[t])
            mine = edges[t]
            left = jnp.where(md.gy > 0, jnp.where(even_y, b, a), zero)
            right = jnp.where(md.gy < md.ny - 1, jnp.where(even_y, a, b), zero)
            low = jnp.where(slot < HALO, left, mine)
            high = jnp.where(slot < HALO, mine, right)
            first = (t - tiles[0]) * sh.per_tile
            for q in range(min(channels - first, sh.per_tile)):
                at = q * 2 * HALO
                strips[base + first + q] = jnp.where(
                    in_group < sh.half, lane_roll(low, -at), lane_roll(high, sh.half - at)
                )

    def mask_at(kind, site):
        if site == STRIP:
            return strips[2 * FIELDS + kind]
        return sh.row(xo, sh.mask_tile, kind * cx + site - HALO)

    md.irr_at = lambda site: mask_at(0, site)
    md.depth_at = lambda site: mask_at(1, site)

    def beside(strip, low, high):
        at = sh.half + high
        return jnp.where(in_group > at, lane_roll(strip, at + 1 - low), strip)

    def to_ends(pair, site, high):
        return lane_roll(pair, end - (site * sh.group + sh.half + high))

    def seam_of(ref, index):
        return lambda site: to_ends(ref[index], site, HALO)

    def prepare(tracers):
        build_strips(tracers)
        wet_strip = md.wet_of(strips[2 * FIELDS + 1])
        wet_pair = beside(wet_strip, HALO - 1, HALO)
        md.wet = Field(
            sh,
            lane,
            lambda j: wet_ref[j],
            lambda: wet_strip,
            lambda site: to_ends(wet_pair, site, HALO),
        )
        d = [strip_field(ch) for ch in range(FIELDS)]
        c = [strip_field(FIELDS + ch) for ch in range(FIELDS)]
        pressure = md.pressure(d, STRIP)
        return d, c, Field(sh, lane, strip=lambda: pressure)

    def strip_field(index):
        return Field(sh, lane, strip=lambda: strips[index])

    def rim(index, site, value):
        rims[index] = value

    def straight(strip, site, low, high):
        back = lane_roll(strip, end - (site * sh.group + sh.half + high))
        front = lane_roll(strip, -(site * sh.group + low))
        return jnp.where(lane < sh.half, front, back)

    def renewed(index, sites, quick=False):
        value = rims[index]
        if not quick:
            seams[index] = beside(value, HALO - 1, HALO)
        ends = beside(value, HALO, HALO - 1)
        for site in sites:
            if quick:
                rows = straight(value, site, HALO, HALO - 1)
            else:
                rows = to_ends(ends, site, HALO - 1)
            cols[md.fresh_at(index, site)] = jnp.where(
                (lane == 0) | (lane == end), rows, fresh[md.fresh_at(index, site)]
            )
        return stored(index, quick)

    def stored(index, quick):
        return Field(
            sh,
            lane,
            lambda j: cols[md.fresh_at(index, j)],
            lambda: rims[index],
            (lambda site: straight(rims[index], site, HALO - 1, HALO))
            if quick
            else seam_of(seams, index),
            lambda j: fresh[md.fresh_at(index, j)],
        )

    def write(ch, k_values):
        for i in range(cx):
            out_ref[pl.ds(ch * sh.lev * cx + i, sh.lev, stride=cx), :] = jnp.where(
                md.odd_x, k_values[cx - 1 - i], k_values[i]
            )

    done = {}

    def keep(ch, site, value):
        done[ch, site] = value

    @pl.when(md.core0)
    def _():
        d, c, pressure = prepare(5)
        md.first_core_site(d, c, pressure, STRIP, rim, True)
        d1 = [renewed(ch, md.own if ch == V else md.first_step) for ch in range(FIELDS)]
        c1 = {i: renewed(GRAZED[i - 2], md.own) for i in (2, 3)}
        rim(PRESSURE, STRIP, md.pressure(d1, STRIP))
        pressure1 = renewed(PRESSURE, md.first_step, True)
        for site in md.own:
            md.first_core_site(d1, c1, pressure1, site, keep, False)
        for ch in range(FIELDS):
            values = [done[ch, site] for site in md.own]
            write(ch, [v * md.mirror for v in values] if ch in VEL_X else values)

    @pl.when(jnp.logical_not(md.core0))
    def _():
        d, c, pressure = prepare(FIELDS)
        md.second_core_site(d, c, pressure, STRIP, rim, True)
        c1 = [renewed(ch, md.first_step) for ch in range(FIELDS)]
        d1 = [renewed(FLOW[ch], md.first_step if ch == U else md.own) for ch in range(4)]
        for site in md.own:
            md.second_core_site(d1, c1, None, site, keep, False)
        for ch in range(FIELDS):
            write(ch, [done[ch, site] for site in md.own])


def tiles(sh, n):
    return jax.ShapeDtypeStruct((n, sh.lev, sh.rows), jnp.float32)


def call(kernel, sh, outs, args, flops, scratch=(), source=pltpu.VMEM):
    spec = pl.BlockSpec(memory_space=pltpu.VMEM)
    size = sum(a.size for a in args) + sum(o.size for o in outs)
    return pl.pallas_call(
        lambda *refs: kernel(sh, *refs),
        out_shape=outs,
        in_specs=[pl.BlockSpec(memory_space=source)] * len(args),
        out_specs=[spec] * len(outs),
        scratch_shapes=list(scratch),
        compiler_params=pltpu.CompilerParams(vmem_limit_bytes=16 << 20),
        cost_estimate=pl.CostEstimate(flops=flops, bytes_accessed=4 * size, transcendentals=0),
    )(*args)


def local(ocean_state, irradiance, land_mask, bottom_level):
    fields, lev, cx, rows = ocean_state.shape
    assert fields == FIELDS
    sh = Shape(lev, cx, rows)
    nx, ny = lax.axis_size("gx"), lax.axis_size("gy")
    assert nx % 2 == 0 and ny % 2 == 0
    axes = ("comp", "gy", "gx")

    def send(value, target):
        pairs = []
        for c in range(2):
            for y in range(ny):
                for x in range(nx):
                    tc, ty, tx = target(c, y, x)
                    pairs.append(((c * ny + y) * nx + x, (tc * ny + ty) * nx + tx))
        return lax.ppermute(value, axes, pairs)

    def odd_pair(i, n):
        return (i + 1) % n if i % 2 else (i - 1) % n

    def pair(i, n, core):
        return i ^ 1 if core == 0 else odd_pair(i, n)

    def edges_x(v):
        return send(v, lambda c, y, x: (c, y, pair(x, nx, c)))

    def bulk_x(v):
        return send(v, lambda c, y, x: (c, y, pair(x, nx, 1 - c)))

    def along_y(v):
        return send(v, lambda c, y, x: (c, pair(y, ny, c), x))

    def swap(v):
        return send(v, lambda c, y, x: (1 - c, y, x))

    flat = ocean_state.reshape(fields * lev * cx, rows)
    partner = swap(flat)
    inputs = (flat, irradiance, land_mask, bottom_level)
    near = tiles(sh, 2)
    xo, own_near = call(
        load_kernel,
        sh,
        [tiles(sh, fields * cx + 1), near],
        tuple(pltpu.with_memory_space_constraint(a, pltpu.HBM) for a in inputs),
        100_000,
        scratch=[pltpu.VMEM(a.shape, a.dtype) for a in inputs] + [pltpu.SemaphoreType.DMA((4,))],
        source=pltpu.HBM,
    )
    edge, message = tiles(sh, sh.edge_tiles), tiles(sh, 2 * sh.halo_tiles + 1)
    xp, nx_edges, m = call(
        send_kernel, sh, [tiles(sh, fields * cx), near, message], (partner, xo, own_near), 100_000
    )
    ex = edges_x(nx_edges)
    rx = bulk_x(m)
    ep = swap(ex)
    (e0,) = call(edge_kernel, sh, [edge], (xo, xp), 100_000)
    (e1,) = call(merge_kernel, sh, [edge], (e0, ex, ep), 10_000)
    y = along_y(e1)
    rp = swap(rx)
    yp = swap(y)
    n_sites = sh.cols - 2
    fresh, wet = call(
        column_kernel,
        sh,
        [tiles(sh, FRESH * n_sites), tiles(sh, sh.cols)],
        (xo, xp, rx, rp),
        1_000_000,
        scratch=[pltpu.VMEM((sh.cols, lev, rows), jnp.float32)],
    )
    (out,) = call(
        step_kernel,
        sh,
        [jax.ShapeDtypeStruct(flat.shape, jnp.float32)],
        (xo, wet, fresh, e1, y, yp),
        1_000_000,
        scratch=[
            pltpu.VMEM((2 * FIELDS + 2, lev, rows), jnp.float32),
            pltpu.VMEM((FRESH * n_sites, lev, rows), jnp.float32),
            pltpu.VMEM((FRESH, lev, rows), jnp.float32),
            pltpu.VMEM((FRESH, lev, rows), jnp.float32),
        ],
    )
    return out.reshape(ocean_state.shape)


def solution(mesh):
    return jax.shard_map(
        local,
        mesh=mesh,
        in_specs=(P("comp", None, "gx", "gy"), P("gx", "gy"), P("gx", "gy"), P("gx", "gy")),
        out_specs=P("comp", None, "gx", "gy"),
        check_vma=False,
    )
```

```python
import jax
import jax.numpy as jnp
from jax import lax
from jax.experimental import pallas as pl
from jax.experimental.pallas import tpu as pltpu
from jax.sharding import PartitionSpec as P


HALO = 2
FIELDS = 8
U, V, TEMP, SALT, UB, VB, TB, SB = range(FIELDS)
VEL_X = (U, UB)


def lane_roll(x, shift):
    shift %= x.shape[1]
    return pltpu.roll(x, shift, 1) if shift else x


def level_roll(x, shift):
    shift %= x.shape[0]
    return pltpu.roll(x, shift, 0) if shift else x


class Shape:
    def __init__(self, lev, cx, rows):
        self.lev, self.cx, self.rows = lev, cx, rows
        self.cols = cx + 2 * HALO
        self.group = rows // self.cols
        self.per_tile = self.group // (2 * HALO)
        self.half = self.group // 2
        self.field_tiles = -(-FIELDS // self.per_tile)
        self.edge_tiles = 2 * self.field_tiles + 1
        assert self.per_tile >= 2 and self.group >= 4 * HALO and 2 * cx <= lev
        assert self.cols * self.group == rows and HALO * 2 * self.field_tiles <= self.cols
        self.mask_tile = FIELDS * cx
        self.halo_tiles = FIELDS * HALO

    def lanes(self):
        return lax.broadcasted_iota(jnp.int32, (self.lev, self.rows), 1)

    def levels(self):
        return lax.broadcasted_iota(jnp.int32, (self.lev, self.rows), 0)

    def row(self, ref, tile, r):
        return jnp.broadcast_to(ref[tile, r : r + 1, :], (self.lev, self.rows))

    def edge_at(self, comp, ch):
        t, q = divmod(ch, self.per_tile)
        return comp * self.field_tiles + t, q

    def halo_at(self, comp, side, ch, d):
        return (self.halo_tiles if comp == side else 0) + ch * HALO + d

    def near_block(self, part, t, d):
        return (d * 2 + part) * self.field_tiles + t

    def edge_place(self, acc, value, j, channel, lane):
        at = (j * self.group + channel * 2 * HALO + HALO) % self.rows
        return jnp.where((lane >= at - HALO) & (lane < at + HALO), lane_roll(value, at), acc)


def load_kernel(sh, *refs):
    sources, x_ref, near_ref, arrived, sem = refs[:4], refs[4], refs[5], refs[6:10], refs[10]
    copies = [
        pltpu.make_async_copy(a, b, sem.at[i]) for i, (a, b) in enumerate(zip(sources, arrived))
    ]
    for copy in copies:
        copy.start()
    for copy in copies:
        copy.wait()
    state_ref, irr_ref, land_ref, bottom_ref = arrived
    odd, core0 = is_odd("gx"), first_core()
    zero = jnp.zeros((sh.lev, sh.rows), jnp.float32)
    own_columns(sh, state_ref, x_ref, odd, core0)
    near_ref[0] = near_edges(sh, x_ref, 0, core0, zero)
    cx = sh.cx
    lane = sh.lanes()
    depth = jnp.where(land_ref[...] == 1, bottom_ref[...], 0).astype(jnp.float32)
    masks = zero
    for q, value in enumerate((irr_ref[...], depth)):
        rows = [
            jnp.where(odd, value[cx - 1 - k : cx - k, :], value[k : k + 1, :]) for k in range(cx)
        ]
        for k in range(cx):
            x_ref[sh.mask_tile, q * cx + k : q * cx + k + 1, :] = rows[k]
        for d in range(HALO):
            row = jnp.where(core0, rows[cx - 1 - d], rows[d])
            wide = jnp.broadcast_to(row, (sh.lev, sh.rows))
            masks = sh.edge_place(masks, wide, d, q, lane)
    near_ref[1] = masks


def near_edges(sh, x_ref, part, core0, acc):
    lane = sh.lanes()
    flip = turned(part, core0)
    for ch in range(FIELDS):
        t, q = sh.edge_at(0, ch)
        for d in range(HALO):
            value = jnp.where(core0, x_ref[ch * sh.cx + sh.cx - 1 - d], x_ref[ch * sh.cx + d])
            if ch in VEL_X:
                value = value * flip
            acc = sh.edge_place(acc, value, sh.near_block(part, t, d), q, lane)
    return acc


def turned(part, core0):
    return jnp.where(core0, -1.0, 1.0) if part == 0 else jnp.where(core0, 1.0, -1.0)


def is_odd(axis):
    return lax.axis_index(axis) & 1 == 1


def first_core():
    return lax.axis_index("comp") == 0


def own_columns(sh, state_ref, x_ref, odd, dynamics):
    flip = jnp.where(odd & dynamics, -1.0, 1.0)
    cx = sh.cx
    for ch in range(FIELDS):
        raw = [state_ref[pl.ds(ch * sh.lev * cx + i, sh.lev, stride=cx), :] for i in range(cx)]
        for k in range(cx):
            value = jnp.where(odd, raw[cx - 1 - k], raw[k])
            x_ref[ch * cx + k] = value * flip if ch in VEL_X else value


def send_kernel(sh, state_ref, xo_ref, own_ref, xp_ref, near_ref, m_ref):
    core0 = first_core()
    own_columns(sh, state_ref, xp_ref, is_odd("gx"), jnp.logical_not(core0))
    near_ref[0] = near_edges(sh, xp_ref, 1, core0, own_ref[0])
    near_ref[1] = own_ref[1]
    cx = sh.cx
    for part, x_ref in enumerate((xo_ref, xp_ref)):
        for ch in range(FIELDS):
            for d in range(HALO):
                value = jnp.where(core0, x_ref[ch * cx + d], x_ref[ch * cx + cx - 1 - d])
                if ch in VEL_X:
                    value = value * turned(part, core0)
                m_ref[part * sh.halo_tiles + ch * HALO + d] = value
    m_ref[2 * sh.halo_tiles] = xo_ref[sh.mask_tile]


def edge_kernel(sh, xo_ref, xp_ref, near_ref, e_ref):
    lane = sh.lanes()
    core0 = first_core()
    cx = sh.cx
    edges = [jnp.zeros((sh.lev, sh.rows), jnp.float32)] * sh.edge_tiles
    for comp in range(2):
        for ch in range(FIELDS):
            t, q = sh.edge_at(comp, ch)
            for k in range(cx):
                pair = xo_ref[ch * cx + k], xp_ref[ch * cx + k]
                value = jnp.where(core0, pair[comp], pair[1 - comp])
                edges[t] = sh.edge_place(edges[t], value, k + HALO, q, lane)
    for q in range(2):
        for k in range(cx):
            value = sh.row(xo_ref, sh.mask_tile, q * cx + k)
            edges[-1] = sh.edge_place(edges[-1], value, k + HALO, q, lane)
    place_side(sh, edges, near_ref, core0)
    for t in range(sh.edge_tiles):
        e_ref[t] = edges[t]


def place_side(sh, edges, near_ref, first):
    column = sh.lanes() // sh.group
    got = near_ref[0], near_ref[1]
    for tile in range(sh.edge_tiles):
        comp, t = divmod(tile, sh.field_tiles)
        for d in range(HALO):
            where = [sh.cx + HALO + d, HALO - 1 - d]
            last = tile == sh.edge_tiles - 1
            shifts = [
                (place - (d if last else sh.near_block(int(comp != side), t, d))) * sh.group % sh.rows
                for side, place in enumerate(where)
            ]
            moved = pltpu.roll(got[int(last)], jnp.where(first, *shifts), 1)
            edges[tile] = jnp.where(column == jnp.where(first, *where), moved, edges[tile])


def merge_kernel(sh, e_ref, near_ref, eo_ref):
    edges = [e_ref[t] for t in range(sh.edge_tiles)]
    place_side(sh, edges, near_ref, jnp.logical_not(first_core()))
    for t in range(sh.edge_tiles):
        eo_ref[t] = edges[t]


STRIP = "strip"


class Field:
    def __init__(self, sh, lane, col=None, strip=None, seam=None, rough=None):
        self.sh, self.lane, self.col, self.strip = sh, lane, col, strip
        self.seam, self.rough = seam, rough

    def centre(self, site):
        return self.strip() if site == STRIP else self.col(site)

    def east(self, site):
        return lane_roll(self.strip(), -self.sh.group) if site == STRIP else self.col(site + 1)

    def west(self, site):
        return lane_roll(self.strip(), self.sh.group) if site == STRIP else self.col(site - 1)

    def along_rows(self, site):
        inner = site == STRIP or self.rough is None
        value = self.centre(site) if inner else self.rough(site)
        north, south = lane_roll(value, -1), lane_roll(value, 1)
        if site == STRIP or self.seam is None:
            return north, south
        beyond = self.seam(site)
        more = 0 if inner else 1
        last = self.lane >= self.sh.rows - 1 - more
        return jnp.where(last, beyond, north), jnp.where(self.lane <= more, beyond, south)

    def around(self, site):
        return (self.east(site), self.west(site)) + self.along_rows(site)


GRAZED = (FIELDS, FIELDS + 1)
FLOW = tuple(FIELDS + ch for ch in (U, V, TEMP, SALT))
PRESSURE = FIELDS + 2
FRESH = FIELDS + 4


class Model:
    def __init__(self, sh):
        self.sh = sh
        self.lane, self.level = sh.lanes(), sh.levels()
        self.levelf = self.level.astype(jnp.float32)
        self.in_group = self.lane % sh.group
        self.core0 = first_core()
        self.odd_x = is_odd("gx")
        self.mirror = jnp.where(self.odd_x, -1.0, 1.0)
        self.gy, self.ny = lax.axis_index("gy"), lax.axis_size("gy")
        self.first_step = list(range(1, sh.cols - 1))
        self.own = list(range(HALO, HALO + sh.cx))
        self.n_sites = len(self.first_step)

    def fresh_at(self, index, site):
        return index * self.n_sites + site - 1

    def cumulate(self, x):
        reach = 1
        while reach < self.sh.lev:
            x = x + jnp.where(self.level >= reach, level_roll(x, reach), 0.0)
            reach *= 2
        return x

    def wet_of(self, depth):
        return jnp.where(self.levelf < depth, 1.0, 0.0)

    def faces(self, site):
        w = self.wet.centre(site)
        return [w * value for value in self.wet.around(site)]

    def density(self, d, site):
        rho = 0.8 * d[SALT].centre(site) - 0.2 * d[TEMP].centre(site)
        return rho * self.wet.centre(site)

    def pressure(self, d, site):
        return 0.1 * self.cumulate(self.density(d, site))

    def speeds(self, u, v, site, m):
        uc, vc = u.centre(site), v.centre(site)
        north, south = v.along_rows(site)
        qe = 0.025 * (uc + u.east(site)) * m[0]
        qw = 0.025 * (uc + u.west(site)) * m[1]
        qn = 0.025 * (vc + north) * m[2]
        qs = 0.025 * (vc + south) * m[3]
        return qe, qw, qn, qs, (qw - qe) + (qs - qn)

    def laplacian(self, f, site, m, total):
        e, w, n, s = f.around(site)
        return (m[0] * e + m[1] * w) + (m[2] * n + m[3] * s) - total * f.centre(site)

    def coriolis(self, site):
        sh, at = self.sh, self.in_group
        row = self.lane
        if site == STRIP:
            row = jnp.where(at < sh.half, at - HALO, sh.rows - HALO + at - sh.half)
        row = (row + self.gy * sh.rows).astype(jnp.float32)
        return self.mirror * (0.3 + 0.4 * row / (self.ny * sh.rows))

    def dynamics(self, d, pressure, site, heat, q, m):
        w = self.wet.centre(site)
        total = (m[0] + m[1]) + (m[2] + m[3])
        uc, vc = d[U].centre(site), d[V].centre(site)
        pc = pressure.centre(site)
        pe, pw, pn, ps = pressure.around(site)
        push_x = 0.1 * (m[0] * (pe - pc) + m[1] * (pc - pw))
        push_y = 0.1 * (m[2] * (pn - pc) + m[3] * (pc - ps))
        f = 0.2 * self.coriolis(site) * w
        spread = {ch: 0.04 * self.laplacian(d[ch], site, m, total) for ch in (UB, VB)}
        after = {
            U: d[UB].centre(site) + (f * vc - push_x + spread[UB]),
            V: d[VB].centre(site) + (spread[VB] - f * uc - push_y),
        }
        if heat is None:
            return after
        qe, qw, qn, qs, qc = q
        for now, before in ((TEMP, TB), (SALT, SB)):
            e, w_, n, s = d[now].around(site)
            carried = (qw * w_ - qe * e) + (qs * s - qn * n) + qc * d[now].centre(site)
            change = 2.0 * carried + 0.04 * self.laplacian(d[before], site, m, total)
            if now == TEMP:
                change = change + 0.6 * heat
            after[now] = d[before].centre(site) + change
        return after

    def filtered(self, d, site, ch, after):
        now, before = d[ch].centre(site), d[ch + 4].centre(site)
        return now + 0.1 * (before - 2.0 * now + after) * self.wet.centre(site)

    def optics(self, c, site):
        absorb = 0.08 + 0.05 * (jnp.abs(c[2].centre(site)) + jnp.abs(c[3].centre(site)))
        return absorb, self.cumulate(absorb)

    def heating(self, absorb, depthsum, site):
        fade = jnp.exp(-depthsum)
        above = jnp.where(self.level == 0, 1.0, level_roll(fade, 1))
        return self.irr_at(site) * self.wet.centre(site) * (above - fade)

    def light(self, absorb, depthsum, site):
        return self.irr_at(site) * jnp.exp(0.5 * absorb - depthsum)

    def mixing(self, d, site):
        rho = self.density(d, site)
        below = level_roll(rho, -1)
        wet_below = jnp.where(self.levelf + 1.0 < self.depth_at(site), 1.0, 0.0)
        return (0.005 + 0.1 / (1.0 + 4.0 * jnp.maximum(below - rho, 0.0))) * wet_below

    def reactions(self, c, temp, lit, which):
        nn, na = jnp.abs(c[0]), jnp.abs(c[1])
        base = jnp.exp(0.06 * temp) * (lit / (lit + 0.5))
        total = nn + na
        small = 0.6 * base * c[2] / (0.2 + total)
        large = 0.9 * base * c[3] / (0.8 + total)
        graze = 0.8 * c[4] / (1.0 + (jnp.abs(c[2]) + jnp.abs(c[3])))
        gs, gl = graze * c[2], graze * c[3]
        up_s, up_l = small * total, large * total
        r = {2: up_s - gs - 0.1 * c[2], 3: up_l - gl - 0.1 * c[3]}
        if len(which) > 2:
            both = small + large
            remin = 0.3 * c[5] + 0.1 * c[6]
            nitrify = 0.2 * c[1]
            r[0] = nitrify - both * nn
            r[1] = remin + 0.1 * c[4] - nitrify - both * na
            r[4] = 0.7 * (gs + gl) - 0.25 * c[4]
            r[5] = 0.1 * c[2] + 0.3 * gs - 0.3 * c[5]
            r[6] = 0.1 * c[3] + 0.15 * c[4] + 0.3 * gl - 0.1 * c[6]
            r[7] = 1.3 * (up_s + up_l) - (remin + 2.0 * nitrify)
        return r

    def tracers(self, c, d, site, q, m, lit, which):
        w = self.wet.centre(site)
        qe, qw, qn, qs, qc = q
        total = (m[0] + m[1]) + (m[2] + m[3])
        ke, kw = 0.02 * m[0] - qe, 0.02 * m[1] + qw
        kn, ks = 0.02 * m[2] - qn, 0.02 * m[3] + qs
        kc = (1.0 - 0.02 * total) + qc
        kappa = self.mixing(d, site)
        centre = {i: c[i].centre(site) for i in (which if len(which) > 2 else range(5))}
        r = self.reactions(centre, d[TEMP].centre(site), lit, which)
        tenth = 0.1 * w
        for i in which:
            e, w_, n, s = c[i].around(site)
            here = centre[i]
            down = kappa * (level_roll(here, -1) - here)
            moved = (ke * e + kw * w_) + (kn * n + ks * s)
            yield i, kc * here + moved + (down - level_roll(down, 1)) + tenth * r[i]

    def first_core_site(self, d, c, pressure, site, store, plankton):
        m = self.faces(site)
        q = self.speeds(d[U], d[V], site, m)
        optic = self.optics(c, site)
        after = self.dynamics(d, pressure, site, self.heating(*optic, site), q, m)
        for ch, value in after.items():
            store(ch, site, value)
            store(ch + 4, site, self.filtered(d, site, ch, value))
        if plankton:
            for i, value in self.tracers(c, d, site, q, m, self.light(*optic, site), (2, 3)):
                store(GRAZED[i - 2], site, value)

    def second_core_site(self, d, c, pressure, site, store, heated):
        m = self.faces(site)
        q = self.speeds(d[U], d[V], site, m)
        optic = self.optics(c, site)
        if pressure is not None:
            heat = self.heating(*optic, site) if heated else None
            for ch, value in self.dynamics(d, pressure, site, heat, q, m).items():
                store(FLOW[ch], site, value)
        lit = self.light(*optic, site)
        for i, value in self.tracers(c, d, site, q, m, lit, range(FIELDS)):
            store(i, site, value)


def column_kernel(sh, xo, xp, rx, rp, fresh, wet_ref, press):
    md = Model(sh)
    cx = sh.cx

    def mask_row(kind, j):
        if HALO <= j < HALO + cx:
            return sh.row(xo, sh.mask_tile, kind * cx + j - HALO)
        if j < HALO:
            first, second, at = rx, rp, HALO - 1 - j
        else:
            first, second, at = rp, rx, cx - 1 - (j - HALO - cx)
        tile = 2 * sh.halo_tiles
        return jnp.where(
            md.core0, sh.row(first, tile, kind * cx + at), sh.row(second, tile, kind * cx + at)
        )

    md.irr_at = lambda site: mask_row(0, site)
    md.depth_at = lambda site: mask_row(1, site)
    for j in range(sh.cols):
        wet_ref[j] = md.wet_of(mask_row(1, j))
    md.wet = Field(sh, md.lane, lambda j: wet_ref[j])

    def raw(x, sides, comp, ch):
        def col(j):
            if HALO <= j < HALO + cx:
                return x[ch * cx + j - HALO]
            if j < HALO:
                return sides[1][sh.halo_at(comp, 1, ch, HALO - 1 - j)]
            return sides[0][sh.halo_at(comp, 0, ch, j - HALO - cx)]

        return Field(sh, md.lane, col)

    def store(index, site, value):
        fresh[md.fresh_at(index, site)] = value

    def fields(x, sides, comp):
        return [raw(x, sides, comp, ch) for ch in range(FIELDS)]

    def pressure_of(d):
        for j in range(sh.cols):
            press[j] = md.pressure(d, j)
        return Field(sh, md.lane, lambda j: press[j])

    @pl.when(md.core0)
    def _():
        d, c = fields(xo, (rp, rx), 0), fields(xp, (rp, rx), 1)
        pressure = pressure_of(d)
        for site in md.first_step:
            md.first_core_site(d, c, pressure, site, store, site in md.own)
        d = [
            Field(sh, md.lane, lambda j, ch=ch: fresh[md.fresh_at(ch, j)]) for ch in range(FIELDS)
        ]
        for site in md.first_step:
            store(PRESSURE, site, md.pressure(d, site))

    @pl.when(jnp.logical_not(md.core0))
    def _():
        d, c = fields(xp, (rx, rp), 0), fields(xo, (rx, rp), 1)
        pressure = pressure_of(d)
        for site in md.first_step:
            md.second_core_site(d, c, pressure, site, store, site in md.own)


def step_kernel(sh, xo, wet_ref, fresh, edges, y, yp, out_ref, strips, cols, rims, seams):
    md = Model(sh)
    cx, lane, in_group = sh.cx, md.lane, md.in_group
    end = sh.rows - 1
    even_y = md.gy & 1 == 0
    slot = lane % (2 * HALO)
    zero = jnp.zeros((sh.lev, sh.rows), jnp.float32)

    def build_strips(tracers):
        strips_of(2 * FIELDS, [sh.edge_tiles - 1], 2)
        strips_of(0, range(2 * sh.field_tiles), FIELDS + tracers)

    def strips_of(base, tiles, channels):
        for t in tiles:
            a, b = jnp.where(md.core0, y[t], yp[t]), jnp.where(md.core0, yp[t], y[t])
            mine = edges[t]
            left = jnp.where(md.gy > 0, jnp.where(even_y, b, a), zero)
            right = jnp.where(md.gy < md.ny - 1, jnp.where(even_y, a, b), zero)
            low = jnp.where(slot < HALO, left, mine)
            high = jnp.where(slot < HALO, mine, right)
            first = (t - tiles[0]) * sh.per_tile
            for q in range(min(channels - first, sh.per_tile)):
                at = q * 2 * HALO
                strips[base + first + q] = jnp.where(
                    in_group < sh.half, lane_roll(low, -at), lane_roll(high, sh.half - at)
                )

    def mask_at(kind, site):
        if site == STRIP:
            return strips[2 * FIELDS + kind]
        return sh.row(xo, sh.mask_tile, kind * cx + site - HALO)

    md.irr_at = lambda site: mask_at(0, site)
    md.depth_at = lambda site: mask_at(1, site)

    def beside(strip, low, high):
        at = sh.half + high
        return jnp.where(in_group > at, lane_roll(strip, at + 1 - low), strip)

    def to_ends(pair, site, high):
        return lane_roll(pair, end - (site * sh.group + sh.half + high))

    def seam_of(ref, index):
        return lambda site: to_ends(ref[index], site, HALO)

    def prepare(tracers):
        build_strips(tracers)
        wet_strip = md.wet_of(strips[2 * FIELDS + 1])
        wet_pair = beside(wet_strip, HALO - 1, HALO)
        md.wet = Field(
            sh,
            lane,
            lambda j: wet_ref[j],
            lambda: wet_strip,
            lambda site: to_ends(wet_pair, site, HALO),
        )
        d = [strip_field(ch) for ch in range(FIELDS)]
        c = [strip_field(FIELDS + ch) for ch in range(FIELDS)]
        pressure = md.pressure(d, STRIP)
        return d, c, Field(sh, lane, strip=lambda: pressure)

    def strip_field(index):
        return Field(sh, lane, strip=lambda: strips[index])

    def rim(index, site, value):
        rims[index] = value

    def straight(strip, site, low, high):
        back = lane_roll(strip, end - (site * sh.group + sh.half + high))
        front = lane_roll(strip, -(site * sh.group + low))
        return jnp.where(lane < sh.half, front, back)

    def renewed(index, sites, quick=False):
        value = rims[index]
        if not quick:
            seams[index] = beside(value, HALO - 1, HALO)
        ends = beside(value, HALO, HALO - 1)
        for site in sites:
            if quick:
                rows = straight(value, site, HALO, HALO - 1)
            else:
                rows = to_ends(ends, site, HALO - 1)
            cols[md.fresh_at(index, site)] = jnp.where(
                (lane == 0) | (lane == end), rows, fresh[md.fresh_at(index, site)]
            )
        return stored(index, quick)

    def stored(index, quick):
        return Field(
            sh,
            lane,
            lambda j: cols[md.fresh_at(index, j)],
            lambda: rims[index],
            (lambda site: straight(rims[index], site, HALO - 1, HALO))
            if quick
            else seam_of(seams, index),
            lambda j: fresh[md.fresh_at(index, j)],
        )

    def write(ch, k_values):
        for i in range(cx):
            out_ref[pl.ds(ch * sh.lev * cx + i, sh.lev, stride=cx), :] = jnp.where(
                md.odd_x, k_values[cx - 1 - i], k_values[i]
            )

    done = {}

    def keep(ch, site, value):
        done[ch, site] = value

    @pl.when(md.core0)
    def _():
        d, c, pressure = prepare(5)
        md.first_core_site(d, c, pressure, STRIP, rim, True)
        d1 = [renewed(ch, md.own if ch == V else md.first_step) for ch in range(FIELDS)]
        c1 = {i: renewed(GRAZED[i - 2], md.own) for i in (2, 3)}
        rim(PRESSURE, STRIP, md.pressure(d1, STRIP))
        pressure1 = renewed(PRESSURE, md.first_step, True)
        for site in md.own:
            md.first_core_site(d1, c1, pressure1, site, keep, False)
        for ch in range(FIELDS):
            values = [done[ch, site] for site in md.own]
            write(ch, [v * md.mirror for v in values] if ch in VEL_X else values)

    @pl.when(jnp.logical_not(md.core0))
    def _():
        d, c, pressure = prepare(FIELDS)
        md.second_core_site(d, c, pressure, STRIP, rim, True)
        c1 = [renewed(ch, md.first_step) for ch in range(FIELDS)]
        d1 = [renewed(FLOW[ch], md.first_step if ch == U else md.own) for ch in range(4)]
        for site in md.own:
            md.second_core_site(d1, c1, None, site, keep, False)
        for ch in range(FIELDS):
            write(ch, [done[ch, site] for site in md.own])


def tiles(sh, n):
    return jax.ShapeDtypeStruct((n, sh.lev, sh.rows), jnp.float32)


def call(kernel, sh, outs, args, flops, scratch=(), source=pltpu.VMEM):
    spec = pl.BlockSpec(memory_space=pltpu.VMEM)
    size = sum(a.size for a in args) + sum(o.size for o in outs)
    return pl.pallas_call(
        lambda *refs: kernel(sh, *refs),
        out_shape=outs,
        in_specs=[pl.BlockSpec(memory_space=source)] * len(args),
        out_specs=[spec] * len(outs),
        scratch_shapes=list(scratch),
        compiler_params=pltpu.CompilerParams(vmem_limit_bytes=16 << 20),
        cost_estimate=pl.CostEstimate(flops=flops, bytes_accessed=4 * size, transcendentals=0),
    )(*args)


def local(ocean_state, irradiance, land_mask, bottom_level):
    fields, lev, cx, rows = ocean_state.shape
    assert fields == FIELDS
    sh = Shape(lev, cx, rows)
    nx, ny = lax.axis_size("gx"), lax.axis_size("gy")
    assert nx % 2 == 0 and ny % 2 == 0
    axes = ("comp", "gy", "gx")

    def send(value, target):
        pairs = []
        for c in range(2):
            for y in range(ny):
                for x in range(nx):
                    tc, ty, tx = target(c, y, x)
                    pairs.append(((c * ny + y) * nx + x, (tc * ny + ty) * nx + tx))
        return lax.ppermute(value, axes, pairs)

    def odd_pair(i, n):
        return (i + 1) % n if i % 2 else (i - 1) % n

    def pair(i, n, core):
        return i ^ 1 if core == 0 else odd_pair(i, n)

    def edges_x(v):
        return send(v, lambda c, y, x: (c, y, pair(x, nx, c)))

    def bulk_x(v):
        return send(v, lambda c, y, x: (c, y, pair(x, nx, 1 - c)))

    def along_y(v):
        return send(v, lambda c, y, x: (c, pair(y, ny, c), x))

    def swap(v):
        return send(v, lambda c, y, x: (1 - c, y, x))

    flat = ocean_state.reshape(fields * lev * cx, rows)
    partner = swap(flat)
    inputs = (flat, irradiance, land_mask, bottom_level)
    near = tiles(sh, 2)
    xo, own_near = call(
        load_kernel,
        sh,
        [tiles(sh, fields * cx + 1), near],
        tuple(pltpu.with_memory_space_constraint(a, pltpu.HBM) for a in inputs),
        100_000,
        scratch=[pltpu.VMEM(a.shape, a.dtype) for a in inputs] + [pltpu.SemaphoreType.DMA((4,))],
        source=pltpu.HBM,
    )
    edge, message = tiles(sh, sh.edge_tiles), tiles(sh, 2 * sh.halo_tiles + 1)
    xp, nx_edges, m = call(
        send_kernel, sh, [tiles(sh, fields * cx), near, message], (partner, xo, own_near), 100_000
    )
    ex = edges_x(nx_edges)
    rx = bulk_x(m)
    ep = swap(ex)
    (e0,) = call(edge_kernel, sh, [edge], (xo, xp, ex), 100_000)
    (e1,) = call(merge_kernel, sh, [edge], (e0, ep), 10_000)
    y = along_y(e1)
    rp = swap(rx)
    yp = swap(y)
    n_sites = sh.cols - 2
    fresh, wet = call(
        column_kernel,
        sh,
        [tiles(sh, FRESH * n_sites), tiles(sh, sh.cols)],
        (xo, xp, rx, rp),
        1_000_000,
        scratch=[pltpu.VMEM((sh.cols, lev, rows), jnp.float32)],
    )
    (out,) = call(
        step_kernel,
        sh,
        [jax.ShapeDtypeStruct(flat.shape, jnp.float32)],
        (xo, wet, fresh, e1, y, yp),
        1_000_000,
        scratch=[
            pltpu.VMEM((2 * FIELDS + 2, lev, rows), jnp.float32),
            pltpu.VMEM((FRESH * n_sites, lev, rows), jnp.float32),
            pltpu.VMEM((FRESH, lev, rows), jnp.float32),
            pltpu.VMEM((FRESH, lev, rows), jnp.float32),
        ],
    )
    return out.reshape(ocean_state.shape)


def solution(mesh):
    return jax.shard_map(
        local,
        mesh=mesh,
        in_specs=(P("comp", None, "gx", "gy"), P("gx", "gy"), P("gx", "gy"), P("gx", "gy")),
        out_specs=P("comp", None, "gx", "gy"),
        check_vma=False,
    )
```

```python
import jax
import jax.numpy as jnp
from jax import lax
from jax.experimental import pallas as pl
from jax.experimental.pallas import tpu as pltpu
from jax.sharding import PartitionSpec as P


HALO = 2
FIELDS = 8
U, V, TEMP, SALT, UB, VB, TB, SB = range(FIELDS)
VEL_X = (U, UB)


def lane_roll(x, shift):
    shift %= x.shape[1]
    return pltpu.roll(x, shift, 1) if shift else x


def level_roll(x, shift):
    shift %= x.shape[0]
    return pltpu.roll(x, shift, 0) if shift else x


class Shape:
    def __init__(self, lev, cx, rows):
        self.lev, self.cx, self.rows = lev, cx, rows
        self.cols = cx + 2 * HALO
        self.group = rows // self.cols
        self.per_tile = self.group // (2 * HALO)
        self.half = self.group // 2
        self.field_tiles = -(-FIELDS // self.per_tile)
        self.edge_tiles = 2 * self.field_tiles + 1
        assert self.per_tile >= 2 and self.group >= 4 * HALO and 2 * cx <= lev
        assert self.cols * self.group == rows and HALO * 2 * self.field_tiles <= self.cols
        self.mask_tile = FIELDS * cx
        self.halo_tiles = FIELDS * HALO

    def lanes(self):
        return lax.broadcasted_iota(jnp.int32, (self.lev, self.rows), 1)

    def levels(self):
        return lax.broadcasted_iota(jnp.int32, (self.lev, self.rows), 0)

    def row(self, ref, tile, r):
        return jnp.broadcast_to(ref[tile, r : r + 1, :], (self.lev, self.rows))

    def edge_at(self, comp, ch):
        t, q = divmod(ch, self.per_tile)
        return comp * self.field_tiles + t, q

    def halo_at(self, comp, side, ch, d):
        return (self.halo_tiles if comp == side else 0) + ch * HALO + d

    def near_block(self, part, t, d):
        return (d * 2 + part) * self.field_tiles + t

    def edge_place(self, acc, value, j, channel, lane):
        at = (j * self.group + channel * 2 * HALO + HALO) % self.rows
        return jnp.where((lane >= at - HALO) & (lane < at + HALO), lane_roll(value, at), acc)


def load_kernel(sh, *refs):
    sources, x_ref, near_ref, arrived, sem = refs[:4], refs[4], refs[5], refs[6:10], refs[10]
    copies = [
        pltpu.make_async_copy(a, b, sem.at[i]) for i, (a, b) in enumerate(zip(sources, arrived))
    ]
    for copy in copies:
        copy.start()
    for copy in copies:
        copy.wait()
    state_ref, irr_ref, land_ref, bottom_ref = arrived
    odd, core0 = is_odd("gx"), first_core()
    zero = jnp.zeros((sh.lev, sh.rows), jnp.float32)
    own_columns(sh, state_ref, x_ref, odd, core0)
    near_ref[0] = near_edges(sh, x_ref, 0, core0, zero)
    cx = sh.cx
    lane = sh.lanes()
    depth = jnp.where(land_ref[...] == 1, bottom_ref[...], 0).astype(jnp.float32)
    masks = zero
    for q, value in enumerate((irr_ref[...], depth)):
        rows = [
            jnp.where(odd, value[cx - 1 - k : cx - k, :], value[k : k + 1, :]) for k in range(cx)
        ]
        for k in range(cx):
            x_ref[sh.mask_tile, q * cx + k : q * cx + k + 1, :] = rows[k]
        for d in range(HALO):
            row = jnp.where(core0, rows[cx - 1 - d], rows[d])
            wide = jnp.broadcast_to(row, (sh.lev, sh.rows))
            masks = sh.edge_place(masks, wide, d, q, lane)
    near_ref[1] = masks


def near_edges(sh, x_ref, part, core0, acc):
    lane = sh.lanes()
    flip = turned(part, core0)
    for ch in range(FIELDS):
        t, q = sh.edge_at(0, ch)
        for d in range(HALO):
            value = jnp.where(core0, x_ref[ch * sh.cx + sh.cx - 1 - d], x_ref[ch * sh.cx + d])
            if ch in VEL_X:
                value = value * flip
            acc = sh.edge_place(acc, value, sh.near_block(part, t, d), q, lane)
    return acc


def turned(part, core0):
    return jnp.where(core0, -1.0, 1.0) if part == 0 else jnp.where(core0, 1.0, -1.0)


def is_odd(axis):
    return lax.axis_index(axis) & 1 == 1


def first_core():
    return lax.axis_index("comp") == 0


def own_columns(sh, state_ref, x_ref, odd, dynamics):
    flip = jnp.where(odd & dynamics, -1.0, 1.0)
    cx = sh.cx
    for ch in range(FIELDS):
        raw = [state_ref[pl.ds(ch * sh.lev * cx + i, sh.lev, stride=cx), :] for i in range(cx)]
        for k in range(cx):
            value = jnp.where(odd, raw[cx - 1 - k], raw[k])
            x_ref[ch * cx + k] = value * flip if ch in VEL_X else value


def send_kernel(sh, state_ref, xo_ref, own_ref, xp_ref, near_ref, m_ref):
    core0 = first_core()
    own_columns(sh, state_ref, xp_ref, is_odd("gx"), jnp.logical_not(core0))
    near_ref[0] = near_edges(sh, xp_ref, 1, core0, own_ref[0])
    near_ref[1] = own_ref[1]
    cx = sh.cx
    for part, x_ref in enumerate((xo_ref, xp_ref)):
        for ch in range(FIELDS):
            for d in range(HALO):
                value = jnp.where(core0, x_ref[ch * cx + d], x_ref[ch * cx + cx - 1 - d])
                if ch in VEL_X:
                    value = value * turned(part, core0)
                m_ref[part * sh.halo_tiles + ch * HALO + d] = value
    m_ref[2 * sh.halo_tiles] = xo_ref[sh.mask_tile]


def edge_kernel(sh, xo_ref, xp_ref, near_ref, e_ref):
    lane = sh.lanes()
    core0 = first_core()
    cx = sh.cx
    edges = [jnp.zeros((sh.lev, sh.rows), jnp.float32)] * sh.edge_tiles
    for comp in range(2):
        for ch in range(FIELDS):
            t, q = sh.edge_at(comp, ch)
            for k in range(cx):
                pair = xo_ref[ch * cx + k], xp_ref[ch * cx + k]
                value = jnp.where(core0, pair[comp], pair[1 - comp])
                edges[t] = sh.edge_place(edges[t], value, k + HALO, q, lane)
    for q in range(2):
        for k in range(cx):
            value = sh.row(xo_ref, sh.mask_tile, q * cx + k)
            edges[-1] = sh.edge_place(edges[-1], value, k + HALO, q, lane)
    place_side(sh, edges, near_ref, core0)
    for t in range(sh.edge_tiles):
        e_ref[t] = edges[t]


def place_side(sh, edges, near_ref, first):
    column = sh.lanes() // sh.group
    got = near_ref[0], near_ref[1]
    for tile in range(sh.edge_tiles):
        comp, t = divmod(tile, sh.field_tiles)
        for d in range(HALO):
            where = [sh.cx + HALO + d, HALO - 1 - d]
            last = tile == sh.edge_tiles - 1
            shifts = [
                (place - (d if last else sh.near_block(int(comp != side), t, d))) * sh.group % sh.rows
                for side, place in enumerate(where)
            ]
            moved = pltpu.roll(got[int(last)], jnp.where(first, *shifts), 1)
            edges[tile] = jnp.where(column == jnp.where(first, *where), moved, edges[tile])


def merge_kernel(sh, e_ref, near_ref, eo_ref):
    edges = [e_ref[t] for t in range(sh.edge_tiles)]
    place_side(sh, edges, near_ref, jnp.logical_not(first_core()))
    for t in range(sh.edge_tiles):
        eo_ref[t] = edges[t]


STRIP = "strip"


class Field:
    def __init__(self, sh, lane, col=None, strip=None, seam=None, rough=None):
        self.sh, self.lane, self.col, self.strip = sh, lane, col, strip
        self.seam, self.rough = seam, rough

    def centre(self, site):
        return self.strip() if site == STRIP else self.col(site)

    def east(self, site):
        return lane_roll(self.strip(), -self.sh.group) if site == STRIP else self.col(site + 1)

    def west(self, site):
        return lane_roll(self.strip(), self.sh.group) if site == STRIP else self.col(site - 1)

    def along_rows(self, site):
        inner = site == STRIP or self.rough is None
        if inner:
            value = self.centre(site)
            north, south = lane_roll(value, -1), lane_roll(value, 1)
        else:
            north, south = self.rough(site)
        if site == STRIP or self.seam is None:
            return north, south
        beyond = self.seam(site)
        more = 0 if inner else 1
        last = self.lane >= self.sh.rows - 1 - more
        return jnp.where(last, beyond, north), jnp.where(self.lane <= more, beyond, south)

    def around(self, site):
        return (self.east(site), self.west(site)) + self.along_rows(site)


GRAZED = (FIELDS, FIELDS + 1)
FLOW = tuple(FIELDS + ch for ch in (U, V, TEMP, SALT))
PRESSURE = FIELDS + 2
FRESH = FIELDS + 4


class Model:
    def __init__(self, sh):
        self.sh = sh
        self.lane, self.level = sh.lanes(), sh.levels()
        self.levelf = self.level.astype(jnp.float32)
        self.in_group = self.lane % sh.group
        self.core0 = first_core()
        self.odd_x = is_odd("gx")
        self.mirror = jnp.where(self.odd_x, -1.0, 1.0)
        self.gy, self.ny = lax.axis_index("gy"), lax.axis_size("gy")
        self.first_step = list(range(1, sh.cols - 1))
        self.own = list(range(HALO, HALO + sh.cx))
        self.n_sites = len(self.first_step)

    def fresh_at(self, index, site):
        return index * self.n_sites + site - 1

    def beside_at(self, index, site):
        return (index * self.sh.cx + site - HALO) * 2

    def cumulate(self, x):
        reach = 1
        while reach < self.sh.lev:
            x = x + jnp.where(self.level >= reach, level_roll(x, reach), 0.0)
            reach *= 2
        return x

    def wet_of(self, depth):
        return jnp.where(self.levelf < depth, 1.0, 0.0)

    def faces(self, site):
        w = self.wet.centre(site)
        return [w * value for value in self.wet.around(site)]

    def density(self, d, site):
        rho = 0.8 * d[SALT].centre(site) - 0.2 * d[TEMP].centre(site)
        return rho * self.wet.centre(site)

    def pressure(self, d, site):
        return 0.1 * self.cumulate(self.density(d, site))

    def speeds(self, u, v, site, m):
        uc, vc = u.centre(site), v.centre(site)
        north, south = v.along_rows(site)
        qe = 0.025 * (uc + u.east(site)) * m[0]
        qw = 0.025 * (uc + u.west(site)) * m[1]
        qn = 0.025 * (vc + north) * m[2]
        qs = 0.025 * (vc + south) * m[3]
        return qe, qw, qn, qs, (qw - qe) + (qs - qn)

    def laplacian(self, f, site, m, total):
        e, w, n, s = f.around(site)
        return (m[0] * e + m[1] * w) + (m[2] * n + m[3] * s) - total * f.centre(site)

    def coriolis(self, site):
        sh, at = self.sh, self.in_group
        row = self.lane
        if site == STRIP:
            row = jnp.where(at < sh.half, at - HALO, sh.rows - HALO + at - sh.half)
        row = (row + self.gy * sh.rows).astype(jnp.float32)
        return self.mirror * (0.3 + 0.4 * row / (self.ny * sh.rows))

    def dynamics(self, d, pressure, site, heat, q, m):
        w = self.wet.centre(site)
        total = (m[0] + m[1]) + (m[2] + m[3])
        uc, vc = d[U].centre(site), d[V].centre(site)
        pc = pressure.centre(site)
        pe, pw, pn, ps = pressure.around(site)
        push_x = 0.1 * (m[0] * (pe - pc) + m[1] * (pc - pw))
        push_y = 0.1 * (m[2] * (pn - pc) + m[3] * (pc - ps))
        f = 0.2 * self.coriolis(site) * w
        spread = {ch: 0.04 * self.laplacian(d[ch], site, m, total) for ch in (UB, VB)}
        after = {
            U: d[UB].centre(site) + (f * vc - push_x + spread[UB]),
            V: d[VB].centre(site) + (spread[VB] - f * uc - push_y),
        }
        if heat is None:
            return after
        qe, qw, qn, qs, qc = q
        for now, before in ((TEMP, TB), (SALT, SB)):
            e, w_, n, s = d[now].around(site)
            carried = (qw * w_ - qe * e) + (qs * s - qn * n) + qc * d[now].centre(site)
            change = 2.0 * carried + 0.04 * self.laplacian(d[before], site, m, total)
            if now == TEMP:
                change = change + 0.6 * heat
            after[now] = d[before].centre(site) + change
        return after

    def filtered(self, d, site, ch, after):
        now, before = d[ch].centre(site), d[ch + 4].centre(site)
        return now + 0.1 * (before - 2.0 * now + after) * self.wet.centre(site)

    def optics(self, c, site):
        absorb = 0.08 + 0.05 * (jnp.abs(c[2].centre(site)) + jnp.abs(c[3].centre(site)))
        return absorb, self.cumulate(absorb)

    def heating(self, absorb, depthsum, site):
        fade = jnp.exp(-depthsum)
        above = jnp.where(self.level == 0, 1.0, level_roll(fade, 1))
        return self.irr_at(site) * self.wet.centre(site) * (above - fade)

    def light(self, absorb, depthsum, site):
        return self.irr_at(site) * jnp.exp(0.5 * absorb - depthsum)

    def mixing(self, d, site):
        rho = self.density(d, site)
        below = level_roll(rho, -1)
        wet_below = jnp.where(self.levelf + 1.0 < self.depth_at(site), 1.0, 0.0)
        return (0.005 + 0.1 / (1.0 + 4.0 * jnp.maximum(below - rho, 0.0))) * wet_below

    def reactions(self, c, temp, lit, which):
        nn, na = jnp.abs(c[0]), jnp.abs(c[1])
        base = jnp.exp(0.06 * temp) * (lit / (lit + 0.5))
        total = nn + na
        small = 0.6 * base * c[2] / (0.2 + total)
        large = 0.9 * base * c[3] / (0.8 + total)
        graze = 0.8 * c[4] / (1.0 + (jnp.abs(c[2]) + jnp.abs(c[3])))
        gs, gl = graze * c[2], graze * c[3]
        up_s, up_l = small * total, large * total
        r = {2: up_s - gs - 0.1 * c[2], 3: up_l - gl - 0.1 * c[3]}
        if len(which) > 2:
            both = small + large
            remin = 0.3 * c[5] + 0.1 * c[6]
            nitrify = 0.2 * c[1]
            r[0] = nitrify - both * nn
            r[1] = remin + 0.1 * c[4] - nitrify - both * na
            r[4] = 0.7 * (gs + gl) - 0.25 * c[4]
            r[5] = 0.1 * c[2] + 0.3 * gs - 0.3 * c[5]
            r[6] = 0.1 * c[3] + 0.15 * c[4] + 0.3 * gl - 0.1 * c[6]
            r[7] = 1.3 * (up_s + up_l) - (remin + 2.0 * nitrify)
        return r

    def tracers(self, c, d, site, q, m, lit, which):
        w = self.wet.centre(site)
        qe, qw, qn, qs, qc = q
        total = (m[0] + m[1]) + (m[2] + m[3])
        ke, kw = 0.02 * m[0] - qe, 0.02 * m[1] + qw
        kn, ks = 0.02 * m[2] - qn, 0.02 * m[3] + qs
        kc = (1.0 - 0.02 * total) + qc
        kappa = self.mixing(d, site)
        centre = {i: c[i].centre(site) for i in (which if len(which) > 2 else range(5))}
        r = self.reactions(centre, d[TEMP].centre(site), lit, which)
        tenth = 0.1 * w
        for i in which:
            e, w_, n, s = c[i].around(site)
            here = centre[i]
            down = kappa * (level_roll(here, -1) - here)
            moved = (ke * e + kw * w_) + (kn * n + ks * s)
            yield i, kc * here + moved + (down - level_roll(down, 1)) + tenth * r[i]

    def first_core_site(self, d, c, pressure, site, store, plankton):
        m = self.faces(site)
        q = self.speeds(d[U], d[V], site, m)
        optic = self.optics(c, site)
        after = self.dynamics(d, pressure, site, self.heating(*optic, site), q, m)
        for ch, value in after.items():
            store(ch, site, value)
            store(ch + 4, site, self.filtered(d, site, ch, value))
        if plankton:
            for i, value in self.tracers(c, d, site, q, m, self.light(*optic, site), (2, 3)):
                store(GRAZED[i - 2], site, value)

    def second_core_site(self, d, c, pressure, site, store, heated):
        m = self.faces(site)
        q = self.speeds(d[U], d[V], site, m)
        optic = self.optics(c, site)
        if pressure is not None:
            heat = self.heating(*optic, site) if heated else None
            for ch, value in self.dynamics(d, pressure, site, heat, q, m).items():
                store(FLOW[ch], site, value)
        lit = self.light(*optic, site)
        for i, value in self.tracers(c, d, site, q, m, lit, range(FIELDS)):
            store(i, site, value)


def column_kernel(sh, xo, xp, rx, rp, fresh, wet_ref, beside_ref, press):
    md = Model(sh)
    cx = sh.cx

    def mask_row(kind, j):
        if HALO <= j < HALO + cx:
            return sh.row(xo, sh.mask_tile, kind * cx + j - HALO)
        if j < HALO:
            first, second, at = rx, rp, HALO - 1 - j
        else:
            first, second, at = rp, rx, cx - 1 - (j - HALO - cx)
        tile = 2 * sh.halo_tiles
        return jnp.where(
            md.core0, sh.row(first, tile, kind * cx + at), sh.row(second, tile, kind * cx + at)
        )

    md.irr_at = lambda site: mask_row(0, site)
    md.depth_at = lambda site: mask_row(1, site)
    for j in range(sh.cols):
        wet_ref[j] = md.wet_of(mask_row(1, j))
    md.wet = Field(sh, md.lane, lambda j: wet_ref[j])

    def raw(x, sides, comp, ch):
        def col(j):
            if HALO <= j < HALO + cx:
                return x[ch * cx + j - HALO]
            if j < HALO:
                return sides[1][sh.halo_at(comp, 1, ch, HALO - 1 - j)]
            return sides[0][sh.halo_at(comp, 0, ch, j - HALO - cx)]

        return Field(sh, md.lane, col)

    def store(index, site, value):
        fresh[md.fresh_at(index, site)] = value

    def fields(x, sides, comp):
        return [raw(x, sides, comp, ch) for ch in range(FIELDS)]

    def rotate(indices):
        for index in indices:
            for site in md.own:
                value, at = fresh[md.fresh_at(index, site)], md.beside_at(index, site)
                beside_ref[at] = lane_roll(value, -1)
                beside_ref[at + 1] = lane_roll(value, 1)

    def pressure_of(d):
        for j in range(sh.cols):
            press[j] = md.pressure(d, j)
        return Field(sh, md.lane, lambda j: press[j])

    @pl.when(md.core0)
    def _():
        d, c = fields(xo, (rp, rx), 0), fields(xp, (rp, rx), 1)
        pressure = pressure_of(d)
        for site in md.first_step:
            md.first_core_site(d, c, pressure, site, store, site in md.own)
        d = [
            Field(sh, md.lane, lambda j, ch=ch: fresh[md.fresh_at(ch, j)]) for ch in range(FIELDS)
        ]
        for site in md.first_step:
            store(PRESSURE, site, md.pressure(d, site))
        rotate([ch for ch in range(FIELDS) if ch != U] + [PRESSURE])

    @pl.when(jnp.logical_not(md.core0))
    def _():
        d, c = fields(xp, (rx, rp), 0), fields(xo, (rx, rp), 1)
        pressure = pressure_of(d)
        for site in md.first_step:
            md.second_core_site(d, c, pressure, site, store, site in md.own)
        rotate(list(range(FIELDS)) + [FLOW[V]])


def step_kernel(sh, xo, wet_ref, fresh, beside_ref, edges, y, yp, out_ref, strips, cols, rims, seams):
    md = Model(sh)
    cx, lane, in_group = sh.cx, md.lane, md.in_group
    end = sh.rows - 1
    even_y = md.gy & 1 == 0
    slot = lane % (2 * HALO)
    zero = jnp.zeros((sh.lev, sh.rows), jnp.float32)

    def build_strips(tracers):
        strips_of(2 * FIELDS, [sh.edge_tiles - 1], 2)
        strips_of(0, range(2 * sh.field_tiles), FIELDS + tracers)

    def strips_of(base, tiles, channels):
        for t in tiles:
            a, b = jnp.where(md.core0, y[t], yp[t]), jnp.where(md.core0, yp[t], y[t])
            mine = edges[t]
            left = jnp.where(md.gy > 0, jnp.where(even_y, b, a), zero)
            right = jnp.where(md.gy < md.ny - 1, jnp.where(even_y, a, b), zero)
            low = jnp.where(slot < HALO, left, mine)
            high = jnp.where(slot < HALO, mine, right)
            first = (t - tiles[0]) * sh.per_tile
            for q in range(min(channels - first, sh.per_tile)):
                at = q * 2 * HALO
                strips[base + first + q] = jnp.where(
                    in_group < sh.half, lane_roll(low, -at), lane_roll(high, sh.half - at)
                )

    def mask_at(kind, site):
        if site == STRIP:
            return strips[2 * FIELDS + kind]
        return sh.row(xo, sh.mask_tile, kind * cx + site - HALO)

    md.irr_at = lambda site: mask_at(0, site)
    md.depth_at = lambda site: mask_at(1, site)

    def beside(strip, low, high):
        at = sh.half + high
        return jnp.where(in_group > at, lane_roll(strip, at + 1 - low), strip)

    def to_ends(pair, site, high):
        return lane_roll(pair, end - (site * sh.group + sh.half + high))

    def seam_of(ref, index):
        return lambda site: to_ends(ref[index], site, HALO)

    def prepare(tracers):
        build_strips(tracers)
        wet_strip = md.wet_of(strips[2 * FIELDS + 1])
        wet_pair = beside(wet_strip, HALO - 1, HALO)
        md.wet = Field(
            sh,
            lane,
            lambda j: wet_ref[j],
            lambda: wet_strip,
            lambda site: to_ends(wet_pair, site, HALO),
        )
        d = [strip_field(ch) for ch in range(FIELDS)]
        c = [strip_field(FIELDS + ch) for ch in range(FIELDS)]
        pressure = md.pressure(d, STRIP)
        return d, c, Field(sh, lane, strip=lambda: pressure)

    def strip_field(index):
        return Field(sh, lane, strip=lambda: strips[index])

    def rim(index, site, value):
        rims[index] = value

    def straight(strip, site, low, high):
        back = lane_roll(strip, end - (site * sh.group + sh.half + high))
        front = lane_roll(strip, -(site * sh.group + low))
        return jnp.where(lane < sh.half, front, back)

    def renewed(index, sites, quick=False):
        value = rims[index]
        if not quick:
            seams[index] = beside(value, HALO - 1, HALO)
        ends = beside(value, HALO, HALO - 1)
        for site in sites:
            if quick:
                rows = straight(value, site, HALO, HALO - 1)
            else:
                rows = to_ends(ends, site, HALO - 1)
            cols[md.fresh_at(index, site)] = jnp.where(
                (lane == 0) | (lane == end), rows, fresh[md.fresh_at(index, site)]
            )
        return stored(index, quick)

    def stored(index, quick):
        return Field(
            sh,
            lane,
            lambda j: cols[md.fresh_at(index, j)],
            lambda: rims[index],
            (lambda site: straight(rims[index], site, HALO - 1, HALO))
            if quick
            else seam_of(seams, index),
            lambda j: [beside_ref[md.beside_at(index, j) + n] for n in range(2)],
        )

    def write(ch, k_values):
        for i in range(cx):
            out_ref[pl.ds(ch * sh.lev * cx + i, sh.lev, stride=cx), :] = jnp.where(
                md.odd_x, k_values[cx - 1 - i], k_values[i]
            )

    done = {}

    def keep(ch, site, value):
        done[ch, site] = value

    @pl.when(md.core0)
    def _():
        d, c, pressure = prepare(5)
        md.first_core_site(d, c, pressure, STRIP, rim, True)
        d1 = [renewed(ch, md.own if ch == V else md.first_step) for ch in range(FIELDS)]
        c1 = {i: renewed(GRAZED[i - 2], md.own) for i in (2, 3)}
        rim(PRESSURE, STRIP, md.pressure(d1, STRIP))
        pressure1 = renewed(PRESSURE, md.first_step, True)
        for site in md.own:
            md.first_core_site(d1, c1, pressure1, site, keep, False)
        for ch in range(FIELDS):
            values = [done[ch, site] for site in md.own]
            write(ch, [v * md.mirror for v in values] if ch in VEL_X else values)

    @pl.when(jnp.logical_not(md.core0))
    def _():
        d, c, pressure = prepare(FIELDS)
        md.second_core_site(d, c, pressure, STRIP, rim, True)
        c1 = [renewed(ch, md.first_step) for ch in range(FIELDS)]
        d1 = [renewed(FLOW[ch], md.first_step if ch == U else md.own) for ch in range(4)]
        for site in md.own:
            md.second_core_site(d1, c1, None, site, keep, False)
        for ch in range(FIELDS):
            write(ch, [done[ch, site] for site in md.own])


def tiles(sh, n):
    return jax.ShapeDtypeStruct((n, sh.lev, sh.rows), jnp.float32)


def call(kernel, sh, outs, args, flops, scratch=(), source=pltpu.VMEM):
    spec = pl.BlockSpec(memory_space=pltpu.VMEM)
    size = sum(a.size for a in args) + sum(o.size for o in outs)
    return pl.pallas_call(
        lambda *refs: kernel(sh, *refs),
        out_shape=outs,
        in_specs=[pl.BlockSpec(memory_space=source)] * len(args),
        out_specs=[spec] * len(outs),
        scratch_shapes=list(scratch),
        compiler_params=pltpu.CompilerParams(vmem_limit_bytes=16 << 20),
        cost_estimate=pl.CostEstimate(flops=flops, bytes_accessed=4 * size, transcendentals=0),
    )(*args)


def local(ocean_state, irradiance, land_mask, bottom_level):
    fields, lev, cx, rows = ocean_state.shape
    assert fields == FIELDS
    sh = Shape(lev, cx, rows)
    nx, ny = lax.axis_size("gx"), lax.axis_size("gy")
    assert nx % 2 == 0 and ny % 2 == 0
    axes = ("comp", "gy", "gx")

    def send(value, target):
        pairs = []
        for c in range(2):
            for y in range(ny):
                for x in range(nx):
                    tc, ty, tx = target(c, y, x)
                    pairs.append(((c * ny + y) * nx + x, (tc * ny + ty) * nx + tx))
        return lax.ppermute(value, axes, pairs)

    def odd_pair(i, n):
        return (i + 1) % n if i % 2 else (i - 1) % n

    def pair(i, n, core):
        return i ^ 1 if core == 0 else odd_pair(i, n)

    def edges_x(v):
        return send(v, lambda c, y, x: (c, y, pair(x, nx, c)))

    def bulk_x(v):
        return send(v, lambda c, y, x: (c, y, pair(x, nx, 1 - c)))

    def along_y(v):
        return send(v, lambda c, y, x: (c, pair(y, ny, c), x))

    def swap(v):
        return send(v, lambda c, y, x: (1 - c, y, x))

    flat = ocean_state.reshape(fields * lev * cx, rows)
    partner = swap(flat)
    inputs = (flat, irradiance, land_mask, bottom_level)
    near = tiles(sh, 2)
    xo, own_near = call(
        load_kernel,
        sh,
        [tiles(sh, fields * cx + 1), near],
        tuple(pltpu.with_memory_space_constraint(a, pltpu.HBM) for a in inputs),
        100_000,
        scratch=[pltpu.VMEM(a.shape, a.dtype) for a in inputs] + [pltpu.SemaphoreType.DMA((4,))],
        source=pltpu.HBM,
    )
    edge, message = tiles(sh, sh.edge_tiles), tiles(sh, 2 * sh.halo_tiles + 1)
    xp, nx_edges, m = call(
        send_kernel, sh, [tiles(sh, fields * cx), near, message], (partner, xo, own_near), 100_000
    )
    ex = edges_x(nx_edges)
    rx = bulk_x(m)
    ep = swap(ex)
    (e0,) = call(edge_kernel, sh, [edge], (xo, xp, ex), 100_000)
    (e1,) = call(merge_kernel, sh, [edge], (e0, ep), 10_000)
    y = along_y(e1)
    rp = swap(rx)
    yp = swap(y)
    n_sites = sh.cols - 2
    fresh, wet, rotated = call(
        column_kernel,
        sh,
        [tiles(sh, FRESH * n_sites), tiles(sh, sh.cols), tiles(sh, FRESH * cx * 2)],
        (xo, xp, rx, rp),
        1_000_000,
        scratch=[pltpu.VMEM((sh.cols, lev, rows), jnp.float32)],
    )
    (out,) = call(
        step_kernel,
        sh,
        [jax.ShapeDtypeStruct(flat.shape, jnp.float32)],
        (xo, wet, fresh, rotated, e1, y, yp),
        1_000_000,
        scratch=[
            pltpu.VMEM((2 * FIELDS + 2, lev, rows), jnp.float32),
            pltpu.VMEM((FRESH * n_sites, lev, rows), jnp.float32),
            pltpu.VMEM((FRESH, lev, rows), jnp.float32),
            pltpu.VMEM((FRESH, lev, rows), jnp.float32),
        ],
    )
    return out.reshape(ocean_state.shape)


def solution(mesh):
    return jax.shard_map(
        local,
        mesh=mesh,
        in_specs=(P("comp", None, "gx", "gy"), P("gx", "gy"), P("gx", "gy"), P("gx", "gy")),
        out_specs=P("comp", None, "gx", "gy"),
        check_vma=False,
    )
```
